128 devices in a mesh: shard: 16 (over y, z_hi, core), ctx: 8 (over x, z_lo).
Axes of the slice: x: 4, y: 4, z: 4 (z_hi: 2, z_lo: 2; z = z_hi * 2 + z_lo), core: 2. Of those that a mesh axis runs over, the one named last changes fastest.
Arguments:
- tokens: bfloat16 [16, 1024, 1024], P('shard', 'ctx'), may hold values from -6 to 6
- positions: int32 [16, 1024], P('shard', 'ctx'), may hold values from 0 to 3069, as said below
- attn_gain: bfloat16 [1024], P('shard'), may hold values from 0.099609375 to 1.8984375
- query_weight: bfloat16 [1024, 2048], P('shard'), may hold values from -0.1875 to 0.1875
- key_matrix: bfloat16 [1024, 1024], P('shard'), may hold values from -0.1875 to 0.1875
- value_matrix: bfloat16 [1024, 1024], P('shard'), may hold values from -0.1875 to 0.1875
- query_gain: bfloat16 [128], P('shard'), may hold values from 0.099609375 to 1.8984375
- key_gain: bfloat16 [128], P('shard'), may hold values from 0.099609375 to 1.8984375
- out_weight: bfloat16 [2048, 1024], P('shard'), may hold values from -0.5 to 0.5
- mlp_gain: bfloat16 [1024], P('shard'), may hold values from 0.099609375 to 1.8984375
- gate_weight: bfloat16 [1024, 3072], P('shard'), may hold values from -0.1875 to 0.1875
- up_weight: bfloat16 [1024, 3072], P('shard'), may hold values from -0.1875 to 0.1875
- down_weight: bfloat16 [3072, 1024], P('shard'), may hold values from -0.109375 to 0.109375
- cotangent: bfloat16 [16, 1024, 1024], P('shard', 'ctx'), may hold values from -6 to 6
Outputs:
- output: bfloat16 [16, 1024, 1024], P('shard', 'ctx')
- input_grad: float32 [16, 1024, 1024], P('shard', 'ctx')
- attn_gain_grad: float32 [1024], P('shard')
- query_weight_grad: float32 [1024, 2048], P('shard')
- key_weight_grad: float32 [1024, 1024], P('shard')
- value_weight_grad: float32 [1024, 1024], P('shard')
- query_gain_grad: float32 [128], P('shard')
- key_gain_grad: float32 [128], P('shard')
- out_weight_grad: float32 [2048, 1024], P('shard')
- mlp_gain_grad: float32 [1024], P('shard')
- gate_weight_grad: float32 [1024, 3072], P('shard')
- up_weight_grad: float32 [1024, 3072], P('shard')
- down_weight_grad: float32 [3072, 1024], P('shard')
The draws below stay inside these ranges and needn't reach their ends.
Inputs may be any that keep to these rules, and one draw needn't show every extreme that they name: Each row of positions starts at 0 and rises by 1, 2 or 3 from one token to the next; the last row rises by 3 throughout and ends at 3069.
All inputs are finite; a program needn't handle non-finite values.
Results may differ from the reference program's by a relative error of at most 0.025.
Values may be sent and summed in bfloat16 or wider, within the bound.
A program may use at most 192 MiB of HBM per device.

```python
import jax
import jax.numpy as jnp
from jax import lax

MODEL_WIDTH = 1024
QUERY_HEADS = 16
SHARED_KV_GROUPS = 8
PER_HEAD_DIM = 128
FF = 3072
SEQ_LEN = 1024
SEQS = 16


def draw_positions(key, part):
    steps = jax.random.randint(key, (SEQS, SEQ_LEN - 1), 1, 4, dtype=jnp.int32)
    last_row = jnp.arange(SEQS, dtype=jnp.int32)[:, None] == SEQS - 1
    steps = jnp.where(last_row, jnp.int32(3), steps).astype(jnp.int32)
    rising = jnp.cumsum(steps, axis=1).astype(jnp.int32)
    return jnp.concatenate([jnp.zeros((SEQS, 1), jnp.int32), rising], axis=1).astype(jnp.int32)


def steps_of(rng, shape, split, low, largest):
    loudness = 1.0
    for position, blocks in split:
        steps = jax.random.uniform(jax.random.fold_in(jax.random.fold_in(rng, 6), position), (blocks,), jnp.float32, low / len(split), largest / len(split))
        loudness = loudness * jnp.repeat(jnp.exp(steps), shape[position] // blocks).reshape((-1,) + (1,) * (len(shape) - 1 - position))
    return loudness


def normal_values(own_key, dims, deviation, limit, pieces=(), kind=jnp.bfloat16):
    entries = jax.random.normal(own_key, dims, jnp.float32) * deviation
    if len(pieces) > 0:
        entries = steps_of(own_key, dims, pieces, -0.22, 0.18) * entries
    return jnp.clip(entries, min=-limit, max=limit).astype(kind)


def setup_inputs(seed: int = 0) -> dict:
    key_list = jax.random.split(jax.random.key(seed), 15)
    return {
        "tokens": normal_values(key_list[0], (SEQS, SEQ_LEN, MODEL_WIDTH), 1.0, 6.0, ((0, 16), (1, 8))),
        "positions": draw_positions(jax.random.fold_in(key_list[14], 71), 0),
        "attn_gain": jnp.clip(1.0 + 0.18 * jax.random.normal(key_list[2], (MODEL_WIDTH,), jnp.float32), 0.099609375, 1.8984375).astype(jnp.bfloat16),
        "query_weight": normal_values(key_list[3], (MODEL_WIDTH, QUERY_HEADS * PER_HEAD_DIM), MODEL_WIDTH ** -0.5, 0.1875, ((0, 16),)),
        "key_matrix": normal_values(key_list[4], (MODEL_WIDTH, SHARED_KV_GROUPS * PER_HEAD_DIM), MODEL_WIDTH ** -0.5, 0.1875, ((0, 16),)),
        "value_matrix": normal_values(key_list[5], (MODEL_WIDTH, SHARED_KV_GROUPS * PER_HEAD_DIM), MODEL_WIDTH ** -0.5, 0.1875, ((0, 16),)),
        "query_gain": jnp.clip(1.0 + 0.18 * jax.random.normal(key_list[6], (PER_HEAD_DIM,), jnp.float32), 0.099609375, 1.8984375).astype(jnp.bfloat16),
        "key_gain": jnp.clip(1.0 + 0.18 * jax.random.normal(key_list[7], (PER_HEAD_DIM,), jnp.float32), 0.099609375, 1.8984375).astype(jnp.bfloat16),
        "out_weight": normal_values(key_list[8], (QUERY_HEADS * PER_HEAD_DIM, MODEL_WIDTH), (QUERY_HEADS * PER_HEAD_DIM // 16) ** -0.5, 0.5, ((0, 16),)),
        "mlp_gain": jnp.clip(1.0 + 0.18 * jax.random.normal(key_list[9], (MODEL_WIDTH,), jnp.float32), 0.099609375, 1.8984375).astype(jnp.bfloat16),
        "gate_weight": normal_values(key_list[10], (MODEL_WIDTH, FF), MODEL_WIDTH ** -0.5, 0.1875, ((0, 16),)),
        "up_weight": normal_values(key_list[11], (MODEL_WIDTH, FF), MODEL_WIDTH ** -0.5, 0.1875, ((0, 16),)),
        "down_weight": normal_values(key_list[12], (FF, MODEL_WIDTH), FF ** -0.5, 0.109375, ((0, 16),)),
        "cotangent": normal_values(key_list[13], (SEQS, SEQ_LEN, MODEL_WIDTH), 1.0, 6.0, ((0, 16), (1, 8))),
    }


EPSILON = 1e-06
ROPE_BASE = 1000000.0
BLOCKED_SCORE = -1e+30

@jax.custom_vjp
def low(v):
    return lax.optimization_barrier(v.astype(jnp.bfloat16)).astype(jnp.float32)

@jax.custom_vjp
def low_back(v):
    return v

def low_keep(v):
    return (low(v), None)

def low_pass(kept, grad):
    return (grad,)

def back_keep(v):
    return (v, None)

def back_low(kept, grad):
    return (low(grad),)
low.defvjp(low_keep, low_pass)
low_back.defvjp(back_keep, back_low)

def matrix_product(left_side, right_side):
    return jnp.dot(left_side, right_side, precision=lax.Precision.HIGHEST, preferred_element_type=jnp.float32)

def rms_scale(values):
    return values * lax.rsqrt(lax.optimization_barrier(jnp.mean(values * values, -1, keepdims=True)) + EPSILON)

def rotary_tables(positions_row):
    half_dim = PER_HEAD_DIM // 2
    freq = jnp.power(ROPE_BASE, -jnp.arange(half_dim, dtype=jnp.float32) * (2.0 / PER_HEAD_DIM))
    angle = positions_row.astype(jnp.float32)[:, None] * freq[None, :]
    cos_half = jnp.cos(angle)
    sin_half = jnp.sin(angle)
    return (jnp.concatenate([cos_half, cos_half], -1), jnp.concatenate([sin_half, sin_half], -1))

def rotate(values, cosine_table, sine_table):
    half_dim = values.shape[-1] // 2
    turned = jnp.concatenate([-values[..., half_dim:], values[..., :half_dim]], -1)
    return values * cosine_table[:, None, :] + turned * sine_table[:, None, :]

def attend_heads(query_rows_all, key_rows_all, value_input_rows):
    length_steps = query_rows_all.shape[0]
    block_step = min(512, length_steps)
    count_total = length_steps // block_step
    query_block_list = query_rows_all.reshape(count_total, block_step, SHARED_KV_GROUPS, QUERY_HEADS // SHARED_KV_GROUPS, PER_HEAD_DIM)
    starts = (jnp.arange(count_total) * block_step).astype(jnp.int32)

    def one_block(pair):
        query_block, start = pair
        scores = jnp.einsum('bkgd,nkd->kgbn', query_block, key_rows_all, precision=lax.Precision.HIGHEST) * PER_HEAD_DIM ** (-0.5)
        scores = low_back(scores)
        rows_index = start + jnp.arange(block_step, dtype=jnp.int32)
        cols_index = jnp.arange(length_steps, dtype=jnp.int32)
        allowed = cols_index[None, :] <= rows_index[:, None]
        scores = jnp.where(allowed, scores, BLOCKED_SCORE)
        weights = low(jax.nn.softmax(scores, axis=-1))
        mixed = jnp.einsum('kgbn,nkd->bkgd', weights, value_input_rows, precision=lax.Precision.HIGHEST)
        return mixed.reshape(block_step, QUERY_HEADS * PER_HEAD_DIM)
    return lax.map(jax.checkpoint(one_block), (query_block_list, starts)).reshape(length_steps, QUERY_HEADS * PER_HEAD_DIM)

def layer_forward(inputs, params, cosine_table, sine_table):
    attn_gain, query_weight, key_matrix, value_matrix, query_gain, key_gain, out_weight, mlp_gain, gate_weight, up_weight, down_weight = params
    length_steps = inputs.shape[0]
    normed_input = low(rms_scale(inputs) * attn_gain)
    query_raw = low_back(matrix_product(normed_input, query_weight)).reshape(length_steps, QUERY_HEADS, PER_HEAD_DIM)
    query_rows_all = low(rotate(rms_scale(query_raw) * query_gain, cosine_table, sine_table))
    key_unrotated = low_back(matrix_product(normed_input, key_matrix)).reshape(length_steps, SHARED_KV_GROUPS, PER_HEAD_DIM)
    key_rows_all = low(rotate(rms_scale(key_unrotated) * key_gain, cosine_table, sine_table))
    value_input_rows = low(low_back(matrix_product(normed_input, value_matrix))).reshape(length_steps, SHARED_KV_GROUPS, PER_HEAD_DIM)
    attended_rows = attend_heads(query_rows_all.reshape(length_steps, SHARED_KV_GROUPS, QUERY_HEADS // SHARED_KV_GROUPS, PER_HEAD_DIM), key_rows_all, value_input_rows)
    attended_rows = low(low_back(attended_rows))
    resid = inputs + low_back(matrix_product(attended_rows, out_weight))
    normed_two = low(rms_scale(resid) * mlp_gain)
    gate_value = low_back(matrix_product(normed_two, gate_weight))
    up_value = low_back(matrix_product(normed_two, up_weight))
    hidden = low(jax.nn.silu(gate_value) * up_value)
    return resid + low_back(matrix_product(hidden, down_weight))

def reference(tokens, positions, attn_gain, query_weight, key_matrix, value_matrix, query_gain, key_gain, out_weight, mlp_gain, gate_weight, up_weight, down_weight, cotangent):
    params = tuple((member.astype(jnp.float32) for member in (attn_gain, query_weight, key_matrix, value_matrix, query_gain, key_gain, out_weight, mlp_gain, gate_weight, up_weight, down_weight)))

    def one_sequence(totals, inputs):
        seq_tokens, seq_positions, seq_cotangent = inputs
        cosine_table, sine_table = rotary_tables(seq_positions)

        def forward(inputs_float, params_float):
            return layer_forward(inputs_float, params_float, cosine_table, sine_table)
        result, pullback = jax.vjp(forward, seq_tokens.astype(jnp.float32), params)
        input_grad, param_grads = pullback(seq_cotangent.astype(jnp.float32))
        totals = jax.tree.map(lambda summed, adding: summed + adding, totals, param_grads)
        return (totals, (result.astype(jnp.bfloat16), input_grad))
    zero_filled = jax.tree.map(jnp.zeros_like, params)
    totals, (outputs, input_grads) = lax.scan(one_sequence, zero_filled, (tokens, positions, cotangent))
    return (outputs, input_grads, totals[0], totals[1], totals[2], totals[3], totals[4], totals[5], totals[6], totals[7], totals[8], totals[9], totals[10])
```

```python
import jax
import jax.numpy as jnp
from jax import lax
from jax.experimental import pallas as pl
from jax.experimental.pallas import tpu as pltpu
from jax.sharding import PartitionSpec as P

MESH = pl.DeviceIdType.MESH
BF = jnp.bfloat16
F32 = jnp.float32

NS = 16
NC = 8
T = 128
SEQ = 1024
D = 1024
HD = 128
QW = 256
FW = 384
EPSILON = 1e-06
ROPE_BASE = 1000000.0
BLOCKED_SCORE = -1e30
SMALL = 2304

ALL = slice(None)
ROWS = ((slice(0, 48), ALL), (slice(48, 96), ALL), (slice(96, 128), ALL))


def lanes(width):
    n = width // 128
    a = (n + 2) // 3 * 128
    b = a + (n + 1) // 3 * 128
    return ((ALL, slice(0, a)), (ALL, slice(a, b)), (ALL, slice(b, width)))


def view(ref, part):
    return ref.at[tuple(pl.ds(p.start, p.stop - p.start) if p != ALL else p for p in part)]


class Ring:
    def __init__(self, me, device):
        self.a = me // 2
        self.b = lax.rem(me, 2)
        self.device = device

    def idx(self, da, db):
        return lax.rem(self.a + da + 4, 4) * 2 + lax.rem(self.b + db, 2)

    def dev(self, da, db):
        return self.device(self.idx(da, db))


class Net:
    def __init__(self, send, recv, local):
        self.s, self.r, self.l = send, recv, local
        self.n = 0
        self.m = 0

    def send(self, src, dst, to):
        k = self.n
        self.n += 1
        c = pltpu.make_async_remote_copy(
            src_ref=src, dst_ref=dst, send_sem=self.s.at[k], recv_sem=self.r.at[k],
            device_id=to, device_id_type=MESH,
        )
        c.start()
        return c

    def copy(self, src, dst):
        k = self.m
        self.m += 1
        c = pltpu.make_async_copy(src, dst, self.l.at[k])
        c.start()
        return c


def places():
    s = lax.axis_index("shard")
    c = lax.axis_index("ctx")
    core = lax.rem(s, 2)
    ctx = Ring(c, lambda i: (s, i))
    chips = Ring(s // 2, lambda i: (i * 2 + core, c))
    sibling = (s + 1 - 2 * core, c)
    half, rest = lax.rem(s, 2), s // 2
    goes = (8 * half + c, rest)
    comes = (2 * c + s // 8, lax.rem(s, 8))
    stays = jnp.logical_and(goes[0] == s, goes[1] == c)
    return s, c, core, ctx, chips, sibling, goes, comes, stays


def ring_devices(ring):
    return [ring.dev(-1, 0), ring.dev(1, 0), ring.dev(0, 1)]


def greet(devices, moved=None):
    barrier = pltpu.get_barrier_semaphore()
    for d in devices:
        pl.semaphore_signal(barrier, inc=1, device_id=d, device_id_type=MESH)
    if moved is not None:
        goes, comes, stays = moved

        @pl.when(jnp.logical_not(stays))
        def _():
            for d in (goes, comes):
                pl.semaphore_signal(barrier, inc=1, device_id=d, device_id_type=MESH)
            pl.semaphore_wait(barrier, len(devices) + 2)

        @pl.when(stays)
        def _():
            pl.semaphore_wait(barrier, len(devices))

    else:
        pl.semaphore_wait(barrier, len(devices))


def drive(*threads):
    threads = list(threads)
    while threads:
        for t in list(threads):
            try:
                next(t)
            except StopIteration:
                threads.remove(t)


def move(net, items, to, stays):
    base = net.n
    net.n += len(items)

    def remote(k, src, dst):
        return pltpu.make_async_remote_copy(
            src_ref=src, dst_ref=dst, send_sem=net.s.at[base + k], recv_sem=net.r.at[base + k],
            device_id=to, device_id_type=MESH,
        )

    @pl.when(jnp.logical_not(stays))
    def _():
        for k, (src, dst) in enumerate(items):
            remote(k, src, dst).start()

    @pl.when(stays)
    def _():
        for k, (src, dst) in enumerate(items):
            pltpu.make_async_copy(src, dst, net.r.at[base + k]).start()

    yield

    @pl.when(jnp.logical_not(stays))
    def _():
        for k, (src, dst) in enumerate(items):
            remote(k, src, dst).wait()

    @pl.when(stays)
    def _():
        for k, (src, dst) in enumerate(items):
            pltpu.make_async_copy(src, dst, net.r.at[base + k]).wait()


def gather(net, ring, items, slot=lambda i: i, sibling=None):
    left, right, pair = ring_devices(ring)
    me = ring.idx(0, 0)
    over = []

    def pass_on(places):
        if sibling is not None:
            for _, dst, _ in items:
                for i in places:
                    over.append(net.send(dst.at[slot(i)], dst.at[slot(i)], sibling))

    first, local = [], []
    for own, dst, _ in items:
        here = dst.at[slot(me)]
        src = here if own is None else own
        for n in (left, right, pair):
            first.append(net.send(src, here, n))
        if sibling is not None:
            over.append(net.send(src, here, sibling))
        if own is not None:
            local.append(net.copy(own, here))
    yield
    for c in first:
        c.wait_recv()
    second = []
    a, b, z = ring.idx(-1, 0), ring.idx(1, 0), ring.idx(0, 1)
    for _, dst, _ in items:
        for i, n in ((a, right), (z, left), (a, pair)):
            second.append(net.send(dst.at[slot(i)], dst.at[slot(i)], n))
    pass_on((a, b, z))
    yield
    for c in second:
        c.wait_recv()
    third = []
    az, bz, o, oz = ring.idx(-1, 1), ring.idx(1, 1), ring.idx(2, 0), ring.idx(2, 1)
    for _, dst, parts in items:
        for i, n, part in ((az, right, parts[0]), (bz, left, parts[1]), (o, pair, parts[2])):
            if part is not None:
                r = view(dst.at[slot(i)], part)
                third.append(net.send(r, r, n))
    pass_on((az, bz, o))
    yield
    for c in third:
        c.wait_recv()
    pass_on((oz,))
    for c in local:
        c.wait()
    for c in first + second + third:
        c.wait_send()
    if sibling is not None:
        yield
        for c in over:
            c.wait()


def reduce(net, ring, items, result):
    left, right, pair = ring_devices(ring)
    me, a, b, z = ring.idx(0, 0), ring.idx(-1, 0), ring.idx(1, 0), ring.idx(0, 1)
    az, bz, o, oz = ring.idx(-1, 1), ring.idx(1, 1), ring.idx(2, 0), ring.idx(2, 1)

    def plus(x, y):
        return (x.astype(F32) + y.astype(F32)).astype(BF)

    first, second, third = [], [], []
    for p, parts, land, _ in items:
        for n, part in zip((left, right, pair), parts):
            first.append(net.send(view(p.at[oz], part), view(land.at[0], part), n))
    yield
    for c in first:
        c.wait_recv()
    for p, parts, land, sums in items:
        for k, (i, part) in enumerate(((o, parts[2]), (bz, parts[1]), (az, parts[0]))):
            sums[k] = p[i]
            sums[(k,) + part] = plus(p[(i,) + part], land[(0,) + part])
        for k, n in enumerate((left, right, pair)):
            second.append(net.send(sums.at[k], land.at[1 + k], n))
    yield
    for c in second:
        c.wait_recv()
    for p, parts, land, sums in items:
        third.append(net.send(p.at[b], land.at[5], right))
        sums[3] = (p[a].astype(F32) + land[1].astype(F32) + land[3].astype(F32)).astype(BF)
        third.append(net.send(sums.at[3], land.at[4], left))
        sums[4] = plus(p[z], land[2])
        third.append(net.send(sums.at[4], land.at[6], pair))
    yield
    for c in third:
        c.wait_recv()
    for k, (p, parts, land, sums) in enumerate(items):
        result(
            k,
            (p[me].astype(F32) + land[4].astype(F32))
            + (land[5].astype(F32) + land[6].astype(F32)),
        )
    for c in first + second + third:
        c.wait_send()


def reduce_scratch(shape):
    return [pltpu.VMEM((7,) + shape, BF), pltpu.VMEM((5,) + shape, BF)]


def reduce_shard(net, chips, core, sibling, items, result):
    over = []
    for p, _, half, _, _, _ in items:
        over.append(net.send(p.at[1 - core], half, sibling))
    yield
    for c in over:
        c.wait_recv()
    for p, _, half, both, _, _ in items:

        @pl.loop(0, 8)
        def _(j):
            both[j] = (p[core, j].astype(F32) + half[j].astype(F32)).astype(BF)

    yield from reduce(net, chips, [(i[3], i[1], i[4], i[5]) for i in items], result)
    for c in over:
        c.wait_send()


def shard_scratch(shape):
    return [pltpu.VMEM((8,) + shape, BF), pltpu.VMEM((8,) + shape, BF)] + reduce_scratch(shape)


def rms_parts(v):
    inverse = lax.rsqrt(jnp.mean(v * v, -1, keepdims=True) + EPSILON)
    return v * inverse, inverse


def rms_back(g, n, inverse):
    return inverse * (g - n * jnp.mean(g * n, -1, keepdims=True))


def remote_call(body, outs, ins, args, scratch, copies, locals_, number, vmem=None):
    sems = [
        pltpu.SemaphoreType.DMA((copies,)),
        pltpu.SemaphoreType.DMA((copies,)),
        pltpu.SemaphoreType.DMA((locals_,)),
    ]
    space = {"v": pl.BlockSpec(memory_space=pltpu.VMEM), "h": pl.BlockSpec(memory_space=pl.ANY)}
    return pl.pallas_call(
        body,
        out_shape=[jax.ShapeDtypeStruct(s, d) for s, d, _ in outs],
        in_specs=[space[k] for k in ins],
        out_specs=[space[k] for _, _, k in outs],
        scratch_shapes=list(scratch) + sems,
        compiler_params=pltpu.CompilerParams(
            collective_id=number, has_side_effects=True, vmem_limit_bytes=vmem
        ),
    )(*args)


WCOL1 = 640
WCOL2 = 768


def start_body(tok, cot, pos, w1, wo, x_all, g_all, p_all, w1_all, wo_all, ss, rs, ls):
    s, c, core, ctx, chips, sibling, goes, comes, stays = places()
    net = Net(ss, rs, ls)
    greet(ring_devices(ctx) + ring_devices(chips) + [sibling], (goes, comes, stays))

    def by_shard():
        yield from move(net, [(wo.at[c], wo_all.at[goes[0]])], goes, stays)
        yield from gather(
            net, chips, [(w1, w1_all, lanes(WCOL1)), (None, wo_all, lanes(D))],
            lambda i: i * 2 + core, sibling,
        )

    def by_ctx():
        yield from gather(net, ctx, [(tok, x_all, ROWS), (pos, p_all, ((ALL, ALL), None, None))])
        yield from gather(net, ctx, [(cot, g_all, ROWS)])

    drive(by_ctx(), by_shard())


def attn_join_body(
    part, tok, gain, w2, wd, h_all, resid_ref, w2_all, wd_all,
    hid, land, sums, ss, rs, ls,
):
    s, c, core, ctx, chips, sibling, goes, comes, stays = places()
    net = Net(ss, rs, ls)
    greet(ring_devices(ctx) + ring_devices(chips) + [sibling], (goes, comes, stays))

    def by_shard():
        yield from move(net, [(wd.at[c], wd_all.at[goes[0]])], goes, stays)
        yield from gather(
            net, chips, [(w2, w2_all, lanes(WCOL2)), (None, wd_all, lanes(D))],
            lambda i: i * 2 + core, sibling,
        )

    def got(k, total):
        resid = tok[...].astype(F32) + total
        resid_ref[...] = resid
        normed, _ = rms_parts(resid)
        hid[...] = (normed * gain[...]).astype(BF)

    def by_ctx():
        yield from reduce(net, ctx, [(part, ROWS, land, sums)], got)
        yield from gather(net, ctx, [(hid, h_all, ROWS)])

    drive(by_ctx(), by_shard())


def mlp_join_body(
    down_part, back_part, resid_ref, cot, gain, gw2, gwd,
    out_ref, ga_all, gres_ref, ggain_ref, gw2_sum, gwd_sum,
    ga, land1, sums1, land2, sums2, h1, b1, l1, t1, h2, b2, l2, t2, ss, rs, ls,
):
    s, c, core, ctx, chips, sibling, goes, comes, stays = places()
    net = Net(ss, rs, ls)
    greet(ring_devices(ctx) + ring_devices(chips) + [sibling])

    def got_shard(k, total):
        (gw2_sum, gwd_sum)[k][...] = total.astype(BF)

    def got_down(k, total):
        out_ref[...] = (resid_ref[...] + total).astype(BF)

    def got_back(k, total):
        normed, inverse = rms_parts(resid_ref[...])
        ggain_ref[...] = jnp.sum(total * normed, 0, keepdims=True)
        gres = cot[...].astype(F32) + rms_back(total * gain[...], normed, inverse)
        gres_ref[...] = gres
        ga[...] = gres.astype(BF)

    def by_ctx():
        yield from reduce(net, ctx, [(back_part, ROWS, land1, sums1)], got_back)
        yield from gather(net, ctx, [(ga, ga_all, ROWS)])

    def later():
        yield
        yield
        yield
        yield from reduce(net, ctx, [(down_part, ROWS, land2, sums2)], got_down)

    by_shard = reduce_shard(
        net, chips, core, sibling,
        [(gw2, lanes(WCOL2), h1, b1, l1, t1), (gwd, lanes(D), h2, b2, l2, t2)], got_shard,
    )
    drive(by_ctx(), later(), by_shard)


def end_body(
    part, tok, gres_ref, gain, ggain, gqk, gw1, gwo, gw2_sum, gwd_sum,
    gx_ref, small_ref, q_out, k_out, v_out, o_out, gate_out, up_out, down_out,
    land, sums, h1, b1, l1, t1, h2, b2, l2, t2,
    s1, so, a1, ao, a2, ad, own_d, sm, smc, sm2, sms, ss, rs, ls,
):
    s, c, core, ctx, chips, sibling, goes, comes, stays = places()
    net = Net(ss, rs, ls)
    ctx_peers = [(s, lax.rem(c + d, NC)) for d in range(1, NC)]
    shard_peers = [(lax.rem(s + d, NS), c) for d in range(1, NS)]
    greet(ctx_peers + shard_peers, (goes, comes, stays))

    def got_input(k, total):
        normed, inverse = rms_parts(tok[...].astype(F32))
        sm[:, 0:D] = jnp.sum(total * normed, 0, keepdims=True)
        sm[:, D : 2 * D] = ggain[...]
        sm[:, 2 * D :] = gqk[...]
        gx_ref[...] = gres_ref[...] + rms_back(total * gain[...], normed, inverse)

    def by_ctx():
        yield from reduce(net, ctx, [(part, ROWS, land, sums)], got_input)
        smc[c] = sm[...]
        sent = [net.send(sm, smc.at[c], d) for d in ctx_peers]
        yield
        for x in sent:
            x.wait()
        total = smc[0]
        for i in range(1, NC):
            total = total + smc[i]
        sm2[...] = total
        sms[s] = total
        sent = [net.send(sm2, sms.at[s], d) for d in shard_peers]
        yield
        for x in sent:
            x.wait()
        total = sms[0]
        for i in range(1, NS):
            total = total + sms[i]
        small_ref[...] = total

    def mlp():
        yield
        yield
        yield from move(net, [(gwd_sum, own_d)], comes, stays)
        yield from gather(net, ctx, [(gw2_sum, a2, lanes(WCOL2)), (own_d, ad, lanes(D))])
        for i in range(NC):
            gate_out[:, FW * i : FW * (i + 1)] = a2[i, :, 0:FW].astype(F32)
            up_out[:, FW * i : FW * (i + 1)] = a2[i, :, FW : 2 * FW].astype(F32)
            down_out[24 * i : 24 * (i + 1), :] = ad[i].astype(F32)

    def got_shard(k, total):
        (s1, so)[k][...] = total.astype(BF)

    def attn():
        yield from reduce_shard(
            net, chips, core, sibling,
            [(gw1, lanes(512), h1, b1, l1, t1), (gwo, lanes(D), h2, b2, l2, t2)], got_shard,
        )
        yield from move(net, [(so, ao.at[comes[1]])], comes, stays)
        yield from gather(net, ctx, [(s1, a1, lanes(512)), (None, ao, lanes(D))])
        for i in range(NC):
            q_out[:, QW * i : QW * (i + 1)] = a1[i, :, 0:QW].astype(F32)
            k_out[:, HD * i : HD * (i + 1)] = a1[i, :, QW : QW + HD].astype(F32)
            v_out[:, HD * i : HD * (i + 1)] = a1[i, :, QW + HD :].astype(F32)
            o_out[16 * i : 16 * (i + 1), :] = ao[i].astype(F32)

    drive(by_ctx(), attn(), mlp())


def rotate(values, cosine, sine):
    turned = jnp.concatenate([-values[..., HD // 2 :], values[..., : HD // 2]], -1)
    return values * cosine + turned * sine


def rotate_reverse(grads, cosine, sine):
    t = grads * sine
    return grads * cosine + jnp.concatenate([t[..., HD // 2 :], -t[..., : HD // 2]], -1)


def dot(a, b, dims, out=F32):
    return lax.dot_general(a, b, (dims, ((), ())), preferred_element_type=F32).astype(out)


NN = ((1,), (0,))
NT = ((1,), (1,))
TN = ((0,), (0,))


def by_owner(g, rows):
    return jnp.transpose(g.reshape(8, 2, rows, g.shape[1]), (1, 0, 2, 3))


def shards(
    tokens, positions, attn_gain, query_weight, key_matrix, value_matrix, query_gain, key_gain,
    out_weight, mlp_gain, gate_weight, up_weight, down_weight, cotangent,
):
    c = lax.axis_index("ctx")
    s = lax.axis_index("shard")
    tok, cot = tokens[0], cotangent[0]

    def cut(w, width):
        return lax.dynamic_slice(w, (0, c * width), (w.shape[0], width))

    row0 = jnp.concatenate([attn_gain, mlp_gain])[None]
    row1 = jnp.concatenate([query_gain, key_gain, jnp.zeros((112,), BF)])[None]
    gains = jnp.concatenate([row0, row1, jnp.zeros((62, 128), BF)], 0)
    w1 = jnp.concatenate(
        [cut(query_weight, QW), cut(key_matrix, HD), cut(value_matrix, HD), gains], 1
    )
    w2 = jnp.concatenate([cut(gate_weight, FW), cut(up_weight, FW)], 1)
    wo = out_weight.reshape(8, 16, D)
    wd = down_weight.reshape(8, 24, D)

    x_all, g_all, p_all, w1_all, wo_all = remote_call(
        start_body,
        [
            ((NC, T, D), BF, "h"), ((NC, T, D), BF, "h"), ((NC, 1, T), jnp.int32, "h"),
            ((NS, 64, WCOL1), BF, "h"), ((NS, 16, D), BF, "h"),
        ],
        "hhhhh", (tok, cot, positions, w1, wo), [], 80, 8, 0,
    )
    gain_attn = w1_all[:, 0, 512:576].reshape(1, D).astype(F32)
    gain_mlp = w1_all[:, 0, 576:640].reshape(1, D).astype(F32)
    gain_q = w1_all[:, 1, 512:520].reshape(HD).astype(F32)
    gain_k = w1_all[:, 1, 520:528].reshape(HD).astype(F32)
    wqkv = w1_all[:, :, 0:512].reshape(D, 512)
    wout = wo_all.reshape(QW, D)
    half = HD // 2
    freq = jnp.power(ROPE_BASE, -jnp.arange(half, dtype=F32) * (2.0 / HD))
    angle = p_all.reshape(SEQ).astype(F32)[:, None] * freq[None, :]
    cosine = jnp.concatenate([jnp.cos(angle)] * 2, -1)
    sine = jnp.concatenate([jnp.sin(angle)] * 2, -1)

    x = x_all.reshape(SEQ, D)
    normed_one, _ = rms_parts(x.astype(F32))
    hidden_one = (normed_one * gain_attn).astype(BF)
    raw = dot(hidden_one, wqkv, NN)
    value = raw[:, QW + HD :].astype(BF)
    q_raw = raw[:, :QW].reshape(SEQ, 2, HD)
    k_raw = raw[:, QW : QW + HD]
    q_normed, q_inverse = rms_parts(q_raw)
    k_normed, k_inverse = rms_parts(k_raw)
    cosine_q, sine_q = cosine[:, None, :], sine[:, None, :]
    queries = rotate(q_normed * gain_q, cosine_q, sine_q).astype(BF)
    keys = rotate(k_normed * gain_k, cosine, sine).astype(BF)
    scale = HD**-0.5
    scores = jnp.einsum("thd,nd->htn", queries, keys, preferred_element_type=F32) * scale
    order = jnp.arange(SEQ)
    allowed = order[None, :] <= order[:, None]
    scores = jnp.where(allowed, scores, BLOCKED_SCORE)
    top = jnp.max(scores, -1, keepdims=True)
    weights = jnp.where(allowed, jnp.exp(scores - top), 0.0)
    total = jnp.sum(weights, -1, keepdims=True)
    heads = (
        jnp.einsum("htn,nd->htd", weights.astype(BF), value, preferred_element_type=F32) / total
    )
    log_total = top + jnp.log(total)
    attended = jnp.transpose(heads, (1, 0, 2)).reshape(SEQ, QW).astype(BF)
    out_part = dot(attended, wout, NN, BF).reshape(NC, T, D)

    h_all, resid, w2_all, wd_all = remote_call(
        attn_join_body,
        [
            ((NC, T, D), BF, "h"), ((T, D), F32, "v"),
            ((NS, 64, WCOL2), BF, "h"), ((NS, 24, D), BF, "h"),
        ],
        "vvvhh", (out_part, tok, gain_mlp, w2, wd),
        [pltpu.VMEM((T, D), BF)] + reduce_scratch((T, D)), 80, 8, 1, 40 << 20,
    )
    hidden_two = h_all.reshape(SEQ, D)
    wgu = w2_all.reshape(D, 2 * FW)
    wdown = wd_all.reshape(FW, D)
    g_full = g_all.reshape(SEQ, D)
    both = dot(hidden_two, wgu, NN)
    gate, up = both[:, :FW], both[:, FW:]
    sig = jax.nn.sigmoid(gate)
    act = gate * sig
    mixed = (act * up).astype(BF)
    down_part = dot(mixed, wdown, NN, BF).reshape(NC, T, D)
    grad_mixed = dot(g_full, wdown, NT)
    grad_gate = (grad_mixed * up * sig * (1.0 + gate * (1.0 - sig))).astype(BF)
    grad_up = (grad_mixed * act).astype(BF)
    grad_gu = jnp.concatenate([grad_gate, grad_up], 1)
    back_part = dot(grad_gu, wgu, NT, BF).reshape(NC, T, D)
    gw2 = by_owner(dot(hidden_two, grad_gu, TN, BF), 64)
    gwd = by_owner(dot(mixed, g_full, TN, BF), 24)

    output, ga_all, grad_resid, ggain_mlp, gw2_sum, gwd_sum = remote_call(
        mlp_join_body,
        [
            ((T, D), BF, "v"), ((NC, T, D), BF, "h"), ((T, D), F32, "v"), ((1, D), F32, "v"),
            ((64, WCOL2), BF, "v"), ((24, D), BF, "v"),
        ],
        "v" * 7, (down_part, back_part, resid, cot, gain_mlp, gw2, gwd),
        [pltpu.VMEM((T, D), BF)] + reduce_scratch((T, D)) * 2
        + shard_scratch((64, WCOL2)) + shard_scratch((24, D)),
        80, 8, 2, 56 << 20,
    )
    ga = ga_all.reshape(SEQ, D)
    gwo = by_owner(dot(attended, ga, TN, BF), 16)
    grad_att = dot(ga, wout, NT, BF).reshape(SEQ, 2, HD)
    delta = jnp.einsum("thd,htd->ht", grad_att.astype(F32), heads)
    scores = jnp.einsum("thd,nd->htn", queries, keys, preferred_element_type=F32) * scale
    probs = jnp.where(allowed, jnp.exp(scores - log_total), 0.0)
    probs_bf = probs.astype(BF)
    grad_value = jnp.einsum("htn,thd->nd", probs_bf, grad_att, preferred_element_type=F32)
    grad_probs = jnp.einsum("thd,nd->htn", grad_att, value, preferred_element_type=F32)
    grad_scores = (probs * (grad_probs - delta[..., None])).astype(BF)
    grad_q = jnp.einsum("htn,nd->thd", grad_scores, keys, preferred_element_type=F32) * scale
    grad_k = jnp.einsum("htn,thd->nd", grad_scores, queries, preferred_element_type=F32) * scale
    wq = rotate_reverse(grad_q, cosine_q, sine_q)
    wk = rotate_reverse(grad_k, cosine, sine)
    gq_gain = jnp.sum(wq * q_normed, (0, 1))
    gk_gain = jnp.sum(wk * k_normed, 0)
    gq = rms_back(wq * gain_q, q_normed, q_inverse).reshape(SEQ, QW).astype(BF)
    gk = rms_back(wk * gain_k, k_normed, k_inverse).astype(BF)
    gqkv = jnp.concatenate([gq, gk, grad_value.astype(BF)], 1)
    gw1 = by_owner(dot(hidden_one, gqkv, TN, BF), 64)
    in_part = dot(gqkv, wqkv, NT, BF).reshape(NC, T, D)
    gqk = jnp.concatenate([gq_gain, gk_gain])[None]

    outs = remote_call(
        end_body,
        [
            ((T, D), F32, "v"), ((1, SMALL), F32, "v"),
            ((64, 2048), F32, "v"), ((64, 1024), F32, "v"), ((64, 1024), F32, "v"),
            ((128, D), F32, "v"), ((64, 3072), F32, "v"), ((64, 3072), F32, "v"),
            ((192, D), F32, "v"),
        ],
        "v" * 10,
        (in_part, tok, grad_resid, gain_attn, ggain_mlp, gqk, gw1, gwo, gw2_sum, gwd_sum),
        reduce_scratch((T, D)) + shard_scratch((64, 512)) + shard_scratch((16, D))
        + [
            pltpu.VMEM((64, 512), BF), pltpu.VMEM((16, D), BF),
            pltpu.VMEM((NC, 64, 512), BF), pltpu.VMEM((NC, 16, D), BF),
            pltpu.VMEM((NC, 64, WCOL2), BF), pltpu.VMEM((NC, 24, D), BF),
            pltpu.VMEM((24, D), BF),
            pltpu.VMEM((1, SMALL), F32), pltpu.VMEM((NC, 1, SMALL), F32),
            pltpu.VMEM((1, SMALL), F32), pltpu.VMEM((NS, 1, SMALL), F32),
        ],
        128, 8, 3, 56 << 20,
    )
    gx, small, gwq, gwk, gwv, gwo_out, gwg, gwu, gwd_out = outs
    small = small[0]

    def own(offset, width):
        return lax.dynamic_slice(small, (offset + s * width,), (width,))

    return (
        output[None], gx[None], own(0, 64), gwq, gwk, gwv, own(2 * D, 8), own(2 * D + HD, 8),
        gwo_out, own(D, 64), gwg, gwu, gwd_out,
    )


def solution(mesh):
    split = P("shard", "ctx", None)
    rows, vec = P("shard", None), P("shard")
    in_specs = (
        split, P("shard", "ctx"), vec, rows, rows, rows, vec, vec, rows, vec, rows, rows, rows, split,
    )
    out_specs = (split, split, vec, rows, rows, rows, vec, vec, rows, vec, rows, rows, rows)
    return jax.shard_map(shards, mesh=mesh, in_specs=in_specs, out_specs=out_specs, check_vma=False)
```

```python
import jax
import jax.numpy as jnp
from jax import lax
from jax.experimental import pallas as pl
from jax.experimental.pallas import tpu as pltpu
from jax.sharding import PartitionSpec as P

MESH = pl.DeviceIdType.MESH
BF = jnp.bfloat16
F32 = jnp.float32

NS = 16
NC = 8
T = 128
SEQ = 1024
D = 1024
HD = 128
QW = 256
FW = 384
EPSILON = 1e-06
ROPE_BASE = 1000000.0
BLOCKED_SCORE = -1e30
SMALL = 2304

ALL = slice(None)


def lanes(width):
    n = width // 128
    a = (n + 2) // 3 * 128
    b = a + (n + 1) // 3 * 128
    return ((ALL, slice(0, a)), (ALL, slice(a, b)), (ALL, slice(b, width)))


def view(ref, part):
    return ref.at[tuple(pl.ds(p.start, p.stop - p.start) if p != ALL else p for p in part)]


class Ring:
    def __init__(self, me, device):
        self.a = me // 2
        self.b = lax.rem(me, 2)
        self.device = device

    def idx(self, da, db):
        return lax.rem(self.a + da + 4, 4) * 2 + lax.rem(self.b + db, 2)

    def dev(self, da, db):
        return self.device(self.idx(da, db))


class Net:
    def __init__(self, send, recv, local):
        self.s, self.r, self.l = send, recv, local
        self.n = 0
        self.m = 0

    def send(self, src, dst, to):
        k = self.n
        self.n += 1
        c = pltpu.make_async_remote_copy(
            src_ref=src, dst_ref=dst, send_sem=self.s.at[k], recv_sem=self.r.at[k],
            device_id=to, device_id_type=MESH,
        )
        c.start()
        return c

    def copy(self, src, dst):
        k = self.m
        self.m += 1
        c = pltpu.make_async_copy(src, dst, self.l.at[k])
        c.start()
        return c


def places():
    s = lax.axis_index("shard")
    c = lax.axis_index("ctx")
    core = lax.rem(s, 2)
    ctx = Ring(c, lambda i: (s, i))
    chips = Ring(s // 2, lambda i: (i * 2 + core, c))
    sibling = (s + 1 - 2 * core, c)
    half, rest = lax.rem(s, 2), s // 2
    goes = (8 * half + c, rest)
    comes = (2 * c + s // 8, lax.rem(s, 8))
    stays = jnp.logical_and(goes[0] == s, goes[1] == c)
    return s, c, core, ctx, chips, sibling, goes, comes, stays


def ring_devices(ring):
    return [ring.dev(-1, 0), ring.dev(1, 0), ring.dev(0, 1)]


def greet(devices, moved=None):
    barrier = pltpu.get_barrier_semaphore()
    for d in devices:
        pl.semaphore_signal(barrier, inc=1, device_id=d, device_id_type=MESH)
    if moved is not None:
        goes, comes, stays = moved

        @pl.when(jnp.logical_not(stays))
        def _():
            for d in (goes, comes):
                pl.semaphore_signal(barrier, inc=1, device_id=d, device_id_type=MESH)
            pl.semaphore_wait(barrier, len(devices) + 2)

        @pl.when(stays)
        def _():
            pl.semaphore_wait(barrier, len(devices))

    else:
        pl.semaphore_wait(barrier, len(devices))


def drive(*threads):
    threads = list(threads)
    while threads:
        for t in list(threads):
            try:
                next(t)
            except StopIteration:
                threads.remove(t)


def move(net, items, to, stays):
    base = net.n
    net.n += len(items)

    def remote(k, src, dst):
        return pltpu.make_async_remote_copy(
            src_ref=src, dst_ref=dst, send_sem=net.s.at[base + k], recv_sem=net.r.at[base + k],
            device_id=to, device_id_type=MESH,
        )

    @pl.when(jnp.logical_not(stays))
    def _():
        for k, (src, dst) in enumerate(items):
            remote(k, src, dst).start()

    @pl.when(stays)
    def _():
        for k, (src, dst) in enumerate(items):
            pltpu.make_async_copy(src, dst, net.r.at[base + k]).start()

    yield

    @pl.when(jnp.logical_not(stays))
    def _():
        for k, (src, dst) in enumerate(items):
            remote(k, src, dst).wait()

    @pl.when(stays)
    def _():
        for k, (src, dst) in enumerate(items):
            pltpu.make_async_copy(src, dst, net.r.at[base + k]).wait()


def gather(net, ring, items, slot=lambda i: i, sibling=None):
    left, right, pair = ring_devices(ring)
    me = ring.idx(0, 0)
    over = []

    def pass_on(places):
        if sibling is not None:
            for _, at, _ in items:
                for i in places:
                    over.append(net.send(at(slot(i)), at(slot(i)), sibling))

    first, local = [], []
    for own, at, _ in items:
        here = at(slot(me))
        src = here if own is None else own
        for n in (left, right, pair):
            first.append(net.send(src, here, n))
        if sibling is not None:
            over.append(net.send(src, here, sibling))
        if own is not None:
            local.append(net.copy(own, here))
    yield
    for c in first:
        c.wait_recv()
    second = []
    a, b, z = ring.idx(-1, 0), ring.idx(1, 0), ring.idx(0, 1)
    for _, at, _ in items:
        for i, n in ((a, right), (z, left), (a, pair)):
            second.append(net.send(at(slot(i)), at(slot(i)), n))
    pass_on((a, b, z))
    yield
    for c in second:
        c.wait_recv()
    third = []
    az, bz, o, oz = ring.idx(-1, 1), ring.idx(1, 1), ring.idx(2, 0), ring.idx(2, 1)
    for _, at, parts in items:
        for i, n, part in ((az, right, parts[0]), (bz, left, parts[1]), (o, pair, parts[2])):
            if part is not None:
                r = view(at(slot(i)), part)
                third.append(net.send(r, r, n))
    pass_on((az, bz, o))
    yield
    for c in third:
        c.wait_recv()
    pass_on((oz,))
    for c in local:
        c.wait()
    for c in first + second + third:
        c.wait_send()
    if sibling is not None:
        yield
        for c in over:
            c.wait()


def reduce(net, ring, items, result):
    left, right, pair = ring_devices(ring)
    me, a, b, z = ring.idx(0, 0), ring.idx(-1, 0), ring.idx(1, 0), ring.idx(0, 1)
    az, bz, o, oz = ring.idx(-1, 1), ring.idx(1, 1), ring.idx(2, 0), ring.idx(2, 1)

    def plus(x, y):
        return (x.astype(F32) + y.astype(F32)).astype(BF)

    first, second, third = [], [], []
    for p, parts, land, _ in items:
        for n, part in zip((left, right, pair), parts):
            first.append(net.send(view(p(oz), part), view(land.at[0], part), n))
    yield
    for c in first:
        c.wait_recv()
    for p, parts, land, sums in items:
        for k, (i, part, n) in enumerate(
            ((o, parts[2], left), (bz, parts[1], right), (az, parts[0], pair))
        ):
            sums[k] = p(i)[...]
            sums[(k,) + part] = plus(p(i)[part], land[(0,) + part])
            second.append(net.send(sums.at[k], land.at[1 + k], n))
    yield
    for c in second:
        c.wait_recv()
    for p, parts, land, sums in items:
        third.append(net.send(p(b), land.at[5], right))
        sums[4] = plus(p(z)[...], land[2])
        third.append(net.send(sums.at[4], land.at[6], pair))
        sums[3] = (p(a)[...].astype(F32) + land[1].astype(F32) + land[3].astype(F32)).astype(BF)
        third.append(net.send(sums.at[3], land.at[4], left))
    yield
    for c in third:
        c.wait_recv()
    for k, (p, parts, land, sums) in enumerate(items):
        result(
            k,
            (p(me)[...].astype(F32) + land[4].astype(F32))
            + (land[5].astype(F32) + land[6].astype(F32)),
        )
    for c in first + second + third:
        c.wait_send()


def at(ref):
    return lambda i: ref.at[i]


CHUNKS = 2
CROWS = T // CHUNKS
CPARTS = ((slice(0, 32), ALL), (slice(32, 48), ALL), (slice(48, 64), ALL))


def rows(h):
    return pl.ds(CROWS * h, CROWS)


def chunk(ref, h):
    return lambda i: ref.at[i, rows(h)]


def chunk_scratch():
    return [pltpu.VMEM((7, CROWS, D), BF), pltpu.VMEM((5, CROWS, D), BF)] * CHUNKS


def reduce_scratch(shape):
    return [pltpu.VMEM((7,) + shape, BF), pltpu.VMEM((5,) + shape, BF)]


def reduce_shard(net, chips, core, sibling, items, result):
    over = []
    for p, _, half, _, _, _ in items:
        over.append(net.send(p.at[1 - core], half, sibling))
    yield
    for c in over:
        c.wait_recv()
    for p, _, half, both, _, _ in items:

        @pl.loop(0, 8)
        def _(j):
            both[j] = (p[core, j].astype(F32) + half[j].astype(F32)).astype(BF)

    yield from reduce(net, chips, [(at(i[3]), i[1], i[4], i[5]) for i in items], result)
    for c in over:
        c.wait_send()


def shard_scratch(shape):
    return [pltpu.VMEM((8,) + shape, BF), pltpu.VMEM((8,) + shape, BF)] + reduce_scratch(shape)


def rms_parts(v):
    inverse = lax.rsqrt(jnp.mean(v * v, -1, keepdims=True) + EPSILON)
    return v * inverse, inverse


def rms_back(g, n, inverse):
    return inverse * (g - n * jnp.mean(g * n, -1, keepdims=True))


def dot(a, b, dims, out=F32):
    return lax.dot_general(a, b, (dims, ((), ())), preferred_element_type=F32).astype(out)


NN = ((1,), (0,))
NT = ((1,), (1,))
TN = ((0,), (0,))


def remote_call(body, outs, ins, args, scratch, copies, locals_, number, vmem=None):
    sems = [
        pltpu.SemaphoreType.DMA((copies,)),
        pltpu.SemaphoreType.DMA((copies,)),
        pltpu.SemaphoreType.DMA((locals_,)),
    ]
    space = {"v": pl.BlockSpec(memory_space=pltpu.VMEM), "h": pl.BlockSpec(memory_space=pl.ANY)}
    return pl.pallas_call(
        body,
        out_shape=[jax.ShapeDtypeStruct(s, d) for s, d, _ in outs],
        in_specs=[space[k] for k in ins],
        out_specs=[space[k] for _, _, k in outs],
        scratch_shapes=list(scratch) + sems,
        compiler_params=pltpu.CompilerParams(
            collective_id=number, has_side_effects=True, vmem_limit_bytes=vmem
        ),
    )(*args)


WCOL1 = 640
WCOL2 = 768


def start_body(
    tok, cot, pos, w1, wo, w2, wd, x_all, g_all, p_all, w1_all, wo_all, w2_all, wd_all, ss, rs, ls
):
    s, c, core, ctx, chips, sibling, goes, comes, stays = places()
    net = Net(ss, rs, ls)
    greet(ring_devices(ctx) + ring_devices(chips) + [sibling], (goes, comes, stays))

    def by_shard():
        moved = [(wo.at[c], wo_all.at[goes[0]]), (wd.at[c], wd_all.at[goes[0]])]
        yield from move(net, moved, goes, stays)
        yield from gather(
            net, chips,
            [
                (w1, at(w1_all), lanes(WCOL1)), (None, at(wo_all), lanes(D)),
                (w2, at(w2_all), lanes(WCOL2)), (None, at(wd_all), lanes(D)),
            ],
            lambda i: i * 2 + core, sibling,
        )

    def by_ctx(h):
        items = [(tok.at[rows(h)], chunk(x_all, h), CPARTS)]
        if h == 0:
            items.append((pos, at(p_all), ((ALL, ALL), None, None)))
        yield from gather(net, ctx, items)
        yield from gather(net, ctx, [(cot.at[rows(h)], chunk(g_all, h), CPARTS)])

    drive(*[by_ctx(h) for h in range(CHUNKS)], by_shard())


def mid_body(
    part, tok, cot, gain, wgu, wd, g_all,
    out_ref, ga_all, gres_ref, ggain_ref, gw2_sum, gwd_sum,
    h_all, mixed, ggu, down_part, back_part, resid, ga, gw2, gwd, gwd_f,
    la0, sa0, la1, sa1, lb0, sb0, lb1, sb1, lc0, sc0, lc1, sc1,
    h1, b1, l1, t1, h2, b2, l2, t2, ss, rs, ls,
):
    s, c, core, ctx, chips, sibling, goes, comes, stays = places()
    net = Net(ss, rs, ls)
    greet(ring_devices(ctx) + ring_devices(chips) + [sibling])

    def forward(h, land, sums):
        def got(k, total):
            r = tok[rows(h)].astype(F32) + total
            resid[rows(h)] = r
            normed, _ = rms_parts(r)
            h_all[c, rows(h)] = (normed * gain[...]).astype(BF)

        yield from reduce(net, ctx, [(chunk(part, h), CPARTS, land, sums)], got)
        yield from gather(net, ctx, [(None, chunk(h_all, h), CPARTS)])

    def block(i):
        both = dot(h_all[i], wgu[...], NN)
        gate, up = both[:, :FW], both[:, FW:]
        sig = jax.nn.sigmoid(gate)
        act = gate * sig
        m = (act * up).astype(BF)
        mixed[i] = m
        gm = dot(g_all[i], wd[...], NT)
        gg = (gm * up * sig * (1.0 + gate * (1.0 - sig))).astype(BF)
        gu = (gm * act).astype(BF)
        ggu[i, :, 0:FW] = gg
        ggu[i, :, FW:] = gu
        back_part[i] = dot(jnp.concatenate([gg, gu], 1), wgu[...], NT, BF)
        down_part[i] = dot(m, wd[...], NN, BF)

    def blocks(places):
        n = len(places)

        @pl.loop(0, n)
        def _(j):
            i = places[0]
            for k in range(1, n):
                i = jnp.where(j == k, places[k], i)
            block(i)

    def work():
        yield
        yield
        yield
        blocks([c])
        yield
        blocks([ctx.idx(-1, 0), ctx.idx(1, 0), ctx.idx(0, 1)])
        yield
        blocks([ctx.idx(-1, 1), ctx.idx(1, 1), ctx.idx(2, 0)])
        yield
        blocks([ctx.idx(2, 1)])

    drive(forward(0, la0, sa0), forward(1, la1, sa1), work())

    def got_back(h):
        def got(k, total):
            normed, inverse = rms_parts(resid[rows(h)])
            g = jnp.sum(total * normed, 0, keepdims=True)
            if h == 0:
                ggain_ref[...] = g
            else:
                ggain_ref[...] += g
            gres = cot[rows(h)].astype(F32) + rms_back(total * gain[...], normed, inverse)
            gres_ref[rows(h)] = gres
            ga[rows(h)] = gres.astype(BF)

        return got

    def backward(h, land, sums):
        yield from reduce(net, ctx, [(chunk(back_part, h), CPARTS, land, sums)], got_back(h))
        yield from gather(net, ctx, [(ga.at[rows(h)], chunk(ga_all, h), CPARTS)])

    def later(h, land, sums):
        def got(k, total):
            out_ref[rows(h)] = (resid[rows(h)] + total).astype(BF)

        yield
        yield
        yield
        yield
        yield from reduce(net, ctx, [(chunk(down_part, h), CPARTS, land, sums)], got)

    def got_shard(k, total):
        (gw2_sum, gwd_sum)[k][...] = total.astype(BF)

    def grads():
        for q in range(2):

            @pl.loop(4 * q, 4 * q + 4)
            def _(j):
                left = h_all[:, :, pl.ds(pl.multiple_of(j * 128, 128), 128)].reshape(SEQ, 128)
                g = dot(left, ggu[...].reshape(SEQ, 2 * FW), TN, BF)
                gw2[0, j] = g[0:64]
                gw2[1, j] = g[64:128]

            yield
        for j in range(3):
            left = mixed[:, :, 128 * j : 128 * (j + 1)].reshape(SEQ, 128)
            gwd_f[128 * j : 128 * (j + 1)] = dot(left, g_all[...].reshape(SEQ, D), TN)
        for i in range(NS):
            gwd[i % 2, i // 2] = gwd_f[24 * i : 24 * (i + 1)].astype(BF)
        yield
        yield from reduce_shard(
            net, chips, core, sibling,
            [(gw2, lanes(WCOL2), h1, b1, l1, t1), (gwd, lanes(D), h2, b2, l2, t2)], got_shard,
        )

    drive(
        backward(0, lb0, sb0), backward(1, lb1, sb1),
        later(0, lc0, sc0), later(1, lc1, sc1), grads(),
    )


def end_body(
    part, tok, gres_ref, gain, ggain, gqk, gw1, gwo, gw2_sum, gwd_sum,
    gx_ref, small_ref, q_out, k_out, v_out, o_out, gate_out, up_out, down_out,
    la0, sa0, la1, sa1, h1, b1, l1, t1, h2, b2, l2, t2,
    s1, so, a1, ao, a2, ad, own_d, sm, smc, sm2, sms, ss, rs, ls,
):
    s, c, core, ctx, chips, sibling, goes, comes, stays = places()
    net = Net(ss, rs, ls)
    ctx_peers = [(s, lax.rem(c + d, NC)) for d in range(1, NC)]
    shard_peers = [(lax.rem(s + d, NS), c) for d in range(1, NS)]
    greet(ctx_peers + shard_peers, (goes, comes, stays))

    def got_input(h):
        def got(k, total):
            normed, inverse = rms_parts(tok[rows(h)].astype(F32))
            g = jnp.sum(total * normed, 0, keepdims=True)
            if h == 0:
                sm[:, 0:D] = g
            else:
                sm[:, 0:D] += g
            gx_ref[rows(h)] = gres_ref[rows(h)] + rms_back(total * gain[...], normed, inverse)

        return got

    def by_ctx(h, land, sums):
        yield from reduce(net, ctx, [(chunk(part, h), CPARTS, land, sums)], got_input(h))

    def small():
        yield
        yield
        yield
        yield
        sm[:, D : 2 * D] = ggain[...]
        sm[:, 2 * D :] = gqk[...]
        smc[c] = sm[...]
        sent = [net.send(sm, smc.at[c], d) for d in ctx_peers]
        yield
        for x in sent:
            x.wait()
        total = smc[0]
        for i in range(1, NC):
            total = total + smc[i]
        sm2[...] = total
        sms[s] = total
        sent = [net.send(sm2, sms.at[s], d) for d in shard_peers]
        yield
        for x in sent:
            x.wait()
        total = sms[0]
        for i in range(1, NS):
            total = total + sms[i]
        small_ref[...] = total

    def mlp():
        yield
        yield
        yield from move(net, [(gwd_sum, own_d)], comes, stays)
        yield from gather(net, ctx, [(gw2_sum, at(a2), lanes(WCOL2)), (own_d, at(ad), lanes(D))])
        for i in range(NC):
            gate_out[:, FW * i : FW * (i + 1)] = a2[i, :, 0:FW].astype(F32)
            up_out[:, FW * i : FW * (i + 1)] = a2[i, :, FW : 2 * FW].astype(F32)
            down_out[24 * i : 24 * (i + 1), :] = ad[i].astype(F32)

    def got_shard(k, total):
        (s1, so)[k][...] = total.astype(BF)

    def attn():
        yield from reduce_shard(
            net, chips, core, sibling,
            [(gw1, lanes(512), h1, b1, l1, t1), (gwo, lanes(D), h2, b2, l2, t2)], got_shard,
        )
        yield from move(net, [(so, ao.at[comes[1]])], comes, stays)
        yield from gather(net, ctx, [(s1, at(a1), lanes(512)), (None, at(ao), lanes(D))])
        for i in range(NC):
            q_out[:, QW * i : QW * (i + 1)] = a1[i, :, 0:QW].astype(F32)
            k_out[:, HD * i : HD * (i + 1)] = a1[i, :, QW : QW + HD].astype(F32)
            v_out[:, HD * i : HD * (i + 1)] = a1[i, :, QW + HD :].astype(F32)
            o_out[16 * i : 16 * (i + 1), :] = ao[i].astype(F32)

    drive(by_ctx(0, la0, sa0), by_ctx(1, la1, sa1), small(), attn(), mlp())


def rotate(values, cosine, sine):
    turned = jnp.concatenate([-values[..., HD // 2 :], values[..., : HD // 2]], -1)
    return values * cosine + turned * sine


def rotate_reverse(grads, cosine, sine):
    t = grads * sine
    return grads * cosine + jnp.concatenate([t[..., HD // 2 :], -t[..., : HD // 2]], -1)


def by_owner(g, rows):
    return jnp.transpose(g.reshape(8, 2, rows, g.shape[1]), (1, 0, 2, 3))


def shards(
    tokens, positions, attn_gain, query_weight, key_matrix, value_matrix, query_gain, key_gain,
    out_weight, mlp_gain, gate_weight, up_weight, down_weight, cotangent,
):
    c = lax.axis_index("ctx")
    s = lax.axis_index("shard")
    tok, cot = tokens[0], cotangent[0]

    def cut(w, width):
        return lax.dynamic_slice(w, (0, c * width), (w.shape[0], width))

    row0 = jnp.concatenate([attn_gain, mlp_gain])[None]
    row1 = jnp.concatenate([query_gain, key_gain, jnp.zeros((112,), BF)])[None]
    gains = jnp.concatenate([row0, row1, jnp.zeros((62, 128), BF)], 0)
    w1 = jnp.concatenate(
        [cut(query_weight, QW), cut(key_matrix, HD), cut(value_matrix, HD), gains], 1
    )
    w2 = jnp.concatenate([cut(gate_weight, FW), cut(up_weight, FW)], 1)
    wo = out_weight.reshape(8, 16, D)
    wd = down_weight.reshape(8, 24, D)

    x_all, g_all, p_all, w1_all, wo_all, w2_all, wd_all = remote_call(
        start_body,
        [
            ((NC, T, D), BF, "h"), ((NC, T, D), BF, "h"), ((NC, 1, T), jnp.int32, "h"),
            ((NS, 64, WCOL1), BF, "h"), ((NS, 16, D), BF, "h"),
            ((NS, 64, WCOL2), BF, "h"), ((NS, 24, D), BF, "h"),
        ],
        "hhhhhhh", (tok, cot, positions, w1, wo, w2, wd), [], 128, 8, 0,
    )
    gain_attn = w1_all[:, 0, 512:576].reshape(1, D).astype(F32)
    gain_mlp = w1_all[:, 0, 576:640].reshape(1, D).astype(F32)
    gain_q = w1_all[:, 1, 512:520].reshape(HD).astype(F32)
    gain_k = w1_all[:, 1, 520:528].reshape(HD).astype(F32)
    wqkv = w1_all[:, :, 0:512].reshape(D, 512)
    wout = wo_all.reshape(QW, D)
    half = HD // 2
    freq = jnp.power(ROPE_BASE, -jnp.arange(half, dtype=F32) * (2.0 / HD))
    angle = p_all.reshape(SEQ).astype(F32)[:, None] * freq[None, :]
    cosine = jnp.concatenate([jnp.cos(angle)] * 2, -1)
    sine = jnp.concatenate([jnp.sin(angle)] * 2, -1)

    x = x_all.reshape(SEQ, D)
    normed_one, _ = rms_parts(x.astype(F32))
    hidden_one = (normed_one * gain_attn).astype(BF)
    raw = dot(hidden_one, wqkv, NN)
    value = raw[:, QW + HD :].astype(BF)
    q_raw = raw[:, :QW].reshape(SEQ, 2, HD)
    k_raw = raw[:, QW : QW + HD]
    q_normed, q_inverse = rms_parts(q_raw)
    k_normed, k_inverse = rms_parts(k_raw)
    cosine_q, sine_q = cosine[:, None, :], sine[:, None, :]
    queries = rotate(q_normed * gain_q, cosine_q, sine_q).astype(BF)
    keys = rotate(k_normed * gain_k, cosine, sine).astype(BF)
    scale = HD**-0.5
    scores = jnp.einsum("thd,nd->htn", queries, keys, preferred_element_type=F32) * scale
    order = jnp.arange(SEQ)
    allowed = order[None, :] <= order[:, None]
    scores = jnp.where(allowed, scores, BLOCKED_SCORE)
    top = jnp.max(scores, -1, keepdims=True)
    weights = jnp.where(allowed, jnp.exp(scores - top), 0.0)
    total = jnp.sum(weights, -1, keepdims=True)
    heads = (
        jnp.einsum("htn,nd->htd", weights.astype(BF), value, preferred_element_type=F32) / total
    )
    log_total = top + jnp.log(total)
    attended = jnp.transpose(heads, (1, 0, 2)).reshape(SEQ, QW).astype(BF)
    out_part = dot(attended, wout, NN, BF).reshape(NC, T, D)

    output, ga_all, grad_resid, ggain_mlp, gw2_sum, gwd_sum = remote_call(
        mid_body,
        [
            ((T, D), BF, "v"), ((NC, T, D), BF, "h"), ((T, D), F32, "v"), ((1, D), F32, "v"),
            ((64, WCOL2), BF, "v"), ((24, D), BF, "v"),
        ],
        "v" * 7,
        (out_part, tok, cot, gain_mlp, w2_all.reshape(D, 2 * FW), wd_all.reshape(FW, D), g_all),
        [
            pltpu.VMEM((NC, T, D), BF), pltpu.VMEM((NC, T, FW), BF), pltpu.VMEM((NC, T, 2 * FW), BF),
            pltpu.VMEM((NC, T, D), BF), pltpu.VMEM((NC, T, D), BF), pltpu.VMEM((T, D), F32),
            pltpu.VMEM((T, D), BF), pltpu.VMEM((2, 8, 64, WCOL2), BF), pltpu.VMEM((2, 8, 24, D), BF),
            pltpu.VMEM((FW, D), F32),
        ]
        + chunk_scratch() * 3 + shard_scratch((64, WCOL2)) + shard_scratch((24, D)),
        128, 8, 1, 58 << 20,
    )
    ga = ga_all.reshape(SEQ, D)
    gwo = by_owner(dot(attended, ga, TN, BF), 16)
    grad_att = dot(ga, wout, NT, BF).reshape(SEQ, 2, HD)
    delta = jnp.einsum("thd,htd->ht", grad_att.astype(F32), heads)
    scores = jnp.einsum("thd,nd->htn", queries, keys, preferred_element_type=F32) * scale
    probs = jnp.where(allowed, jnp.exp(scores - log_total), 0.0)
    probs_bf = probs.astype(BF)
    grad_value = jnp.einsum("htn,thd->nd", probs_bf, grad_att, preferred_element_type=F32)
    grad_probs = jnp.einsum("thd,nd->htn", grad_att, value, preferred_element_type=F32)
    grad_scores = (probs * (grad_probs - delta[..., None])).astype(BF)
    grad_q = jnp.einsum("htn,nd->thd", grad_scores, keys, preferred_element_type=F32) * scale
    grad_k = jnp.einsum("htn,thd->nd", grad_scores, queries, preferred_element_type=F32) * scale
    wq = rotate_reverse(grad_q, cosine_q, sine_q)
    wk = rotate_reverse(grad_k, cosine, sine)
    gq_gain = jnp.sum(wq * q_normed, (0, 1))
    gk_gain = jnp.sum(wk * k_normed, 0)
    gq = rms_back(wq * gain_q, q_normed, q_inverse).reshape(SEQ, QW).astype(BF)
    gk = rms_back(wk * gain_k, k_normed, k_inverse).astype(BF)
    gqkv = jnp.concatenate([gq, gk, grad_value.astype(BF)], 1)
    gw1 = by_owner(dot(hidden_one, gqkv, TN, BF), 64)
    in_part = dot(gqkv, wqkv, NT, BF).reshape(NC, T, D)
    gqk = jnp.concatenate([gq_gain, gk_gain])[None]

    outs = remote_call(
        end_body,
        [
            ((T, D), F32, "v"), ((1, SMALL), F32, "v"),
            ((64, 2048), F32, "v"), ((64, 1024), F32, "v"), ((64, 1024), F32, "v"),
            ((128, D), F32, "v"), ((64, 3072), F32, "v"), ((64, 3072), F32, "v"),
            ((192, D), F32, "v"),
        ],
        "v" * 10,
        (in_part, tok, grad_resid, gain_attn, ggain_mlp, gqk, gw1, gwo, gw2_sum, gwd_sum),
        chunk_scratch() + shard_scratch((64, 512)) + shard_scratch((16, D))
        + [
            pltpu.VMEM((64, 512), BF), pltpu.VMEM((16, D), BF),
            pltpu.VMEM((NC, 64, 512), BF), pltpu.VMEM((NC, 16, D), BF),
            pltpu.VMEM((NC, 64, WCOL2), BF), pltpu.VMEM((NC, 24, D), BF),
            pltpu.VMEM((24, D), BF),
            pltpu.VMEM((1, SMALL), F32), pltpu.VMEM((NC, 1, SMALL), F32),
            pltpu.VMEM((1, SMALL), F32), pltpu.VMEM((NS, 1, SMALL), F32),
        ],
        128, 8, 2, 56 << 20,
    )
    gx, small, gwq, gwk, gwv, gwo_out, gwg, gwu, gwd_out = outs
    small = small[0]

    def own(offset, width):
        return lax.dynamic_slice(small, (offset + s * width,), (width,))

    return (
        output[None], gx[None], own(0, 64), gwq, gwk, gwv, own(2 * D, 8), own(2 * D + HD, 8),
        gwo_out, own(D, 64), gwg, gwu, gwd_out,
    )


def solution(mesh):
    split = P("shard", "ctx", None)
    rows, vec = P("shard", None), P("shard")
    in_specs = (
        split, P("shard", "ctx"), vec, rows, rows, rows, vec, vec, rows, vec, rows, rows, rows, split,
    )
    out_specs = (split, split, vec, rows, rows, rows, vec, vec, rows, vec, rows, rows, rows)
    return jax.shard_map(shards, mesh=mesh, in_specs=in_specs, out_specs=out_specs, check_vma=False)
```

```python
import jax
import jax.numpy as jnp
from jax import lax
from jax.experimental import pallas as pl
from jax.experimental.pallas import tpu as pltpu
from jax.sharding import PartitionSpec as P

MESH = pl.DeviceIdType.MESH
BF = jnp.bfloat16
F32 = jnp.float32

NS = 16
NC = 8
T = 128
SEQ = 1024
D = 1024
HD = 128
QW = 256
FW = 384
EPSILON = 1e-06
ROPE_BASE = 1000000.0
BLOCKED_SCORE = -1e30
SMALL = 2304

ALL = slice(None)


def lanes(width):
    n = width // 128
    a = (n + 2) // 3 * 128
    b = a + (n + 1) // 3 * 128
    return ((ALL, slice(0, a)), (ALL, slice(a, b)), (ALL, slice(b, width)))


def view(ref, part):
    return ref.at[tuple(pl.ds(p.start, p.stop - p.start) if p != ALL else p for p in part)]


class Ring:
    def __init__(self, me, device):
        self.a = me // 2
        self.b = lax.rem(me, 2)
        self.device = device

    def idx(self, da, db):
        return lax.rem(self.a + da + 4, 4) * 2 + lax.rem(self.b + db, 2)

    def dev(self, da, db):
        return self.device(self.idx(da, db))


class Net:
    def __init__(self, send, recv, local):
        self.s, self.r, self.l = send, recv, local
        self.n = 0
        self.m = 0

    def send(self, src, dst, to):
        k = self.n
        self.n += 1
        c = pltpu.make_async_remote_copy(
            src_ref=src, dst_ref=dst, send_sem=self.s.at[k], recv_sem=self.r.at[k],
            device_id=to, device_id_type=MESH,
        )
        c.start()
        return c

    def copy(self, src, dst):
        k = self.m
        self.m += 1
        c = pltpu.make_async_copy(src, dst, self.l.at[k])
        c.start()
        return c


def places():
    s = lax.axis_index("shard")
    c = lax.axis_index("ctx")
    core = lax.rem(s, 2)
    ctx = Ring(c, lambda i: (s, i))
    chips = Ring(s // 2, lambda i: (i * 2 + core, c))
    sibling = (s + 1 - 2 * core, c)
    half, rest = lax.rem(s, 2), s // 2
    goes = (8 * half + c, rest)
    comes = (2 * c + s // 8, lax.rem(s, 8))
    stays = jnp.logical_and(goes[0] == s, goes[1] == c)
    return s, c, core, ctx, chips, sibling, goes, comes, stays


def ring_devices(ring):
    return [ring.dev(-1, 0), ring.dev(1, 0), ring.dev(0, 1)]


def greet(devices, moved=None):
    barrier = pltpu.get_barrier_semaphore()
    for d in devices:
        pl.semaphore_signal(barrier, inc=1, device_id=d, device_id_type=MESH)
    if moved is not None:
        goes, comes, stays = moved

        @pl.when(jnp.logical_not(stays))
        def _():
            for d in (goes, comes):
                pl.semaphore_signal(barrier, inc=1, device_id=d, device_id_type=MESH)
            pl.semaphore_wait(barrier, len(devices) + 2)

        @pl.when(stays)
        def _():
            pl.semaphore_wait(barrier, len(devices))

    else:
        pl.semaphore_wait(barrier, len(devices))


def drive(*threads):
    threads = list(threads)
    while threads:
        for t in list(threads):
            try:
                next(t)
            except StopIteration:
                threads.remove(t)


def move(net, items, to, stays):
    base = net.n
    net.n += len(items)

    def remote(k, src, dst):
        return pltpu.make_async_remote_copy(
            src_ref=src, dst_ref=dst, send_sem=net.s.at[base + k], recv_sem=net.r.at[base + k],
            device_id=to, device_id_type=MESH,
        )

    @pl.when(jnp.logical_not(stays))
    def _():
        for k, (src, dst) in enumerate(items):
            remote(k, src, dst).start()

    @pl.when(stays)
    def _():
        for k, (src, dst) in enumerate(items):
            pltpu.make_async_copy(src, dst, net.r.at[base + k]).start()

    yield

    @pl.when(jnp.logical_not(stays))
    def _():
        for k, (src, dst) in enumerate(items):
            remote(k, src, dst).wait()

    @pl.when(stays)
    def _():
        for k, (src, dst) in enumerate(items):
            pltpu.make_async_copy(src, dst, net.r.at[base + k]).wait()


def gather(net, ring, items, slot=lambda i: i, sibling=None):
    left, right, pair = ring_devices(ring)
    me = ring.idx(0, 0)
    over = []

    def pass_on(places):
        if sibling is not None:
            for _, at, _ in items:
                for i in places:
                    over.append(net.send(at(slot(i)), at(slot(i)), sibling))

    first, local = [], []
    for own, at, _ in items:
        here = at(slot(me))
        src = here if own is None else own
        for n in (left, right, pair):
            first.append(net.send(src, here, n))
        if sibling is not None:
            over.append(net.send(src, here, sibling))
        if own is not None:
            local.append(net.copy(own, here))
    yield
    for c in first:
        c.wait_recv()
    second = []
    a, b, z = ring.idx(-1, 0), ring.idx(1, 0), ring.idx(0, 1)
    for _, at, _ in items:
        for i, n in ((a, right), (z, left), (a, pair)):
            second.append(net.send(at(slot(i)), at(slot(i)), n))
    pass_on((a, b, z))
    yield
    for c in second:
        c.wait_recv()
    third = []
    az, bz, o, oz = ring.idx(-1, 1), ring.idx(1, 1), ring.idx(2, 0), ring.idx(2, 1)
    for _, at, parts in items:
        for i, n, part in ((az, right, parts[0]), (bz, left, parts[1]), (o, pair, parts[2])):
            if part is not None:
                r = view(at(slot(i)), part)
                third.append(net.send(r, r, n))
    pass_on((az, bz, o))
    yield
    for c in third:
        c.wait_recv()
    pass_on((oz,))
    for c in local:
        c.wait()
    for c in first + second + third:
        c.wait_send()
    if sibling is not None:
        yield
        for c in over:
            c.wait()


def reduce(net, ring, items, result):
    left, right, pair = ring_devices(ring)
    me, a, b, z = ring.idx(0, 0), ring.idx(-1, 0), ring.idx(1, 0), ring.idx(0, 1)
    az, bz, o, oz = ring.idx(-1, 1), ring.idx(1, 1), ring.idx(2, 0), ring.idx(2, 1)

    def plus(x, y):
        return (x.astype(F32) + y.astype(F32)).astype(BF)

    first, second, third = [], [], []
    for p, parts, land, _ in items:
        for n, part in zip((left, right, pair), parts):
            first.append(net.send(view(p(oz), part), view(land.at[0], part), n))
    yield
    for c in first:
        c.wait_recv()
    for p, parts, land, sums in items:
        for k, (i, part, n) in enumerate(
            ((o, parts[2], left), (bz, parts[1], right), (az, parts[0], pair))
        ):
            sums[k] = p(i)[...]
            sums[(k,) + part] = plus(p(i)[part], land[(0,) + part])
            second.append(net.send(sums.at[k], land.at[1 + k], n))
    yield
    for c in second:
        c.wait_recv()
    for p, parts, land, sums in items:
        third.append(net.send(p(b), land.at[5], right))
        sums[4] = plus(p(z)[...], land[2])
        third.append(net.send(sums.at[4], land.at[6], pair))
        sums[3] = (p(a)[...].astype(F32) + land[1].astype(F32) + land[3].astype(F32)).astype(BF)
        third.append(net.send(sums.at[3], land.at[4], left))
    yield
    for c in third:
        c.wait_recv()
    for k, (p, parts, land, sums) in enumerate(items):
        result(
            k,
            (p(me)[...].astype(F32) + land[4].astype(F32))
            + (land[5].astype(F32) + land[6].astype(F32)),
        )
    for c in first + second + third:
        c.wait_send()


def at(ref):
    return lambda i: ref.at[i]


CHUNKS = 2
CROWS = T // CHUNKS
CPARTS = ((slice(0, 32), ALL), (slice(32, 48), ALL), (slice(48, 64), ALL))


def rows(h):
    return pl.ds(CROWS * h, CROWS)


def chunk(ref, h):
    return lambda i: ref.at[i, rows(h)]


def chunk_scratch():
    return [pltpu.VMEM((7, CROWS, D), BF), pltpu.VMEM((5, CROWS, D), BF)] * CHUNKS


def reduce_scratch(shape):
    return [pltpu.VMEM((7,) + shape, BF), pltpu.VMEM((5,) + shape, BF)]


def reduce_shard(net, chips, core, sibling, items, result):
    over = []
    for p, _, half, _, _, _ in items:
        over.append(net.send(p.at[1 - core], half, sibling))
    yield
    for c in over:
        c.wait_recv()
    for p, _, half, both, _, _ in items:

        @pl.loop(0, 8)
        def _(j):
            both[j] = (p[core, j].astype(F32) + half[j].astype(F32)).astype(BF)

    yield from reduce(net, chips, [(at(i[3]), i[1], i[4], i[5]) for i in items], result)
    for c in over:
        c.wait_send()


def shard_scratch(shape):
    return [pltpu.VMEM((8,) + shape, BF), pltpu.VMEM((8,) + shape, BF)] + reduce_scratch(shape)


def rms_parts(v):
    inverse = lax.rsqrt(jnp.mean(v * v, -1, keepdims=True) + EPSILON)
    return v * inverse, inverse


def rms_back(g, n, inverse):
    return inverse * (g - n * jnp.mean(g * n, -1, keepdims=True))


def dot(a, b, dims, out=F32):
    return lax.dot_general(a, b, (dims, ((), ())), preferred_element_type=F32).astype(out)


NN = ((1,), (0,))
NT = ((1,), (1,))
TN = ((0,), (0,))


def remote_call(body, outs, ins, args, scratch, copies, locals_, number, vmem=None):
    sems = [
        pltpu.SemaphoreType.DMA((copies,)),
        pltpu.SemaphoreType.DMA((copies,)),
        pltpu.SemaphoreType.DMA((locals_,)),
    ]
    space = {"v": pl.BlockSpec(memory_space=pltpu.VMEM), "h": pl.BlockSpec(memory_space=pl.ANY)}
    return pl.pallas_call(
        body,
        out_shape=[jax.ShapeDtypeStruct(s, d) for s, d, _ in outs],
        in_specs=[space[k] for k in ins],
        out_specs=[space[k] for _, _, k in outs],
        scratch_shapes=list(scratch) + sems,
        compiler_params=pltpu.CompilerParams(
            collective_id=number, has_side_effects=True, vmem_limit_bytes=vmem
        ),
    )(*args)


WCOL1 = 640
WCOL2 = 768


def start_body(
    tok, cot, pos, w1, wo, w2, wd, freq,
    g_all, w1_all, wo_all, w2_all, wd_all, hid, raw, qkv, tab, lse, heads, part, gvec, ghead,
    x_all, p_all, ss, rs, ls,
):
    s, c, core, ctx, chips, sibling, goes, comes, stays = places()
    net = Net(ss, rs, ls)
    greet(ring_devices(ctx) + ring_devices(chips) + [sibling], (goes, comes, stays))

    def by_shard():
        moved = [(wo.at[c], wo_all.at[goes[0]]), (wd.at[c], wd_all.at[goes[0]])]
        yield from move(net, moved, goes, stays)
        yield from gather(
            net, chips, [(w1, at(w1_all), lanes(WCOL1)), (None, at(wo_all), lanes(D))],
            lambda i: i * 2 + core, sibling,
        )

    def first(h):
        items = [(tok.at[rows(h)], chunk(x_all, h), CPARTS)]
        if h == 0:
            items.append((pos, at(p_all), ((ALL, ALL), None, None)))
        yield from gather(net, ctx, items)

    drive(first(0), first(1), by_shard())

    def second(h):
        yield from gather(net, ctx, [(cot.at[rows(h)], chunk(g_all, h), CPARTS)])

    def by_shard_second():
        yield from gather(
            net, chips, [(w2, at(w2_all), lanes(WCOL2)), (None, at(wd_all), lanes(D))],
            lambda i: i * 2 + core, sibling,
        )

    def gains():
        lane = lax.broadcasted_iota(jnp.int32, (8, 128), 1)
        t = [w1_all[i, 0:16, 512:640].astype(F32)[0:8] for i in range(NS)]
        for j in range(8):
            x, y = t[2 * j], t[2 * j + 1]
            low = lane < 64
            gvec[0:1, 128 * j : 128 * (j + 1)] = jnp.where(low, x, pltpu.roll(y, 64, 1))[0:1]
            gvec[1:2, 128 * j : 128 * (j + 1)] = jnp.where(low, pltpu.roll(x, 64, 1), y)[0:1]
        q = jnp.zeros((8, 128), F32)
        k = jnp.zeros((8, 128), F32)
        for i in range(NS):
            here = lane // 8 == i
            q = jnp.where(here, pltpu.roll(t[i], 8 * i, 1), q)
            k = jnp.where(here, pltpu.roll(t[i], (8 * i + 120) % 128, 1), k)
        ghead[0:1] = q[1:2]
        ghead[1:2] = k[1:2]

    def project(i):
        normed, _ = rms_parts(x_all[i].astype(F32))
        h = (normed * gvec[0:1]).astype(BF)
        hid[i] = h
        r = dot(h, w1_all[:, :, 0:512].reshape(D, 512), NN)
        raw[i] = r
        angle = freq[...] * p_all[i].astype(F32)
        cosine = jnp.cos(angle).T
        sine = jnp.sin(angle).T
        sine = jnp.where(lax.broadcasted_iota(jnp.int32, (T, HD), 1) < HD // 2, -sine, sine)
        tab[i, :, 0:HD] = cosine
        tab[i, :, HD:] = sine
        for k in range(3):
            n, _ = rms_parts(r[:, HD * k : HD * (k + 1)])
            u = n * ghead[k // 2 : k // 2 + 1]
            qkv[i, :, HD * k : HD * (k + 1)] = (u * cosine + pltpu.roll(u, 64, 1) * sine).astype(BF)
        qkv[i, :, 3 * HD :] = r[:, 3 * HD :].astype(BF)

    def attend(h, n):
        width = 256 * (n + 1)
        q = qkv[2 * n : 2 * n + 2, :, HD * h : HD * (h + 1)].reshape(256, HD)
        k = qkv[0 : 2 * n + 2, :, 2 * HD : 3 * HD].reshape(width, HD)
        v = qkv[0 : 2 * n + 2, :, 3 * HD :].reshape(width, HD)
        score = dot(q, k, NT) * HD**-0.5
        row = lax.broadcasted_iota(jnp.int32, (256, width), 0) + 256 * n
        col = lax.broadcasted_iota(jnp.int32, (256, width), 1)
        score = jnp.where(col <= row, score, BLOCKED_SCORE)
        top = jnp.max(score, -1, keepdims=True)
        e = jnp.exp(score - top)
        total = jnp.sum(e, -1, keepdims=True)
        o = dot(e.astype(BF), v, NN) / total
        heads[2 * n : 2 * n + 2, :, HD * h : HD * (h + 1)] = o.reshape(2, T, HD)
        lse[h, 256 * n : 256 * (n + 1)] = top + jnp.log(total)

    def work():
        gains()
        pl.loop(0, 4)(project)
        yield
        pl.loop(4, 8)(project)
        for h in range(2):
            attend(h, 0)
        yield
        for n in range(1, 4):
            for h in range(2):
                attend(h, n)
            if n < 3:
                yield

        @pl.loop(0, NC)
        def _(i):
            part[i] = dot(heads[i].astype(BF), wo_all[...].reshape(QW, D), NN, BF)

    drive(second(0), second(1), by_shard_second(), work())


def mid_body(
    part, tok, cot, gain, wgu, wd, g_all,
    out_ref, ga_all, gres_ref, ggain_ref, gw2_sum, gwd_sum,
    h_all, mixed, ggu, down_part, back_part, resid, ga, gw2, gwd, gwd_f,
    la0, sa0, la1, sa1, lb0, sb0, lb1, sb1, lc0, sc0, lc1, sc1,
    h1, b1, l1, t1, h2, b2, l2, t2, ss, rs, ls,
):
    s, c, core, ctx, chips, sibling, goes, comes, stays = places()
    net = Net(ss, rs, ls)
    greet(ring_devices(ctx) + ring_devices(chips) + [sibling])

    def forward(h, land, sums):
        def got(k, total):
            r = tok[rows(h)].astype(F32) + total
            resid[rows(h)] = r
            normed, _ = rms_parts(r)
            h_all[c, rows(h)] = (normed * gain[...]).astype(BF)

        yield from reduce(net, ctx, [(chunk(part, h), CPARTS, land, sums)], got)
        yield from gather(net, ctx, [(None, chunk(h_all, h), CPARTS)])

    def block(i):
        both = dot(h_all[i], wgu[...], NN)
        gate, up = both[:, :FW], both[:, FW:]
        sig = jax.nn.sigmoid(gate)
        act = gate * sig
        m = (act * up).astype(BF)
        mixed[i] = m
        gm = dot(g_all[i], wd[...], NT)
        gg = (gm * up * sig * (1.0 + gate * (1.0 - sig))).astype(BF)
        gu = (gm * act).astype(BF)
        ggu[i, :, 0:FW] = gg
        ggu[i, :, FW:] = gu
        back_part[i] = dot(jnp.concatenate([gg, gu], 1), wgu[...], NT, BF)
        down_part[i] = dot(m, wd[...], NN, BF)

    def blocks(places):
        n = len(places)

        @pl.loop(0, n)
        def _(j):
            i = places[0]
            for k in range(1, n):
                i = jnp.where(j == k, places[k], i)
            block(i)

    def work():
        yield
        yield
        yield
        blocks([c])
        yield
        blocks([ctx.idx(-1, 0), ctx.idx(1, 0), ctx.idx(0, 1)])
        yield
        blocks([ctx.idx(-1, 1), ctx.idx(1, 1), ctx.idx(2, 0)])
        yield
        blocks([ctx.idx(2, 1)])

    drive(forward(0, la0, sa0), forward(1, la1, sa1), work())

    def got_back(h):
        def got(k, total):
            normed, inverse = rms_parts(resid[rows(h)])
            g = jnp.sum(total * normed, 0, keepdims=True)
            if h == 0:
                ggain_ref[...] = g
            else:
                ggain_ref[...] += g
            gres = cot[rows(h)].astype(F32) + rms_back(total * gain[...], normed, inverse)
            gres_ref[rows(h)] = gres
            ga[rows(h)] = gres.astype(BF)

        return got

    def backward(h, land, sums):
        yield from reduce(net, ctx, [(chunk(back_part, h), CPARTS, land, sums)], got_back(h))
        yield from gather(net, ctx, [(ga.at[rows(h)], chunk(ga_all, h), CPARTS)])

    def later(h, land, sums):
        def got(k, total):
            out_ref[rows(h)] = (resid[rows(h)] + total).astype(BF)

        yield
        yield
        yield
        yield
        yield from reduce(net, ctx, [(chunk(down_part, h), CPARTS, land, sums)], got)

    def got_shard(k, total):
        (gw2_sum, gwd_sum)[k][...] = total.astype(BF)

    def grads():
        for q in range(2):

            @pl.loop(4 * q, 4 * q + 4)
            def _(j):
                left = h_all[:, :, pl.ds(pl.multiple_of(j * 128, 128), 128)].reshape(SEQ, 128)
                g = dot(left, ggu[...].reshape(SEQ, 2 * FW), TN, BF)
                gw2[0, j] = g[0:64]
                gw2[1, j] = g[64:128]

            yield
        for j in range(3):
            left = mixed[:, :, 128 * j : 128 * (j + 1)].reshape(SEQ, 128)
            gwd_f[128 * j : 128 * (j + 1)] = dot(left, g_all[...].reshape(SEQ, D), TN)
        for i in range(NS):
            gwd[i % 2, i // 2] = gwd_f[24 * i : 24 * (i + 1)].astype(BF)
        yield
        yield from reduce_shard(
            net, chips, core, sibling,
            [(gw2, lanes(WCOL2), h1, b1, l1, t1), (gwd, lanes(D), h2, b2, l2, t2)], got_shard,
        )

    drive(
        backward(0, lb0, sb0), backward(1, lb1, sb1),
        later(0, lc0, sc0), later(1, lc1, sc1), grads(),
    )


def end_body(
    part, tok, gres_ref, gain, ggain, gqk, gw1, gwo, gw2_sum, gwd_sum,
    gx_ref, small_ref, q_out, k_out, v_out, o_out, gate_out, up_out, down_out,
    la0, sa0, la1, sa1, h1, b1, l1, t1, h2, b2, l2, t2,
    s1, so, a1, ao, a2, ad, own_d, sm, smc, sm2, sms, ss, rs, ls,
):
    s, c, core, ctx, chips, sibling, goes, comes, stays = places()
    net = Net(ss, rs, ls)
    ctx_peers = [(s, lax.rem(c + d, NC)) for d in range(1, NC)]
    shard_peers = [(lax.rem(s + d, NS), c) for d in range(1, NS)]
    greet(ctx_peers + shard_peers, (goes, comes, stays))

    def got_input(h):
        def got(k, total):
            normed, inverse = rms_parts(tok[rows(h)].astype(F32))
            g = jnp.sum(total * normed, 0, keepdims=True)
            if h == 0:
                sm[:, 0:D] = g
            else:
                sm[:, 0:D] += g
            gx_ref[rows(h)] = gres_ref[rows(h)] + rms_back(total * gain[...], normed, inverse)

        return got

    def by_ctx(h, land, sums):
        yield from reduce(net, ctx, [(chunk(part, h), CPARTS, land, sums)], got_input(h))

    def small():
        yield
        yield
        yield
        yield
        sm[:, D : 2 * D] = ggain[...]
        sm[:, 2 * D :] = gqk[...]
        smc[c] = sm[...]
        sent = [net.send(sm, smc.at[c], d) for d in ctx_peers]
        yield
        for x in sent:
            x.wait()
        total = smc[0]
        for i in range(1, NC):
            total = total + smc[i]
        sm2[...] = total
        sms[s] = total
        sent = [net.send(sm2, sms.at[s], d) for d in shard_peers]
        yield
        for x in sent:
            x.wait()
        total = sms[0]
        for i in range(1, NS):
            total = total + sms[i]
        small_ref[...] = total

    def mlp():
        yield
        yield
        yield from move(net, [(gwd_sum, own_d)], comes, stays)
        yield from gather(net, ctx, [(gw2_sum, at(a2), lanes(WCOL2)), (own_d, at(ad), lanes(D))])
        for i in range(NC):
            gate_out[:, FW * i : FW * (i + 1)] = a2[i, :, 0:FW].astype(F32)
            up_out[:, FW * i : FW * (i + 1)] = a2[i, :, FW : 2 * FW].astype(F32)
            down_out[24 * i : 24 * (i + 1), :] = ad[i].astype(F32)

    def got_shard(k, total):
        (s1, so)[k][...] = total.astype(BF)

    def attn():
        yield from reduce_shard(
            net, chips, core, sibling,
            [(gw1, lanes(512), h1, b1, l1, t1), (gwo, lanes(D), h2, b2, l2, t2)], got_shard,
        )
        yield from move(net, [(so, ao.at[comes[1]])], comes, stays)
        yield from gather(net, ctx, [(s1, at(a1), lanes(512)), (None, at(ao), lanes(D))])
        for i in range(NC):
            q_out[:, QW * i : QW * (i + 1)] = a1[i, :, 0:QW].astype(F32)
            k_out[:, HD * i : HD * (i + 1)] = a1[i, :, QW : QW + HD].astype(F32)
            v_out[:, HD * i : HD * (i + 1)] = a1[i, :, QW + HD :].astype(F32)
            o_out[16 * i : 16 * (i + 1), :] = ao[i].astype(F32)

    drive(by_ctx(0, la0, sa0), by_ctx(1, la1, sa1), small(), attn(), mlp())


def rotate(values, cosine, sine):
    turned = jnp.concatenate([-values[..., HD // 2 :], values[..., : HD // 2]], -1)
    return values * cosine + turned * sine


def rotate_reverse(grads, cosine, sine):
    t = grads * sine
    return grads * cosine + jnp.concatenate([t[..., HD // 2 :], -t[..., : HD // 2]], -1)


def by_owner(g, rows):
    return jnp.transpose(g.reshape(8, 2, rows, g.shape[1]), (1, 0, 2, 3))


def shards(
    tokens, positions, attn_gain, query_weight, key_matrix, value_matrix, query_gain, key_gain,
    out_weight, mlp_gain, gate_weight, up_weight, down_weight, cotangent,
):
    c = lax.axis_index("ctx")
    s = lax.axis_index("shard")
    tok, cot = tokens[0], cotangent[0]

    def cut(w, width):
        return lax.dynamic_slice(w, (0, c * width), (w.shape[0], width))

    row0 = jnp.concatenate([attn_gain, mlp_gain])[None]
    row1 = jnp.concatenate([query_gain, key_gain, jnp.zeros((112,), BF)])[None]
    gains = jnp.concatenate([row0, row1, jnp.zeros((62, 128), BF)], 0)
    w1 = jnp.concatenate(
        [cut(query_weight, QW), cut(key_matrix, HD), cut(value_matrix, HD), gains], 1
    )
    w2 = jnp.concatenate([cut(gate_weight, FW), cut(up_weight, FW)], 1)
    wo = out_weight.reshape(8, 16, D)
    wd = down_weight.reshape(8, 24, D)

    half = HD // 2
    freq = jnp.power(ROPE_BASE, -jnp.arange(half, dtype=F32) * (2.0 / HD))
    freq = jnp.broadcast_to(jnp.concatenate([freq, freq])[:, None], (HD, T))

    (
        g_all, w1_all, wo_all, w2_all, wd_all, hid, raw, qkv, tab, lse, heads, out_part, gvec, ghead,
    ) = remote_call(
        start_body,
        [
            ((NC, T, D), BF, "h"), ((NS, 64, WCOL1), BF, "v"), ((NS, 16, D), BF, "v"),
            ((NS, 64, WCOL2), BF, "h"), ((NS, 24, D), BF, "h"),
            ((NC, T, D), BF, "v"), ((NC, T, 512), F32, "v"), ((NC, T, 512), BF, "v"),
            ((NC, T, 2 * HD), F32, "v"), ((2, SEQ, 1), F32, "v"), ((NC, T, QW), F32, "v"),
            ((NC, T, D), BF, "v"), ((2, D), F32, "v"), ((2, HD), F32, "v"),
        ],
        "hhhhhhhv", (tok, cot, positions, w1, wo, w2, wd, freq),
        [pltpu.VMEM((NC, T, D), BF), pltpu.VMEM((NC, 1, T), jnp.int32)], 128, 8, 0, 56 << 20,
    )
    gain_attn, gain_mlp = gvec[0:1], gvec[1:2]
    wqkv = w1_all[:, :, 0:512].reshape(D, 512)
    wout = wo_all.reshape(QW, D)
    cosine, sine = tab.reshape(SEQ, 2 * HD)[:, :HD], tab.reshape(SEQ, 2 * HD)[:, HD:]
    sine = jnp.concatenate([-sine[:, :half], sine[:, half:]], 1)
    cosine_q, sine_q = cosine[:, None, :], sine[:, None, :]
    gain_q, gain_k = ghead[0], ghead[1]
    hidden_one = hid.reshape(SEQ, D)
    raw = raw.reshape(SEQ, 512)
    q_normed, q_inverse = rms_parts(raw[:, :QW].reshape(SEQ, 2, HD))
    k_normed, k_inverse = rms_parts(raw[:, QW : QW + HD])
    qkv = qkv.reshape(SEQ, 512)
    queries, keys, value = qkv[:, :QW].reshape(SEQ, 2, HD), qkv[:, QW : QW + HD], qkv[:, QW + HD :]
    scale = HD**-0.5
    order = jnp.arange(SEQ)
    allowed = order[None, :] <= order[:, None]
    log_total = lse
    attended = heads.reshape(SEQ, QW).astype(BF)
    heads = jnp.transpose(heads.reshape(SEQ, 2, HD), (1, 0, 2))

    output, ga_all, grad_resid, ggain_mlp, gw2_sum, gwd_sum = remote_call(
        mid_body,
        [
            ((T, D), BF, "v"), ((NC, T, D), BF, "h"), ((T, D), F32, "v"), ((1, D), F32, "v"),
            ((64, WCOL2), BF, "v"), ((24, D), BF, "v"),
        ],
        "v" * 7,
        (out_part, tok, cot, gain_mlp, w2_all.reshape(D, 2 * FW), wd_all.reshape(FW, D), g_all),
        [
            pltpu.VMEM((NC, T, D), BF), pltpu.VMEM((NC, T, FW), BF), pltpu.VMEM((NC, T, 2 * FW), BF),
            pltpu.VMEM((NC, T, D), BF), pltpu.VMEM((NC, T, D), BF), pltpu.VMEM((T, D), F32),
            pltpu.VMEM((T, D), BF), pltpu.VMEM((2, 8, 64, WCOL2), BF), pltpu.VMEM((2, 8, 24, D), BF),
            pltpu.VMEM((FW, D), F32),
        ]
        + chunk_scratch() * 3 + shard_scratch((64, WCOL2)) + shard_scratch((24, D)),
        128, 8, 1, 58 << 20,
    )
    ga = ga_all.reshape(SEQ, D)
    gwo = by_owner(dot(attended, ga, TN, BF), 16)
    grad_att = dot(ga, wout, NT, BF).reshape(SEQ, 2, HD)
    delta = jnp.einsum("thd,htd->ht", grad_att.astype(F32), heads)
    scores = jnp.einsum("thd,nd->htn", queries, keys, preferred_element_type=F32) * scale
    probs = jnp.where(allowed, jnp.exp(scores - log_total), 0.0)
    probs_bf = probs.astype(BF)
    grad_value = jnp.einsum("htn,thd->nd", probs_bf, grad_att, preferred_element_type=F32)
    grad_probs = jnp.einsum("thd,nd->htn", grad_att, value, preferred_element_type=F32)
    grad_scores = (probs * (grad_probs - delta[..., None])).astype(BF)
    grad_q = jnp.einsum("htn,nd->thd", grad_scores, keys, preferred_element_type=F32) * scale
    grad_k = jnp.einsum("htn,thd->nd", grad_scores, queries, preferred_element_type=F32) * scale
    wq = rotate_reverse(grad_q, cosine_q, sine_q)
    wk = rotate_reverse(grad_k, cosine, sine)
    gq_gain = jnp.sum(wq * q_normed, (0, 1))
    gk_gain = jnp.sum(wk * k_normed, 0)
    gq = rms_back(wq * gain_q, q_normed, q_inverse).reshape(SEQ, QW).astype(BF)
    gk = rms_back(wk * gain_k, k_normed, k_inverse).astype(BF)
    gqkv = jnp.concatenate([gq, gk, grad_value.astype(BF)], 1)
    gw1 = by_owner(dot(hidden_one, gqkv, TN, BF), 64)
    in_part = dot(gqkv, wqkv, NT, BF).reshape(NC, T, D)
    gqk = jnp.concatenate([gq_gain, gk_gain])[None]

    outs = remote_call(
        end_body,
        [
            ((T, D), F32, "v"), ((1, SMALL), F32, "v"),
            ((64, 2048), F32, "v"), ((64, 1024), F32, "v"), ((64, 1024), F32, "v"),
            ((128, D), F32, "v"), ((64, 3072), F32, "v"), ((64, 3072), F32, "v"),
            ((192, D), F32, "v"),
        ],
        "v" * 10,
        (in_part, tok, grad_resid, gain_attn, ggain_mlp, gqk, gw1, gwo, gw2_sum, gwd_sum),
        chunk_scratch() + shard_scratch((64, 512)) + shard_scratch((16, D))
        + [
            pltpu.VMEM((64, 512), BF), pltpu.VMEM((16, D), BF),
            pltpu.VMEM((NC, 64, 512), BF), pltpu.VMEM((NC, 16, D), BF),
            pltpu.VMEM((NC, 64, WCOL2), BF), pltpu.VMEM((NC, 24, D), BF),
            pltpu.VMEM((24, D), BF),
            pltpu.VMEM((1, SMALL), F32), pltpu.VMEM((NC, 1, SMALL), F32),
            pltpu.VMEM((1, SMALL), F32), pltpu.VMEM((NS, 1, SMALL), F32),
        ],
        128, 8, 2, 56 << 20,
    )
    gx, small, gwq, gwk, gwv, gwo_out, gwg, gwu, gwd_out = outs
    small = small[0]

    def own(offset, width):
        return lax.dynamic_slice(small, (offset + s * width,), (width,))

    return (
        output[None], gx[None], own(0, 64), gwq, gwk, gwv, own(2 * D, 8), own(2 * D + HD, 8),
        gwo_out, own(D, 64), gwg, gwu, gwd_out,
    )


def solution(mesh):
    split = P("shard", "ctx", None)
    rows, vec = P("shard", None), P("shard")
    in_specs = (
        split, P("shard", "ctx"), vec, rows, rows, rows, vec, vec, rows, vec, rows, rows, rows, split,
    )
    out_specs = (split, split, vec, rows, rows, rows, vec, vec, rows, vec, rows, rows, rows)
    return jax.shard_map(shards, mesh=mesh, in_specs=in_specs, out_specs=out_specs, check_vma=False)
```

```python
import jax
import jax.numpy as jnp
from jax import lax
from jax.experimental import pallas as pl
from jax.experimental.pallas import tpu as pltpu
from jax.sharding import PartitionSpec as P

MESH = pl.DeviceIdType.MESH
BF = jnp.bfloat16
F32 = jnp.float32

NS = 16
NC = 8
T = 128
SEQ = 1024
D = 1024
HD = 128
QW = 256
FW = 384
EPSILON = 1e-06
ROPE_BASE = 1000000.0
BLOCKED_SCORE = -1e30
SMALL = 2304

ALL = slice(None)


def lanes(width):
    n = width // 128
    a = (n + 2) // 3 * 128
    b = a + (n + 1) // 3 * 128
    return ((ALL, slice(0, a)), (ALL, slice(a, b)), (ALL, slice(b, width)))


def view(ref, part):
    return ref.at[tuple(pl.ds(p.start, p.stop - p.start) if p != ALL else p for p in part)]


class Ring:
    def __init__(self, me, device):
        self.a = me // 2
        self.b = lax.rem(me, 2)
        self.device = device

    def idx(self, da, db):
        return lax.rem(self.a + da + 4, 4) * 2 + lax.rem(self.b + db, 2)

    def dev(self, da, db):
        return self.device(self.idx(da, db))


class Net:
    def __init__(self, send, recv, local):
        self.s, self.r, self.l = send, recv, local
        self.n = 0
        self.m = 0

    def send(self, src, dst, to):
        k = self.n
        self.n += 1
        c = pltpu.make_async_remote_copy(
            src_ref=src, dst_ref=dst, send_sem=self.s.at[k], recv_sem=self.r.at[k],
            device_id=to, device_id_type=MESH,
        )
        c.start()
        return c

    def copy(self, src, dst):
        k = self.m
        self.m += 1
        c = pltpu.make_async_copy(src, dst, self.l.at[k])
        c.start()
        return c


def places():
    s = lax.axis_index("shard")
    c = lax.axis_index("ctx")
    core = lax.rem(s, 2)
    ctx = Ring(c, lambda i: (s, i))
    chips = Ring(s // 2, lambda i: (i * 2 + core, c))
    sibling = (s + 1 - 2 * core, c)
    half, rest = lax.rem(s, 2), s // 2
    goes = (8 * half + c, rest)
    comes = (2 * c + s // 8, lax.rem(s, 8))
    stays = jnp.logical_and(goes[0] == s, goes[1] == c)
    return s, c, core, ctx, chips, sibling, goes, comes, stays


def ring_devices(ring):
    return [ring.dev(-1, 0), ring.dev(1, 0), ring.dev(0, 1)]


def greet(devices, moved=None):
    barrier = pltpu.get_barrier_semaphore()
    for d in devices:
        pl.semaphore_signal(barrier, inc=1, device_id=d, device_id_type=MESH)
    if moved is not None:
        goes, comes, stays = moved

        @pl.when(jnp.logical_not(stays))
        def _():
            for d in (goes, comes):
                pl.semaphore_signal(barrier, inc=1, device_id=d, device_id_type=MESH)
            pl.semaphore_wait(barrier, len(devices) + 2)

        @pl.when(stays)
        def _():
            pl.semaphore_wait(barrier, len(devices))

    else:
        pl.semaphore_wait(barrier, len(devices))


def drive(*threads):
    threads = list(threads)
    while threads:
        for t in list(threads):
            try:
                next(t)
            except StopIteration:
                threads.remove(t)


def move(net, items, to, stays):
    base = net.n
    net.n += len(items)

    def remote(k, src, dst):
        return pltpu.make_async_remote_copy(
            src_ref=src, dst_ref=dst, send_sem=net.s.at[base + k], recv_sem=net.r.at[base + k],
            device_id=to, device_id_type=MESH,
        )

    @pl.when(jnp.logical_not(stays))
    def _():
        for k, (src, dst) in enumerate(items):
            remote(k, src, dst).start()

    @pl.when(stays)
    def _():
        for k, (src, dst) in enumerate(items):
            pltpu.make_async_copy(src, dst, net.r.at[base + k]).start()

    yield

    @pl.when(jnp.logical_not(stays))
    def _():
        for k, (src, dst) in enumerate(items):
            remote(k, src, dst).wait()

    @pl.when(stays)
    def _():
        for k, (src, dst) in enumerate(items):
            pltpu.make_async_copy(src, dst, net.r.at[base + k]).wait()


def gather(net, ring, items, slot=lambda i: i, sibling=None):
    left, right, pair = ring_devices(ring)
    me = ring.idx(0, 0)
    over = []

    def pass_on(places):
        if sibling is not None:
            for _, at, _ in items:
                for i in places:
                    over.append(net.send(at(slot(i)), at(slot(i)), sibling))

    first, local = [], []
    for own, at, _ in items:
        here = at(slot(me))
        src = here if own is None else own
        for n in (left, right, pair):
            first.append(net.send(src, here, n))
        if sibling is not None:
            over.append(net.send(src, here, sibling))
        if own is not None:
            local.append(net.copy(own, here))
    yield
    for c in first:
        c.wait_recv()
    second = []
    a, b, z = ring.idx(-1, 0), ring.idx(1, 0), ring.idx(0, 1)
    for _, at, _ in items:
        for i, n in ((a, right), (z, left), (a, pair)):
            second.append(net.send(at(slot(i)), at(slot(i)), n))
    pass_on((a, b, z))
    yield
    for c in second:
        c.wait_recv()
    third = []
    az, bz, o, oz = ring.idx(-1, 1), ring.idx(1, 1), ring.idx(2, 0), ring.idx(2, 1)
    for _, at, parts in items:
        for i, n, part in ((az, right, parts[0]), (bz, left, parts[1]), (o, pair, parts[2])):
            if part is not None:
                r = view(at(slot(i)), part)
                third.append(net.send(r, r, n))
    pass_on((az, bz, o))
    yield
    for c in third:
        c.wait_recv()
    pass_on((oz,))
    for c in local:
        c.wait()
    for c in first + second + third:
        c.wait_send()
    if sibling is not None:
        yield
        for c in over:
            c.wait()


def reduce(net, ring, items, result):
    left, right, pair = ring_devices(ring)
    me, a, b, z = ring.idx(0, 0), ring.idx(-1, 0), ring.idx(1, 0), ring.idx(0, 1)
    az, bz, o, oz = ring.idx(-1, 1), ring.idx(1, 1), ring.idx(2, 0), ring.idx(2, 1)

    def plus(x, y):
        return (x.astype(F32) + y.astype(F32)).astype(BF)

    first, second, third = [], [], []
    for p, parts, land, _ in items:
        for n, part in zip((left, right, pair), parts):
            first.append(net.send(view(p(oz), part), view(land.at[0], part), n))
    yield
    for c in first:
        c.wait_recv()
    for p, parts, land, sums in items:
        for k, (i, part, n) in enumerate(
            ((o, parts[2], left), (bz, parts[1], right), (az, parts[0], pair))
        ):
            sums[k] = p(i)[...]
            sums[(k,) + part] = plus(p(i)[part], land[(0,) + part])
            second.append(net.send(sums.at[k], land.at[1 + k], n))
    yield
    for c in second:
        c.wait_recv()
    for p, parts, land, sums in items:
        third.append(net.send(p(b), land.at[5], right))
        sums[4] = plus(p(z)[...], land[2])
        third.append(net.send(sums.at[4], land.at[6], pair))
        sums[3] = (p(a)[...].astype(F32) + land[1].astype(F32) + land[3].astype(F32)).astype(BF)
        third.append(net.send(sums.at[3], land.at[4], left))
    yield
    for c in third:
        c.wait_recv()
    for k, (p, parts, land, sums) in enumerate(items):
        result(
            k,
            (p(me)[...].astype(F32) + land[4].astype(F32))
            + (land[5].astype(F32) + land[6].astype(F32)),
        )
    for c in first + second + third:
        c.wait_send()


def at(ref):
    return lambda i: ref.at[i]


CHUNKS = 2
CROWS = T // CHUNKS
CPARTS = ((slice(0, 32), ALL), (slice(32, 48), ALL), (slice(48, 64), ALL))


def rows(h):
    return pl.ds(CROWS * h, CROWS)


def chunk(ref, h):
    return lambda i: ref.at[i, rows(h)]


def chunk_scratch():
    return [pltpu.VMEM((7, CROWS, D), BF), pltpu.VMEM((5, CROWS, D), BF)] * CHUNKS


def reduce_scratch(shape):
    return [pltpu.VMEM((7,) + shape, BF), pltpu.VMEM((5,) + shape, BF)]


def reduce_shard(net, chips, core, sibling, items, result):
    over = []
    for p, _, half, _, _, _ in items:
        over.append(net.send(p.at[1 - core], half, sibling))
    yield
    for c in over:
        c.wait_recv()
    for p, _, half, both, _, _ in items:

        @pl.loop(0, 8)
        def _(j):
            both[j] = (p[core, j].astype(F32) + half[j].astype(F32)).astype(BF)

    yield from reduce(net, chips, [(at(i[3]), i[1], i[4], i[5]) for i in items], result)
    for c in over:
        c.wait_send()


def shard_scratch(shape):
    return [pltpu.VMEM((8,) + shape, BF), pltpu.VMEM((8,) + shape, BF)] + reduce_scratch(shape)


def rms_parts(v):
    inverse = lax.rsqrt(jnp.mean(v * v, -1, keepdims=True) + EPSILON)
    return v * inverse, inverse


def rms_back(g, n, inverse):
    return inverse * (g - n * jnp.mean(g * n, -1, keepdims=True))


def dot(a, b, dims, out=F32):
    return lax.dot_general(a, b, (dims, ((), ())), preferred_element_type=F32).astype(out)


NN = ((1,), (0,))
NT = ((1,), (1,))
TN = ((0,), (0,))


def remote_call(body, outs, ins, args, scratch, copies, locals_, number, vmem=None):
    sems = [
        pltpu.SemaphoreType.DMA((copies,)),
        pltpu.SemaphoreType.DMA((copies,)),
        pltpu.SemaphoreType.DMA((locals_,)),
    ]
    space = {"v": pl.BlockSpec(memory_space=pltpu.VMEM), "h": pl.BlockSpec(memory_space=pl.ANY)}
    return pl.pallas_call(
        body,
        out_shape=[jax.ShapeDtypeStruct(s, d) for s, d, _ in outs],
        in_specs=[space[k] for k in ins],
        out_specs=[space[k] for _, _, k in outs],
        scratch_shapes=list(scratch) + sems,
        compiler_params=pltpu.CompilerParams(
            collective_id=number, has_side_effects=True, vmem_limit_bytes=vmem
        ),
    )(*args)


WCOL1 = 640
WCOL2 = 768


def start_body(
    tok, cot, pos, w1, wo, w2, wd, freq,
    g_all, w1_all, wo_all, w2_all, wd_all, hid, raw, qkv, tab, lse, heads, part, gvec, ghead,
    x_all, p_all, ss, rs, ls,
):
    s, c, core, ctx, chips, sibling, goes, comes, stays = places()
    net = Net(ss, rs, ls)
    greet(ring_devices(ctx) + ring_devices(chips) + [sibling], (goes, comes, stays))

    def by_shard():
        moved = [(wo.at[c], wo_all.at[goes[0]]), (wd.at[c], wd_all.at[goes[0]])]
        yield from move(net, moved, goes, stays)
        yield from gather(
            net, chips, [(w1, at(w1_all), lanes(WCOL1)), (None, at(wo_all), lanes(D))],
            lambda i: i * 2 + core, sibling,
        )

    def first(h):
        items = [(tok.at[rows(h)], chunk(x_all, h), CPARTS)]
        if h == 0:
            items.append((pos, at(p_all), ((ALL, ALL), None, None)))
        yield from gather(net, ctx, items)

    drive(first(0), first(1), by_shard())

    def second(h):
        yield from gather(net, ctx, [(cot.at[rows(h)], chunk(g_all, h), CPARTS)])

    def by_shard_second():
        yield from gather(
            net, chips, [(w2, at(w2_all), lanes(WCOL2)), (None, at(wd_all), lanes(D))],
            lambda i: i * 2 + core, sibling,
        )

    def gains():
        lane = lax.broadcasted_iota(jnp.int32, (8, 128), 1)
        t = [w1_all[i, 0:16, 512:640].astype(F32)[0:8] for i in range(NS)]
        for j in range(8):
            x, y = t[2 * j], t[2 * j + 1]
            low = lane < 64
            gvec[0:1, 128 * j : 128 * (j + 1)] = jnp.where(low, x, pltpu.roll(y, 64, 1))[0:1]
            gvec[1:2, 128 * j : 128 * (j + 1)] = jnp.where(low, pltpu.roll(x, 64, 1), y)[0:1]
        q = jnp.zeros((8, 128), F32)
        k = jnp.zeros((8, 128), F32)
        for i in range(NS):
            here = lane // 8 == i
            q = jnp.where(here, pltpu.roll(t[i], 8 * i, 1), q)
            k = jnp.where(here, pltpu.roll(t[i], (8 * i + 120) % 128, 1), k)
        ghead[0:1] = q[1:2]
        ghead[1:2] = k[1:2]

    def project(i):
        normed, _ = rms_parts(x_all[i].astype(F32))
        h = (normed * gvec[0:1]).astype(BF)
        hid[i] = h
        r = dot(h, w1_all[:, :, 0:512].reshape(D, 512), NN)
        raw[i] = r
        angle = freq[...] * p_all[i].astype(F32)
        cosine = jnp.cos(angle).T
        sine = jnp.sin(angle).T
        sine = jnp.where(lax.broadcasted_iota(jnp.int32, (T, HD), 1) < HD // 2, -sine, sine)
        tab[i, :, 0:HD] = cosine
        tab[i, :, HD:] = sine
        for k in range(3):
            n, _ = rms_parts(r[:, HD * k : HD * (k + 1)])
            u = n * ghead[k // 2 : k // 2 + 1]
            qkv[i, :, HD * k : HD * (k + 1)] = (u * cosine + pltpu.roll(u, 64, 1) * sine).astype(BF)
        qkv[i, :, 3 * HD :] = r[:, 3 * HD :].astype(BF)

    def attend(h, n):
        width = 256 * (n + 1)
        q = qkv[2 * n : 2 * n + 2, :, HD * h : HD * (h + 1)].reshape(256, HD)
        k = qkv[0 : 2 * n + 2, :, 2 * HD : 3 * HD].reshape(width, HD)
        v = qkv[0 : 2 * n + 2, :, 3 * HD :].reshape(width, HD)
        score = dot(q, k, NT) * HD**-0.5
        row = lax.broadcasted_iota(jnp.int32, (256, width), 0) + 256 * n
        col = lax.broadcasted_iota(jnp.int32, (256, width), 1)
        score = jnp.where(col <= row, score, BLOCKED_SCORE)
        top = jnp.max(score, -1, keepdims=True)
        e = jnp.exp(score - top)
        total = jnp.sum(e, -1, keepdims=True)
        o = dot(e.astype(BF), v, NN) / total
        heads[2 * n : 2 * n + 2, :, HD * h : HD * (h + 1)] = o.reshape(2, T, HD)
        lse[h, 256 * n : 256 * (n + 1)] = top + jnp.log(total)

    def work():
        gains()
        pl.loop(0, 4)(project)
        yield
        pl.loop(4, 8)(project)
        for h in range(2):
            attend(h, 0)
        yield
        for n in range(1, 4):
            for h in range(2):
                attend(h, n)
            if n < 3:
                yield

        @pl.loop(0, NC)
        def _(i):
            part[i] = dot(heads[i].astype(BF), wo_all[...].reshape(QW, D), NN, BF)

    drive(second(0), second(1), by_shard_second(), work())


def mid_body(
    part, tok, cot, gain, wgu, wd, g_all,
    ga_all, gres_ref, ggain_ref, gw2_sum, gwd_sum, down_part, resid,
    h_all, mixed, ggu, back_part, ga, gw2, gwd, gwd_f,
    la0, sa0, la1, sa1, lb0, sb0, lb1, sb1,
    h1, b1, l1, t1, h2, b2, l2, t2, ss, rs, ls,
):
    s, c, core, ctx, chips, sibling, goes, comes, stays = places()
    net = Net(ss, rs, ls)
    greet(ring_devices(ctx) + ring_devices(chips) + [sibling])

    def forward(h, land, sums):
        def got(k, total):
            r = tok[rows(h)].astype(F32) + total
            resid[rows(h)] = r
            normed, _ = rms_parts(r)
            h_all[c, rows(h)] = (normed * gain[...]).astype(BF)

        yield from reduce(net, ctx, [(chunk(part, h), CPARTS, land, sums)], got)
        yield from gather(net, ctx, [(None, chunk(h_all, h), CPARTS)])

    def block(i):
        both = dot(h_all[i], wgu[...], NN)
        gate, up = both[:, :FW], both[:, FW:]
        sig = jax.nn.sigmoid(gate)
        act = gate * sig
        m = (act * up).astype(BF)
        mixed[i] = m
        gm = dot(g_all[i], wd[...], NT)
        gg = (gm * up * sig * (1.0 + gate * (1.0 - sig))).astype(BF)
        gu = (gm * act).astype(BF)
        ggu[i, :, 0:FW] = gg
        ggu[i, :, FW:] = gu
        back_part[i] = dot(jnp.concatenate([gg, gu], 1), wgu[...], NT, BF)
        down_part[i] = dot(m, wd[...], NN, BF)

    def blocks(places):
        n = len(places)

        @pl.loop(0, n)
        def _(j):
            i = places[0]
            for k in range(1, n):
                i = jnp.where(j == k, places[k], i)
            block(i)

    def work():
        yield
        yield
        yield
        blocks([c])
        yield
        blocks([ctx.idx(-1, 0), ctx.idx(1, 0), ctx.idx(0, 1)])
        yield
        blocks([ctx.idx(-1, 1), ctx.idx(1, 1), ctx.idx(2, 0)])
        yield
        blocks([ctx.idx(2, 1)])

    drive(forward(0, la0, sa0), forward(1, la1, sa1), work())

    def got_back(h):
        def got(k, total):
            normed, inverse = rms_parts(resid[rows(h)])
            g = jnp.sum(total * normed, 0, keepdims=True)
            if h == 0:
                ggain_ref[...] = g
            else:
                ggain_ref[...] += g
            gres = cot[rows(h)].astype(F32) + rms_back(total * gain[...], normed, inverse)
            gres_ref[rows(h)] = gres
            ga[rows(h)] = gres.astype(BF)

        return got

    def backward(h, land, sums):
        yield from reduce(net, ctx, [(chunk(back_part, h), CPARTS, land, sums)], got_back(h))
        yield from gather(net, ctx, [(ga.at[rows(h)], chunk(ga_all, h), CPARTS)])

    def got_shard(k, total):
        (gw2_sum, gwd_sum)[k][...] = total.astype(BF)

    def grads():
        for q in range(2):

            @pl.loop(4 * q, 4 * q + 4)
            def _(j):
                left = h_all[:, :, pl.ds(pl.multiple_of(j * 128, 128), 128)].reshape(SEQ, 128)
                g = dot(left, ggu[...].reshape(SEQ, 2 * FW), TN, BF)
                gw2[0, j] = g[0:64]
                gw2[1, j] = g[64:128]

            yield
        for j in range(3):
            left = mixed[:, :, 128 * j : 128 * (j + 1)].reshape(SEQ, 128)
            gwd_f[128 * j : 128 * (j + 1)] = dot(left, g_all[...].reshape(SEQ, D), TN)
        for i in range(NS):
            gwd[i % 2, i // 2] = gwd_f[24 * i : 24 * (i + 1)].astype(BF)
        yield
        yield from reduce_shard(
            net, chips, core, sibling,
            [(gw2, lanes(WCOL2), h1, b1, l1, t1), (gwd, lanes(D), h2, b2, l2, t2)], got_shard,
        )

    drive(
        backward(0, lb0, sb0), backward(1, lb1, sb1), grads(),
    )


def end_body(
    ga_all, tok, gres_ref, resid, gvec, ghead, ggain, wo_all, gw2_sum, gwd_sum,
    down_h, qkv_h, lse_h, heads_h, raw_h, tab_h, hid_h, w1_h,
    out_ref, gx_ref, small_ref, a1, ao, a2, ad,
    down_part, qkv, lse, heads, raw, tab, hid, w1_all,
    gatt, delta, gwo_f, gk_f, gv_f, gqkv, part, gw1, gwo,
    la0, sa0, la1, sa1, lb0, sb0, lb1, sb1, h1, b1, l1, t1, h2, b2, l2, t2,
    s1, so, own_d, sm, smc, sm2, sms, ss, rs, ls,
):
    s, c, core, ctx, chips, sibling, goes, comes, stays = places()
    net = Net(ss, rs, ls)
    loads = [
        net.copy(x, y)
        for x, y in (
            (heads_h, heads), (qkv_h, qkv), (lse_h, lse), (down_h, down_part),
            (raw_h, raw), (tab_h, tab), (hid_h, hid), (w1_h, w1_all),
        )
    ]
    ctx_peers = [(s, lax.rem(c + d, NC)) for d in range(1, NC)]
    shard_peers = [(lax.rem(s + d, NS), c) for d in range(1, NS)]
    greet(ctx_peers + shard_peers, (goes, comes, stays))

    def feed_forward(h, land, sums):
        def got(k, total):
            out_ref[rows(h)] = (resid[rows(h)] + total).astype(BF)

        if h == 0:
            loads[3].wait()
        yield from reduce(net, ctx, [(chunk(down_part, h), CPARTS, land, sums)], got)

    def feed_forward_grads():
        yield from move(net, [(gwd_sum, own_d)], comes, stays)
        yield from gather(net, ctx, [(gw2_sum, at(a2), lanes(WCOL2)), (own_d, at(ad), lanes(D))])

    def got_out(k, total):
        so[...] = total.astype(BF)

    def out_grad():
        for j in range(2):
            left = heads[:, :, HD * j : HD * (j + 1)].reshape(SEQ, HD).astype(BF)
            gwo_f[HD * j : HD * (j + 1)] = dot(left, ga_all[...].reshape(SEQ, D), TN)
        for i in range(NS):
            gwo[i % 2, i // 2] = gwo_f[16 * i : 16 * (i + 1)].astype(BF)
        yield from reduce_shard(
            net, chips, core, sibling, [(gwo, lanes(D), h2, b2, l2, t2)], got_out
        )
        yield from move(net, [(so, ao.at[comes[1]])], comes, stays)
        yield from gather(net, ctx, [(None, at(ao), lanes(D))])

    def head_grads(i):
        g = dot(ga_all[i], wo_all[...].reshape(QW, D), NT, BF)
        gatt[i] = g
        both = g.astype(F32) * heads[i]
        for h in range(2):
            delta[h, pl.ds(pl.multiple_of(i * T, T), T)] = jnp.sum(
                both[:, HD * h : HD * (h + 1)], -1, keepdims=True
            )

    def attend_back(h, n, fresh):
        width = 256 * (n + 1)
        here = slice(2 * n, 2 * n + 2)
        mine = slice(HD * h, HD * (h + 1))
        q = qkv[here, :, mine].reshape(256, HD)
        k = qkv[0 : 2 * n + 2, :, 2 * HD : 3 * HD].reshape(width, HD)
        v = qkv[0 : 2 * n + 2, :, 3 * HD :].reshape(width, HD)
        g = gatt[here, :, mine].reshape(256, HD)
        span = slice(256 * n, 256 * (n + 1))
        score = dot(q, k, NT) * HD**-0.5
        row = lax.broadcasted_iota(jnp.int32, (256, width), 0) + 256 * n
        col = lax.broadcasted_iota(jnp.int32, (256, width), 1)
        p = jnp.where(col <= row, jnp.exp(score - lse[h, span]), 0.0)
        gv = dot(p.astype(BF), g, TN)
        gs = (p * (dot(g, v, NT) - delta[h, span])).astype(BF)
        gk = dot(gs, q, TN)
        if fresh:
            gv_f[0:width] = gv
            gk_f[0:width] = gk
        else:
            gv_f[0:width] += gv
            gk_f[0:width] += gk
        gq = dot(gs, k, NN) * HD**-0.5
        turn_back(gq, here, mine, 0, fresh)

    def turn_back(g, here, mine, kind, fresh):
        n = g.shape[0]
        cosine = tab[here, :, 0:HD].reshape(n, HD)
        sine = tab[here, :, HD:].reshape(n, HD)
        w = g * cosine - pltpu.roll(g, 64, 1) * sine
        u, inverse = rms_parts(raw[here, :, mine].reshape(n, HD))
        gain = jnp.sum(w * u, 0, keepdims=True)
        place = slice(2 * D + HD * kind, 2 * D + HD * (kind + 1))
        if fresh:
            sm[:, place] = gain
        else:
            sm[:, place] += gain
        r = rms_back(w * ghead[kind : kind + 1], u, inverse).astype(BF)
        gqkv[here, :, mine] = r.reshape(n // T, T, HD)

    def work():
        yield
        pl.loop(0, NC)(head_grads)
        loads[1].wait()
        loads[2].wait()
        loads[4].wait()
        loads[5].wait()
        yield
        for n in (3, 2, 1, 0):
            for h in range(2):
                attend_back(h, n, n == 3 and h == 0)
            if n:
                yield
        for m in range(2):
            here = slice(4 * m, 4 * m + 4)
            span = slice(512 * m, 512 * (m + 1))
            turn_back(gk_f[span] * HD**-0.5, here, slice(2 * HD, 3 * HD), 1, m == 0)
            gqkv[here, :, 3 * HD :] = gv_f[span].astype(BF).reshape(4, T, HD)
        loads[6].wait()
        loads[7].wait()

        @pl.loop(0, NC)
        def _(i):
            part[i] = dot(gqkv[i], w1_all[:, :, 0:512].reshape(D, 512), NT, BF)

    loads[0].wait()
    background = out_grad()
    drive(feed_forward(0, lb0, sb0), feed_forward(1, lb1, sb1), background, feed_forward_grads(), work())

    def got_input(h):
        def got(k, total):
            normed, inverse = rms_parts(tok[rows(h)].astype(F32))
            g = jnp.sum(total * normed, 0, keepdims=True)
            if h == 0:
                sm[:, 0:D] = g
            else:
                sm[:, 0:D] += g
            gx_ref[rows(h)] = gres_ref[rows(h)] + rms_back(total * gvec[0:1], normed, inverse)

        return got

    def by_ctx(h, land, sums):
        yield from reduce(net, ctx, [(chunk(part, h), CPARTS, land, sums)], got_input(h))

    def small():
        yield
        yield
        yield
        yield
        sm[:, D : 2 * D] = ggain[...]
        smc[c] = sm[...]
        sent = [net.send(sm, smc.at[c], d) for d in ctx_peers]
        yield
        for x in sent:
            x.wait()
        total = smc[0]
        for i in range(1, NC):
            total = total + smc[i]
        sm2[...] = total
        sms[s] = total
        sent = [net.send(sm2, sms.at[s], d) for d in shard_peers]
        yield
        for x in sent:
            x.wait()
        total = sms[0]
        for i in range(1, NS):
            total = total + sms[i]
        small_ref[...] = total

    def got_shard(k, total):
        s1[...] = total.astype(BF)

    def grads():
        @pl.loop(0, 8)
        def _(j):
            left = hid[:, :, pl.ds(pl.multiple_of(j * 128, 128), 128)].reshape(SEQ, 128)
            g = dot(left, gqkv[...].reshape(SEQ, 512), TN, BF)
            gw1[0, j] = g[0:64]
            gw1[1, j] = g[64:128]

        yield from reduce_shard(
            net, chips, core, sibling, [(gw1, lanes(512), h1, b1, l1, t1)], got_shard
        )
        yield from gather(net, ctx, [(s1, at(a1), lanes(512))])

    drive(by_ctx(0, la0, sa0), by_ctx(1, la1, sa1), grads(), small())


def assemble_body(
    out, gx, a1, ao, a2, ad, out_ref, gx_ref, q_out, k_out, v_out, o_out, gate_out, up_out, down_out
):
    out_ref[...] = out[...]
    gx_ref[...] = gx[...]
    for i in range(NC):
        q_out[:, QW * i : QW * (i + 1)] = a1[i, :, 0:QW].astype(F32)
        k_out[:, HD * i : HD * (i + 1)] = a1[i, :, QW : QW + HD].astype(F32)
        v_out[:, HD * i : HD * (i + 1)] = a1[i, :, QW + HD :].astype(F32)
        o_out[16 * i : 16 * (i + 1), :] = ao[i].astype(F32)
        gate_out[:, FW * i : FW * (i + 1)] = a2[i, :, 0:FW].astype(F32)
        up_out[:, FW * i : FW * (i + 1)] = a2[i, :, FW : 2 * FW].astype(F32)
        down_out[24 * i : 24 * (i + 1), :] = ad[i].astype(F32)


def shards(
    tokens, positions, attn_gain, query_weight, key_matrix, value_matrix, query_gain, key_gain,
    out_weight, mlp_gain, gate_weight, up_weight, down_weight, cotangent,
):
    c = lax.axis_index("ctx")
    s = lax.axis_index("shard")
    tok, cot = tokens[0], cotangent[0]

    def cut(w, width):
        return lax.dynamic_slice(w, (0, c * width), (w.shape[0], width))

    row0 = jnp.concatenate([attn_gain, mlp_gain])[None]
    row1 = jnp.concatenate([query_gain, key_gain, jnp.zeros((112,), BF)])[None]
    gains = jnp.concatenate([row0, row1, jnp.zeros((62, 128), BF)], 0)
    w1 = jnp.concatenate(
        [cut(query_weight, QW), cut(key_matrix, HD), cut(value_matrix, HD), gains], 1
    )
    w2 = jnp.concatenate([cut(gate_weight, FW), cut(up_weight, FW)], 1)
    wo = out_weight.reshape(8, 16, D)
    wd = down_weight.reshape(8, 24, D)

    half = HD // 2
    freq = jnp.power(ROPE_BASE, -jnp.arange(half, dtype=F32) * (2.0 / HD))
    freq = jnp.broadcast_to(jnp.concatenate([freq, freq])[:, None], (HD, T))

    (
        g_all, w1_all, wo_all, w2_all, wd_all, hid, raw, qkv, tab, lse, heads, out_part, gvec, ghead,
    ) = remote_call(
        start_body,
        [
            ((NC, T, D), BF, "h"), ((NS, 64, WCOL1), BF, "v"), ((NS, 16, D), BF, "v"),
            ((NS, 64, WCOL2), BF, "h"), ((NS, 24, D), BF, "h"),
            ((NC, T, D), BF, "v"), ((NC, T, 512), F32, "v"), ((NC, T, 512), BF, "v"),
            ((NC, T, 2 * HD), F32, "v"), ((2, SEQ, 1), F32, "v"), ((NC, T, QW), F32, "v"),
            ((NC, T, D), BF, "v"), ((2, D), F32, "v"), ((2, HD), F32, "v"),
        ],
        "hhhhhhhv", (tok, cot, positions, w1, wo, w2, wd, freq),
        [pltpu.VMEM((NC, T, D), BF), pltpu.VMEM((NC, 1, T), jnp.int32)], 128, 8, 0, 56 << 20,
    )
    ga_all, grad_resid, ggain_mlp, gw2_sum, gwd_sum, down_part, resid = remote_call(
        mid_body,
        [
            ((NC, T, D), BF, "h"), ((T, D), F32, "v"), ((1, D), F32, "v"),
            ((64, WCOL2), BF, "v"), ((24, D), BF, "v"), ((NC, T, D), BF, "v"), ((T, D), F32, "v"),
        ],
        "v" * 7,
        (out_part, tok, cot, gvec[1:2], w2_all.reshape(D, 2 * FW), wd_all.reshape(FW, D), g_all),
        [
            pltpu.VMEM((NC, T, D), BF), pltpu.VMEM((NC, T, FW), BF), pltpu.VMEM((NC, T, 2 * FW), BF),
            pltpu.VMEM((NC, T, D), BF),
            pltpu.VMEM((T, D), BF), pltpu.VMEM((2, 8, 64, WCOL2), BF), pltpu.VMEM((2, 8, 24, D), BF),
            pltpu.VMEM((FW, D), F32),
        ]
        + chunk_scratch() * 2 + shard_scratch((64, WCOL2)) + shard_scratch((24, D)),
        128, 8, 1, 58 << 20,
    )
    output, gx, small, a1, ao, a2, ad = remote_call(
        end_body,
        [
            ((T, D), BF, "v"), ((T, D), F32, "v"), ((1, SMALL), F32, "v"),
            ((NC, 64, 512), BF, "v"), ((NC, 16, D), BF, "v"),
            ((NC, 64, WCOL2), BF, "v"), ((NC, 24, D), BF, "v"),
        ],
        "v" * 10 + "h" * 8,
        (
            ga_all, tok, grad_resid, resid, gvec, ghead, ggain_mlp, wo_all, gw2_sum, gwd_sum,
            down_part, qkv, lse, heads, raw, tab, hid, w1_all,
        ),
        [
            pltpu.VMEM((NC, T, D), BF), pltpu.VMEM((NC, T, 512), BF), pltpu.VMEM((2, SEQ, 1), F32),
            pltpu.VMEM((NC, T, QW), F32), pltpu.VMEM((NC, T, 512), F32),
            pltpu.VMEM((NC, T, 2 * HD), F32), pltpu.VMEM((NC, T, D), BF),
            pltpu.VMEM((NS, 64, WCOL1), BF),
            pltpu.VMEM((NC, T, QW), BF), pltpu.VMEM((2, SEQ, 1), F32), pltpu.VMEM((QW, D), F32),
            pltpu.VMEM((SEQ, HD), F32), pltpu.VMEM((SEQ, HD), F32), pltpu.VMEM((NC, T, 512), BF),
            pltpu.VMEM((NC, T, D), BF), pltpu.VMEM((2, 8, 64, 512), BF),
            pltpu.VMEM((2, 8, 16, D), BF),
        ]
        + chunk_scratch() * 2 + shard_scratch((64, 512)) + shard_scratch((16, D))
        + [
            pltpu.VMEM((64, 512), BF), pltpu.VMEM((16, D), BF), pltpu.VMEM((24, D), BF),
            pltpu.VMEM((1, SMALL), F32), pltpu.VMEM((NC, 1, SMALL), F32),
            pltpu.VMEM((1, SMALL), F32), pltpu.VMEM((NS, 1, SMALL), F32),
        ],
        160, 16, 2, 58 << 20,
    )
    output, gx, gwq, gwk, gwv, gwo_out, gwg, gwu, gwd_out = pl.pallas_call(
        assemble_body,
        out_shape=[
            jax.ShapeDtypeStruct((T, D), BF), jax.ShapeDtypeStruct((T, D), F32),
            jax.ShapeDtypeStruct((64, 2048), F32), jax.ShapeDtypeStruct((64, 1024), F32),
            jax.ShapeDtypeStruct((64, 1024), F32), jax.ShapeDtypeStruct((128, D), F32),
            jax.ShapeDtypeStruct((64, 3072), F32), jax.ShapeDtypeStruct((64, 3072), F32),
            jax.ShapeDtypeStruct((192, D), F32),
        ],
        compiler_params=pltpu.CompilerParams(vmem_limit_bytes=40 << 20),
    )(output, gx, a1, ao, a2, ad)
    small = small[0]

    def own(offset, width):
        return lax.dynamic_slice(small, (offset + s * width,), (width,))

    return (
        output[None], gx[None], own(0, 64), gwq, gwk, gwv, own(2 * D, 8), own(2 * D + HD, 8),
        gwo_out, own(D, 64), gwg, gwu, gwd_out,
    )


def solution(mesh):
    split = P("shard", "ctx", None)
    rows, vec = P("shard", None), P("shard")
    in_specs = (
        split, P("shard", "ctx"), vec, rows, rows, rows, vec, vec, rows, vec, rows, rows, rows, split,
    )
    out_specs = (split, split, vec, rows, rows, rows, vec, vec, rows, vec, rows, rows, rows)
    return jax.shard_map(shards, mesh=mesh, in_specs=in_specs, out_specs=out_specs, check_vma=False)
```

```python
import jax
import jax.numpy as jnp
import numpy as np
from jax import lax
from jax.experimental import pallas as pl
from jax.experimental.pallas import tpu as pltpu
from jax.sharding import PartitionSpec as P

MESH = pl.DeviceIdType.MESH
BF = jnp.bfloat16
F32 = jnp.float32

NS = 16
NC = 8
T = 128
SEQ = 1024
D = 1024
HD = 128
QW = 256
FW = 384
EPSILON = 1e-06
ROPE_BASE = 1000000.0
BLOCKED_SCORE = -1e30
SMALL = 2304

ALL = slice(None)


def lanes(width):
    a = (width // 128 + 1) // 2 * 128
    return ((ALL, slice(0, a)), (ALL, slice(a, width)), None)


def view(ref, part):
    return ref.at[tuple(pl.ds(p.start, p.stop - p.start) if p != ALL else p for p in part)]


class Ring:
    def __init__(self, me, device):
        self.a = me // 2
        self.b = lax.rem(me, 2)
        self.device = device

    def idx(self, da, db):
        return lax.rem(self.a + da + 4, 4) * 2 + lax.rem(self.b + db, 2)

    def dev(self, da, db):
        return self.device(self.idx(da, db))


class Net:
    def __init__(self, send, recv, local):
        self.s, self.r, self.l = send, recv, local
        self.n = 0
        self.m = 0

    def send(self, src, dst, to):
        k = self.n
        self.n += 1
        c = pltpu.make_async_remote_copy(
            src_ref=src, dst_ref=dst, send_sem=self.s.at[k], recv_sem=self.r.at[k],
            device_id=to, device_id_type=MESH,
        )
        c.start()
        return c

    def copy(self, src, dst):
        k = self.m
        self.m += 1
        c = pltpu.make_async_copy(src, dst, self.l.at[k])
        c.start()
        return c


def places():
    s = lax.axis_index("shard")
    c = lax.axis_index("ctx")
    core = lax.rem(s, 2)
    ctx = Ring(c, lambda i: (s, i))
    chips = Ring(s // 2, lambda i: (i * 2 + core, c))
    sibling = (s + 1 - 2 * core, c)
    half, rest = lax.rem(s, 2), s // 2
    goes = (8 * half + c, rest)
    comes = (2 * c + s // 8, lax.rem(s, 8))
    stays = jnp.logical_and(goes[0] == s, goes[1] == c)
    return s, c, core, ctx, chips, sibling, goes, comes, stays


def ring_devices(ring):
    return [ring.dev(-1, 0), ring.dev(1, 0), ring.dev(0, 1)]


def greet(devices, moved=None):
    barrier = pltpu.get_barrier_semaphore()
    for d in devices:
        pl.semaphore_signal(barrier, inc=1, device_id=d, device_id_type=MESH)
    if moved is not None:
        goes, comes, stays = moved

        @pl.when(jnp.logical_not(stays))
        def _():
            for d in (goes, comes):
                pl.semaphore_signal(barrier, inc=1, device_id=d, device_id_type=MESH)
            pl.semaphore_wait(barrier, len(devices) + 2)

        @pl.when(stays)
        def _():
            pl.semaphore_wait(barrier, len(devices))

    else:
        pl.semaphore_wait(barrier, len(devices))


def drive(*threads, until=None):
    threads = list(threads)
    ended = set()
    while threads:
        for x in list(threads):
            if id(x) in ended:
                continue
            try:
                next(x)
            except StopIteration:
                ended.add(id(x))
        threads = [x for x in threads if id(x) not in ended]
        if until is not None and id(until) in ended:
            break
    return threads


def move(net, items, to, stays):
    base = net.n
    net.n += len(items)

    def remote(k, src, dst):
        return pltpu.make_async_remote_copy(
            src_ref=src, dst_ref=dst, send_sem=net.s.at[base + k], recv_sem=net.r.at[base + k],
            device_id=to, device_id_type=MESH,
        )

    @pl.when(jnp.logical_not(stays))
    def _():
        for k, (src, dst) in enumerate(items):
            remote(k, src, dst).start()

    @pl.when(stays)
    def _():
        for k, (src, dst) in enumerate(items):
            pltpu.make_async_copy(src, dst, net.r.at[base + k]).start()

    yield

    @pl.when(jnp.logical_not(stays))
    def _():
        for k, (src, dst) in enumerate(items):
            remote(k, src, dst).wait()

    @pl.when(stays)
    def _():
        for k, (src, dst) in enumerate(items):
            pltpu.make_async_copy(src, dst, net.r.at[base + k]).wait()


def gather(net, ring, items, slot=lambda i: i, sibling=None):
    left, right, pair = ring_devices(ring)
    me = ring.idx(0, 0)
    over = []

    def pass_on(places):
        if sibling is not None:
            for _, at, _ in items:
                for i in places:
                    over.append(net.send(at(slot(i)), at(slot(i)), sibling))

    first, local = [], []
    for own, at, _ in items:
        here = at(slot(me))
        src = here if own is None else own
        for n in (left, right, pair):
            first.append(net.send(src, here, n))
        if sibling is not None:
            over.append(net.send(src, here, sibling))
        if own is not None:
            local.append(net.copy(own, here))
    yield
    for c in first:
        c.wait_recv()
    second = []
    a, b, z = ring.idx(-1, 0), ring.idx(1, 0), ring.idx(0, 1)
    for _, at, _ in items:
        for i, n in ((a, right), (z, left), (a, pair)):
            second.append(net.send(at(slot(i)), at(slot(i)), n))
    pass_on((a, b, z))
    yield
    for c in second:
        c.wait_recv()
    third = []
    az, bz, o, oz = ring.idx(-1, 1), ring.idx(1, 1), ring.idx(2, 0), ring.idx(2, 1)
    for _, at, parts in items:
        for i, n, part in ((az, right, parts[0]), (bz, left, parts[1]), (o, pair, parts[2])):
            if part is not None:
                r = view(at(slot(i)), part)
                third.append(net.send(r, r, n))
    pass_on((az, bz, o))
    yield
    for c in third:
        c.wait_recv()
    pass_on((oz,))
    for c in local:
        c.wait()
    for c in first + second + third:
        c.wait_send()
    if sibling is not None:
        yield
        for c in over:
            c.wait()


def reduce(net, ring, items, result):
    left, right, pair = ring_devices(ring)
    me, a, b, z = ring.idx(0, 0), ring.idx(-1, 0), ring.idx(1, 0), ring.idx(0, 1)
    az, bz, o, oz = ring.idx(-1, 1), ring.idx(1, 1), ring.idx(2, 0), ring.idx(2, 1)

    def plus(x, y):
        return (x.astype(F32) + y.astype(F32)).astype(BF)

    first, second, third = [], [], []
    for p, parts, land, _ in items:
        for n, part in zip((left, right, pair), parts):
            if part is None:
                continue
            first.append(net.send(view(p(oz), part), view(land.at[0], part), n))
    yield
    for c in first:
        c.wait_recv()
    for p, parts, land, sums in items:
        for k, (i, part, n) in enumerate(
            ((o, parts[2], left), (bz, parts[1], right), (az, parts[0], pair))
        ):
            if part is None:
                second.append(net.send(p(i), land.at[1 + k], n))
                continue
            sums[k] = p(i)[...]
            sums[(k,) + part] = plus(p(i)[part], land[(0,) + part])
            second.append(net.send(sums.at[k], land.at[1 + k], n))
    yield
    for c in second:
        c.wait_recv()
    for p, parts, land, sums in items:
        third.append(net.send(p(b), land.at[5], right))
        sums[4] = plus(p(z)[...], land[2])
        third.append(net.send(sums.at[4], land.at[6], pair))
        sums[3] = (p(a)[...].astype(F32) + land[1].astype(F32) + land[3].astype(F32)).astype(BF)
        third.append(net.send(sums.at[3], land.at[4], left))
    yield
    for c in third:
        c.wait_recv()
    for k, (p, parts, land, sums) in enumerate(items):
        result(
            k,
            (p(me)[...].astype(F32) + land[4].astype(F32))
            + (land[5].astype(F32) + land[6].astype(F32)),
        )
    for c in first + second + third:
        c.wait_send()


def at(ref):
    return lambda i: ref.at[i]


CHUNKS = 2
CROWS = T // CHUNKS
CPARTS = ((slice(0, 32), ALL), (slice(32, 64), ALL), None)


def rows(h):
    return pl.ds(CROWS * h, CROWS)


def chunk(ref, h):
    return lambda i: ref.at[i, rows(h)]


def chunk_scratch():
    return [pltpu.VMEM((7, CROWS, D), BF), pltpu.VMEM((5, CROWS, D), BF)] * CHUNKS


def reduce_scratch(shape):
    return [pltpu.VMEM((7,) + shape, BF), pltpu.VMEM((5,) + shape, BF)]


def reduce_shard(net, chips, core, sibling, items, result):
    over = []
    for p, _, half, _, _, _ in items:
        over.append(net.send(p.at[1 - core], half, sibling))
    yield
    for c in over:
        c.wait_recv()
    for p, _, half, both, _, _ in items:

        @pl.loop(0, 8)
        def _(j):
            both[j] = (p[core, j].astype(F32) + half[j].astype(F32)).astype(BF)

    yield from reduce(net, chips, [(at(i[3]), i[1], i[4], i[5]) for i in items], result)
    for c in over:
        c.wait_send()


def shard_scratch(shape):
    return [pltpu.VMEM((8,) + shape, BF), pltpu.VMEM((8,) + shape, BF)] + reduce_scratch(shape)


def rms_parts(v):
    inverse = lax.rsqrt(jnp.mean(v * v, -1, keepdims=True) + EPSILON)
    return v * inverse, inverse


def rms_back(g, n, inverse):
    return inverse * (g - n * jnp.mean(g * n, -1, keepdims=True))


def dot(a, b, dims, out=F32):
    return lax.dot_general(a, b, (dims, ((), ())), preferred_element_type=F32).astype(out)


NN = ((1,), (0,))
NT = ((1,), (1,))
TN = ((0,), (0,))


def remote_call(body, outs, ins, args, scratch, copies, locals_, number, vmem=None):
    sems = [
        pltpu.SemaphoreType.DMA((copies,)),
        pltpu.SemaphoreType.DMA((copies,)),
        pltpu.SemaphoreType.DMA((locals_,)),
    ]
    space = {"v": pl.BlockSpec(memory_space=pltpu.VMEM), "h": pl.BlockSpec(memory_space=pl.ANY)}
    return pl.pallas_call(
        body,
        out_shape=[jax.ShapeDtypeStruct(s, d) for s, d, _ in outs],
        in_specs=[space[k] for k in ins],
        out_specs=[space[k] for _, _, k in outs],
        scratch_shapes=list(scratch) + sems,
        compiler_params=pltpu.CompilerParams(
            collective_id=number, has_side_effects=True, vmem_limit_bytes=vmem
        ),
    )(*args)


WCOL1 = 640
WCOL2 = 768


def start_body(
    tok, cot, pos, wq, wk, wv, wg, wu, gblock, wo, wd, freq,
    g_all, w1_all, wo_all, w2_all, wd_all, hid_h, raw_h, qkv_h, tab_h, lse, heads_h, part, gvec, ghead,
    x_all, p_all, w1, w2, hid, raw, qkv, tab, heads, ss, rs, ls,
):
    s, c, core, ctx, chips, sibling, goes, comes, stays = places()
    net = Net(ss, rs, ls)

    def cut(w, width):
        return w.at[:, pl.ds(pl.multiple_of(c * width, 128), width)]

    loads = [
        net.copy(x, y)
        for x, y in (
            (cut(wq, QW), w1.at[:, 0:QW]), (cut(wk, HD), w1.at[:, QW : QW + HD]),
            (cut(wv, HD), w1.at[:, QW + HD : 512]), (gblock, w1.at[:, 512:WCOL1]),
            (cut(wg, FW), w2.at[:, 0:FW]), (cut(wu, FW), w2.at[:, FW : 2 * FW]),
        )
    ]
    greet(ring_devices(ctx) + ring_devices(chips) + [sibling], (goes, comes, stays))
    for x in loads:
        x.wait()

    def by_shard():
        yield from gather(
            net, chips, [(w1, at(w1_all), lanes(WCOL1))], lambda i: i * 2 + core, sibling
        )

    def moved():
        moved = [(wo.at[c], wo_all.at[goes[0]]), (wd.at[c], wd_all.at[goes[0]])]
        yield from move(net, moved, goes, stays)

    def first(h):
        items = [(tok.at[rows(h)], chunk(x_all, h), CPARTS)]
        if h == 0:
            items.append((pos, at(p_all), ((ALL, ALL), None, None)))
        yield from gather(net, ctx, items)

    weights = by_shard()
    drive(first(0), weights, first(1), weights, moved())

    def second(h):
        yield from gather(net, ctx, [(cot.at[rows(h)], chunk(g_all, h), CPARTS)])

    def by_shard_second():
        yield from gather(
            net, chips,
            [
                (w2, at(w2_all), lanes(WCOL2)), (None, at(wd_all), lanes(D)),
                (None, at(wo_all), lanes(D)),
            ],
            lambda i: i * 2 + core, sibling,
        )

    def gains():
        lane = lax.broadcasted_iota(jnp.int32, (8, 128), 1)
        t = [w1_all[i, 0:16, 512:640].astype(F32)[0:8] for i in range(NS)]
        for j in range(8):
            x, y = t[2 * j], t[2 * j + 1]
            low = lane < 64
            gvec[0:1, 128 * j : 128 * (j + 1)] = jnp.where(low, x, pltpu.roll(y, 64, 1))[0:1]
            gvec[1:2, 128 * j : 128 * (j + 1)] = jnp.where(low, pltpu.roll(x, 64, 1), y)[0:1]
        q = jnp.zeros((8, 128), F32)
        k = jnp.zeros((8, 128), F32)
        for i in range(NS):
            here = lane // 8 == i
            q = jnp.where(here, pltpu.roll(t[i], 8 * i, 1), q)
            k = jnp.where(here, pltpu.roll(t[i], (8 * i + 120) % 128, 1), k)
        ghead[0:1] = q[1:2]
        ghead[1:2] = k[1:2]

    def project(i):
        normed, _ = rms_parts(x_all[i].astype(F32))
        h = (normed * gvec[0:1]).astype(BF)
        hid[i] = h
        r = dot(h, w1_all[:, :, 0:512].reshape(D, 512), NN)
        raw[i] = r
        angle = freq[...] * p_all[i].astype(F32)
        cosine = jnp.cos(angle).T
        sine = jnp.sin(angle).T
        sine = jnp.where(lax.broadcasted_iota(jnp.int32, (T, HD), 1) < HD // 2, -sine, sine)
        tab[i, :, 0:HD] = cosine
        tab[i, :, HD:] = sine
        for k in range(3):
            n, _ = rms_parts(r[:, HD * k : HD * (k + 1)])
            u = n * ghead[k // 2 : k // 2 + 1]
            qkv[i, :, HD * k : HD * (k + 1)] = (u * cosine + pltpu.roll(u, 64, 1) * sine).astype(BF)
        qkv[i, :, 3 * HD :] = r[:, 3 * HD :].astype(BF)

    def attend(h, n):
        width = 256 * (n + 1)
        q = qkv[2 * n : 2 * n + 2, :, HD * h : HD * (h + 1)].reshape(256, HD)
        k = qkv[0 : 2 * n + 2, :, 2 * HD : 3 * HD].reshape(width, HD)
        v = qkv[0 : 2 * n + 2, :, 3 * HD :].reshape(width, HD)
        score = dot(q, k, NT) * HD**-0.5
        row = lax.broadcasted_iota(jnp.int32, (256, width), 0) + 256 * n
        col = lax.broadcasted_iota(jnp.int32, (256, width), 1)
        score = jnp.where(col <= row, score, BLOCKED_SCORE)
        top = jnp.max(score, -1, keepdims=True)
        e = jnp.exp(score - top)
        total = jnp.sum(e, -1, keepdims=True)
        o = dot(e.astype(BF), v, NN) / total
        heads[2 * n : 2 * n + 2, :, HD * h : HD * (h + 1)] = o.reshape(2, T, HD)
        lse[h, 256 * n : 256 * (n + 1)] = top + jnp.log(total)

    def work():
        gains()
        pl.loop(0, 4)(project)
        yield
        pl.loop(4, 8)(project)
        for x, y in ((hid, hid_h), (raw, raw_h), (qkv, qkv_h), (tab, tab_h)):
            stores.append(net.copy(x, y))
        for h in range(2):
            attend(h, 0)
        yield
        for n in range(1, 4):
            for h in range(2):
                attend(h, n)
            if n < 3:
                yield
        stores.append(net.copy(heads, heads_h))

        @pl.loop(0, NC)
        def _(i):
            part[i] = dot(heads[i].astype(BF), wo_all[...].reshape(QW, D), NN, BF)

    stores = []
    drive(second(0), second(1), by_shard_second(), work())
    for x in stores:
        x.wait()


def mid_body(
    part, tok, cot, gain, wgu_h, wd_h, g_h,
    ga_all, gres_ref, ggain_ref, gw2_h, gwd_h, down_h, resid,
    wgu, wd, g_all, down_part, gw2, gwd, h_all, mixed, ggu, back_part, ga, gwd_f,
    la0, sa0, la1, sa1, lb0, sb0, lb1, sb1, ss, rs, ls,
):
    s, c, core, ctx, chips, sibling, goes, comes, stays = places()
    net = Net(ss, rs, ls)
    loads = [net.copy(x, y) for x, y in ((wgu_h, wgu), (wd_h, wd), (g_h, g_all))]
    stores = []
    greet(ring_devices(ctx))

    def forward(h, land, sums):
        def got(k, total):
            r = tok[rows(h)].astype(F32) + total
            resid[rows(h)] = r
            normed, _ = rms_parts(r)
            h_all[c, rows(h)] = (normed * gain[...]).astype(BF)

        yield from reduce(net, ctx, [(chunk(part, h), CPARTS, land, sums)], got)
        yield from gather(net, ctx, [(None, chunk(h_all, h), CPARTS)])

    def block(i):
        both = dot(h_all[i], wgu[...], NN)
        gate, up = both[:, :FW], both[:, FW:]
        sig = jax.nn.sigmoid(gate)
        act = gate * sig
        m = (act * up).astype(BF)
        mixed[i] = m
        gm = dot(g_all[i], wd[...], NT)
        gg = (gm * up * sig * (1.0 + gate * (1.0 - sig))).astype(BF)
        gu = (gm * act).astype(BF)
        ggu[i, :, 0:FW] = gg
        ggu[i, :, FW:] = gu
        back_part[i] = dot(jnp.concatenate([gg, gu], 1), wgu[...], NT, BF)
        down_part[i] = dot(m, wd[...], NN, BF)

    def blocks(places):
        n = len(places)

        @pl.loop(0, n)
        def _(j):
            i = places[0]
            for k in range(1, n):
                i = jnp.where(j == k, places[k], i)
            block(i)

    def work():
        yield
        yield
        yield
        for x in loads:
            x.wait()
        blocks([c])
        yield
        blocks([ctx.idx(-1, 0), ctx.idx(1, 0), ctx.idx(0, 1)])
        yield
        blocks([ctx.idx(-1, 1), ctx.idx(1, 1), ctx.idx(2, 0)])
        yield
        blocks([ctx.idx(2, 1)])

    drive(forward(0, la0, sa0), forward(1, la1, sa1), work())
    stores.append(net.copy(down_part, down_h))

    def got_back(h):
        def got(k, total):
            normed, inverse = rms_parts(resid[rows(h)])
            g = jnp.sum(total * normed, 0, keepdims=True)
            if h == 0:
                ggain_ref[...] = g
            else:
                ggain_ref[...] += g
            gres = cot[rows(h)].astype(F32) + rms_back(total * gain[...], normed, inverse)
            gres_ref[rows(h)] = gres
            ga[rows(h)] = gres.astype(BF)

        return got

    def backward(h, land, sums):
        yield from reduce(net, ctx, [(chunk(back_part, h), CPARTS, land, sums)], got_back(h))
        yield from gather(net, ctx, [(ga.at[rows(h)], chunk(ga_all, h), CPARTS)])

    def grads():
        for q in range(2):

            @pl.loop(4 * q, 4 * q + 4)
            def _(j):
                left = h_all[:, :, pl.ds(pl.multiple_of(j * 128, 128), 128)].reshape(SEQ, 128)
                g = dot(left, ggu[...].reshape(SEQ, 2 * FW), TN, BF)
                gw2[0, j] = g[0:64]
                gw2[1, j] = g[64:128]

            yield
        for j in range(3):
            left = mixed[:, :, 128 * j : 128 * (j + 1)].reshape(SEQ, 128)
            gwd_f[128 * j : 128 * (j + 1)] = dot(left, g_all[...].reshape(SEQ, D), TN)
        for i in range(NS):
            gwd[i % 2, i // 2] = gwd_f[24 * i : 24 * (i + 1)].astype(BF)
        stores.append(net.copy(gw2, gw2_h))
        stores.append(net.copy(gwd, gwd_h))

    drive(backward(0, lb0, sb0), backward(1, lb1, sb1), grads())
    for x in stores:
        x.wait()


def end_body(
    ga_all, tok, gres_ref, resid, gvec, ghead, ggain, wo_all,
    gw2_h, gwd_h, down_h, qkv_h, lse_h, heads_h, raw_h, tab_h, hid_h, w1_h,
    out_ref, gx_ref, small_ref, a1, ao, a2, ad,
    down_part, qkv, lse, heads, raw, tab, hid, w1_all, gw2, gwd,
    gatt, delta, gwo_f, gk_f, gv_f, gqkv, part, gw1, gwo,
    la0, sa0, la1, sa1, lb0, sb0, lb1, sb1, h1, b1, l1, t1, h2, b2, l2, t2,
    h3, b3, l3, t3, h4, b4, l4, t4,
    s1, so, gw2_sum, gwd_sum, own_d, sm, smc, sm2, sms, ss, rs, ls,
):
    s, c, core, ctx, chips, sibling, goes, comes, stays = places()
    net = Net(ss, rs, ls)
    loads = [
        net.copy(x, y)
        for x, y in (
            (heads_h, heads), (qkv_h, qkv), (lse_h, lse), (down_h, down_part),
            (raw_h, raw), (tab_h, tab), (hid_h, hid), (w1_h, w1_all), (gw2_h, gw2), (gwd_h, gwd),
        )
    ]
    ctx_peers = [(s, lax.rem(c + d, NC)) for d in range(1, NC)]
    shard_peers = [(lax.rem(s + d, NS), c) for d in range(1, NS)]
    greet(ctx_peers + shard_peers, (goes, comes, stays))

    def feed_forward(h, land, sums):
        def got(k, total):
            out_ref[rows(h)] = (resid[rows(h)] + total).astype(BF)

        if h == 0:
            loads[3].wait()
        yield from reduce(net, ctx, [(chunk(down_part, h), CPARTS, land, sums)], got)

    def got_ff(k, total):
        (gw2_sum, gwd_sum)[k][...] = total.astype(BF)

    def feed_forward_grads():
        loads[8].wait()
        loads[9].wait()
        yield from reduce_shard(
            net, chips, core, sibling,
            [(gw2, lanes(WCOL2), h3, b3, l3, t3), (gwd, lanes(D), h4, b4, l4, t4)], got_ff,
        )
        yield from move(net, [(gwd_sum, own_d)], comes, stays)
        yield from gather(net, ctx, [(gw2_sum, at(a2), lanes(WCOL2)), (own_d, at(ad), lanes(D))])

    def got_out(k, total):
        so[...] = total.astype(BF)

    def out_grad():
        for j in range(2):
            left = heads[:, :, HD * j : HD * (j + 1)].reshape(SEQ, HD).astype(BF)
            gwo_f[HD * j : HD * (j + 1)] = dot(left, ga_all[...].reshape(SEQ, D), TN)
        for i in range(NS):
            gwo[i % 2, i // 2] = gwo_f[16 * i : 16 * (i + 1)].astype(BF)
        yield from reduce_shard(
            net, chips, core, sibling, [(gwo, lanes(D), h2, b2, l2, t2)], got_out
        )
        yield from move(net, [(so, ao.at[comes[1]])], comes, stays)
        yield from gather(net, ctx, [(None, at(ao), lanes(D))])

    def head_grads(i):
        g = dot(ga_all[i], wo_all[...].reshape(QW, D), NT, BF)
        gatt[i] = g
        both = g.astype(F32) * heads[i]
        for h in range(2):
            delta[h, pl.ds(pl.multiple_of(i * T, T), T)] = jnp.sum(
                both[:, HD * h : HD * (h + 1)], -1, keepdims=True
            )

    def attend_back(h, n, fresh):
        width = 256 * (n + 1)
        here = slice(2 * n, 2 * n + 2)
        mine = slice(HD * h, HD * (h + 1))
        q = qkv[here, :, mine].reshape(256, HD)
        k = qkv[0 : 2 * n + 2, :, 2 * HD : 3 * HD].reshape(width, HD)
        v = qkv[0 : 2 * n + 2, :, 3 * HD :].reshape(width, HD)
        g = gatt[here, :, mine].reshape(256, HD)
        span = slice(256 * n, 256 * (n + 1))
        score = dot(q, k, NT) * HD**-0.5
        row = lax.broadcasted_iota(jnp.int32, (256, width), 0) + 256 * n
        col = lax.broadcasted_iota(jnp.int32, (256, width), 1)
        p = jnp.where(col <= row, jnp.exp(score - lse[h, span]), 0.0)
        gv = dot(p.astype(BF), g, TN)
        gs = (p * (dot(g, v, NT) - delta[h, span])).astype(BF)
        gk = dot(gs, q, TN)
        if fresh:
            gv_f[0:width] = gv
            gk_f[0:width] = gk
        else:
            gv_f[0:width] += gv
            gk_f[0:width] += gk
        gq = dot(gs, k, NN) * HD**-0.5
        turn_back(gq, here, mine, 0, fresh)

    def turn_back(g, here, mine, kind, fresh):
        n = g.shape[0]
        cosine = tab[here, :, 0:HD].reshape(n, HD)
        sine = tab[here, :, HD:].reshape(n, HD)
        w = g * cosine - pltpu.roll(g, 64, 1) * sine
        u, inverse = rms_parts(raw[here, :, mine].reshape(n, HD))
        gain = jnp.sum(w * u, 0, keepdims=True)
        place = slice(2 * D + HD * kind, 2 * D + HD * (kind + 1))
        if fresh:
            sm[:, place] = gain
        else:
            sm[:, place] += gain
        r = rms_back(w * ghead[kind : kind + 1], u, inverse).astype(BF)
        gqkv[here, :, mine] = r.reshape(n // T, T, HD)

    def work():
        pl.loop(0, NC)(head_grads)
        loads[1].wait()
        loads[2].wait()
        loads[4].wait()
        loads[5].wait()
        yield
        for n in (3, 2, 1, 0):
            for h in range(2):
                attend_back(h, n, n == 3 and h == 0)
            if n:
                yield
        for m in range(2):
            here = slice(4 * m, 4 * m + 4)
            span = slice(512 * m, 512 * (m + 1))
            turn_back(gk_f[span] * HD**-0.5, here, slice(2 * HD, 3 * HD), 1, m == 0)
            gqkv[here, :, 3 * HD :] = gv_f[span].astype(BF).reshape(4, T, HD)
        loads[6].wait()
        loads[7].wait()

        @pl.loop(0, NC)
        def _(i):
            part[i] = dot(gqkv[i], w1_all[:, :, 0:512].reshape(D, 512), NT, BF)

    loads[0].wait()
    main = work()
    rest = drive(
        feed_forward(0, lb0, sb0), feed_forward(1, lb1, sb1), out_grad(), feed_forward_grads(), main,
        until=main,
    )

    def got_input(h):
        def got(k, total):
            normed, inverse = rms_parts(tok[rows(h)].astype(F32))
            g = jnp.sum(total * normed, 0, keepdims=True)
            if h == 0:
                sm[:, 0:D] = g
            else:
                sm[:, 0:D] += g
            gx_ref[rows(h)] = gres_ref[rows(h)] + rms_back(total * gvec[0:1], normed, inverse)

        return got

    def by_ctx(h, land, sums):
        yield from reduce(net, ctx, [(chunk(part, h), CPARTS, land, sums)], got_input(h))

    def small():
        yield
        yield
        yield
        yield
        sm[:, D : 2 * D] = ggain[...]
        smc[c] = sm[...]
        sent = [net.send(sm, smc.at[c], d) for d in ctx_peers]
        yield
        for x in sent:
            x.wait()
        total = smc[0]
        for i in range(1, NC):
            total = total + smc[i]
        sm2[...] = total
        sms[s] = total
        sent = [net.send(sm2, sms.at[s], d) for d in shard_peers]
        yield
        for x in sent:
            x.wait()
        total = sms[0]
        for i in range(1, NS):
            total = total + sms[i]
        small_ref[...] = total

    def got_shard(k, total):
        s1[...] = total.astype(BF)

    def grads():
        @pl.loop(0, 8)
        def _(j):
            left = hid[:, :, pl.ds(pl.multiple_of(j * 128, 128), 128)].reshape(SEQ, 128)
            g = dot(left, gqkv[...].reshape(SEQ, 512), TN, BF)
            gw1[0, j] = g[0:64]
            gw1[1, j] = g[64:128]

        yield from reduce_shard(
            net, chips, core, sibling, [(gw1, lanes(512), h1, b1, l1, t1)], got_shard
        )
        yield from gather(net, ctx, [(s1, at(a1), lanes(512))])

    last = grads()
    drive(by_ctx(0, la0, sa0), last, by_ctx(1, la1, sa1), last, *rest, small())


def assemble_body(
    out_h, gx_h, a1_h, ao_h, a2_h, ad_h,
    out_ref, gx_ref, q_out, k_out, v_out, o_out, gate_out, up_out, down_out,
    a1, ao, a2, ad, sem,
):
    pairs = ((a2_h, a2), (a1_h, a1), (ao_h, ao), (ad_h, ad), (out_h, out_ref), (gx_h, gx_ref))
    loads = [pltpu.make_async_copy(x, y, sem.at[k]) for k, (x, y) in enumerate(pairs)]
    for x in loads:
        x.start()
    loads[0].wait()
    for i in range(NC):
        gate_out[:, FW * i : FW * (i + 1)] = a2[i, :, 0:FW].astype(F32)
        up_out[:, FW * i : FW * (i + 1)] = a2[i, :, FW : 2 * FW].astype(F32)
    for x in loads[1:]:
        x.wait()
    for i in range(NC):
        q_out[:, QW * i : QW * (i + 1)] = a1[i, :, 0:QW].astype(F32)
        k_out[:, HD * i : HD * (i + 1)] = a1[i, :, QW : QW + HD].astype(F32)
        v_out[:, HD * i : HD * (i + 1)] = a1[i, :, QW + HD :].astype(F32)
        o_out[16 * i : 16 * (i + 1), :] = ao[i].astype(F32)
        down_out[24 * i : 24 * (i + 1), :] = ad[i].astype(F32)


def shards(
    tokens, positions, attn_gain, query_weight, key_matrix, value_matrix, query_gain, key_gain,
    out_weight, mlp_gain, gate_weight, up_weight, down_weight, cotangent,
):
    c = lax.axis_index("ctx")
    s = lax.axis_index("shard")
    tok, cot = tokens[0], cotangent[0]

    row0 = jnp.concatenate([attn_gain, mlp_gain])[None]
    row1 = jnp.concatenate([query_gain, key_gain, jnp.zeros((112,), BF)])[None]
    gains = jnp.concatenate([row0, row1, jnp.zeros((62, 128), BF)], 0)
    wo = out_weight.reshape(8, 16, D)
    wd = down_weight.reshape(8, 24, D)

    freq = np.power(ROPE_BASE, -np.arange(HD // 2) * (2.0 / HD)).astype(np.float32)
    freq = np.concatenate([freq, freq])[:, None]

    (
        g_all, w1_all, wo_all, w2_all, wd_all, hid, raw, qkv, tab, lse, heads, out_part, gvec, ghead,
    ) = remote_call(
        start_body,
        [
            ((NC, T, D), BF, "h"), ((NS, 64, WCOL1), BF, "v"), ((NS, 16, D), BF, "v"),
            ((NS, 64, WCOL2), BF, "h"), ((NS, 24, D), BF, "h"),
            ((NC, T, D), BF, "h"), ((NC, T, 512), F32, "h"), ((NC, T, 512), BF, "h"),
            ((NC, T, 2 * HD), F32, "h"), ((2, SEQ, 1), F32, "v"), ((NC, T, QW), F32, "h"),
            ((NC, T, D), BF, "v"), ((2, D), F32, "v"), ((2, HD), F32, "v"),
        ],
        "h" * 11 + "v",
        (
            tok, cot, positions, query_weight, key_matrix, value_matrix, gate_weight, up_weight,
            gains, wo, wd, freq,
        ),
        [
            pltpu.VMEM((NC, T, D), BF), pltpu.VMEM((NC, 1, T), jnp.int32),
            pltpu.VMEM((64, WCOL1), BF), pltpu.VMEM((64, WCOL2), BF),
            pltpu.VMEM((NC, T, D), BF), pltpu.VMEM((NC, T, 512), F32),
            pltpu.VMEM((NC, T, 512), BF), pltpu.VMEM((NC, T, 2 * HD), F32),
            pltpu.VMEM((NC, T, QW), F32),
        ],
        144, 24, 0, 58 << 20,
    )
    ga_all, grad_resid, ggain_mlp, gw2, gwd, down_part, resid = remote_call(
        mid_body,
        [
            ((NC, T, D), BF, "h"), ((T, D), F32, "v"), ((1, D), F32, "v"),
            ((2, 8, 64, WCOL2), BF, "h"), ((2, 8, 24, D), BF, "h"),
            ((NC, T, D), BF, "h"), ((T, D), F32, "v"),
        ],
        "vvvvhhh",
        (out_part, tok, cot, gvec[1:2], w2_all.reshape(D, 2 * FW), wd_all.reshape(FW, D), g_all),
        [
            pltpu.VMEM((D, 2 * FW), BF), pltpu.VMEM((FW, D), BF), pltpu.VMEM((NC, T, D), BF),
            pltpu.VMEM((NC, T, D), BF), pltpu.VMEM((2, 8, 64, WCOL2), BF),
            pltpu.VMEM((2, 8, 24, D), BF),
            pltpu.VMEM((NC, T, D), BF), pltpu.VMEM((NC, T, FW), BF), pltpu.VMEM((NC, T, 2 * FW), BF),
            pltpu.VMEM((NC, T, D), BF), pltpu.VMEM((T, D), BF), pltpu.VMEM((FW, D), F32),
        ]
        + chunk_scratch() * 2,
        96, 16, 1, 58 << 20,
    )
    output, gx, small, a1, ao, a2, ad = remote_call(
        end_body,
        [
            ((T, D), BF, "v"), ((T, D), F32, "v"), ((1, SMALL), F32, "v"),
            ((NC, 64, 512), BF, "v"), ((NC, 16, D), BF, "v"),
            ((NC, 64, WCOL2), BF, "v"), ((NC, 24, D), BF, "v"),
        ],
        "v" * 8 + "h" * 10,
        (
            ga_all, tok, grad_resid, resid, gvec, ghead, ggain_mlp, wo_all, gw2, gwd,
            down_part, qkv, lse, heads, raw, tab, hid, w1_all,
        ),
        [
            pltpu.VMEM((NC, T, D), BF), pltpu.VMEM((NC, T, 512), BF), pltpu.VMEM((2, SEQ, 1), F32),
            pltpu.VMEM((NC, T, QW), F32), pltpu.VMEM((NC, T, 512), F32),
            pltpu.VMEM((NC, T, 2 * HD), F32), pltpu.VMEM((NC, T, D), BF),
            pltpu.VMEM((NS, 64, WCOL1), BF),
            pltpu.VMEM((2, 8, 64, WCOL2), BF), pltpu.VMEM((2, 8, 24, D), BF),
            pltpu.VMEM((NC, T, QW), BF), pltpu.VMEM((2, SEQ, 1), F32), pltpu.VMEM((QW, D), F32),
            pltpu.VMEM((SEQ, HD), F32), pltpu.VMEM((SEQ, HD), F32), pltpu.VMEM((NC, T, 512), BF),
            pltpu.VMEM((NC, T, D), BF), pltpu.VMEM((2, 8, 64, 512), BF),
            pltpu.VMEM((2, 8, 16, D), BF),
        ]
        + chunk_scratch() * 2 + shard_scratch((64, 512)) + shard_scratch((16, D))
        + shard_scratch((64, WCOL2)) + shard_scratch((24, D))
        + [
            pltpu.VMEM((64, 512), BF), pltpu.VMEM((16, D), BF),
            pltpu.VMEM((64, WCOL2), BF), pltpu.VMEM((24, D), BF), pltpu.VMEM((24, D), BF),
            pltpu.VMEM((1, SMALL), F32), pltpu.VMEM((NC, 1, SMALL), F32),
            pltpu.VMEM((1, SMALL), F32), pltpu.VMEM((NS, 1, SMALL), F32),
        ],
        176, 24, 2, 58 << 20,
    )
    any_, whole = pl.BlockSpec(memory_space=pl.ANY), pl.BlockSpec(memory_space=pltpu.VMEM)
    output, gx, gwq, gwk, gwv, gwo_out, gwg, gwu, gwd_out = pl.pallas_call(
        assemble_body,
        out_shape=[
            jax.ShapeDtypeStruct((T, D), BF), jax.ShapeDtypeStruct((T, D), F32),
            jax.ShapeDtypeStruct((64, 2048), F32), jax.ShapeDtypeStruct((64, 1024), F32),
            jax.ShapeDtypeStruct((64, 1024), F32), jax.ShapeDtypeStruct((128, D), F32),
            jax.ShapeDtypeStruct((64, 3072), F32), jax.ShapeDtypeStruct((64, 3072), F32),
            jax.ShapeDtypeStruct((192, D), F32),
        ],
        in_specs=[any_] * 6,
        out_specs=[whole] * 9,
        scratch_shapes=[
            pltpu.VMEM((NC, 64, 512), BF), pltpu.VMEM((NC, 16, D), BF),
            pltpu.VMEM((NC, 64, WCOL2), BF), pltpu.VMEM((NC, 24, D), BF),
            pltpu.SemaphoreType.DMA((6,)),
        ],
        compiler_params=pltpu.CompilerParams(vmem_limit_bytes=58 << 20),
    )(output, gx, a1, ao, a2, ad)
    small = small[0]

    def own(offset, width):
        return lax.dynamic_slice(small, (offset + s * width,), (width,))

    return (
        output[None], gx[None], own(0, 64), gwq, gwk, gwv, own(2 * D, 8), own(2 * D + HD, 8),
        gwo_out, own(D, 64), gwg, gwu, gwd_out,
    )


def solution(mesh):
    split = P("shard", "ctx", None)
    rows, vec = P("shard", None), P("shard")
    in_specs = (
        split, P("shard", "ctx"), vec, rows, rows, rows, vec, vec, rows, vec, rows, rows, rows, split,
    )
    out_specs = (split, split, vec, rows, rows, rows, vec, vec, rows, vec, rows, rows, rows)
    return jax.shard_map(shards, mesh=mesh, in_specs=in_specs, out_specs=out_specs, check_vma=False)
```

```python
import jax
import jax.numpy as jnp
import numpy as np
from jax import lax
from jax.experimental import pallas as pl
from jax.experimental.pallas import tpu as pltpu
from jax.sharding import PartitionSpec as P

MESH = pl.DeviceIdType.MESH
BF = jnp.bfloat16
F32 = jnp.float32

NS = 16
NC = 8
T = 128
SEQ = 1024
D = 1024
HD = 128
QW = 256
FW = 384
EPSILON = 1e-06
ROPE_BASE = 1000000.0
BLOCKED_SCORE = -1e30
SMALL = 2304

ALL = slice(None)


def lanes(width):
    a = (width // 128 + 1) // 2 * 128
    return ((ALL, slice(0, a)), (ALL, slice(a, width)), None)


def view(ref, part):
    return ref.at[tuple(pl.ds(p.start, p.stop - p.start) if p != ALL else p for p in part)]


class Ring:
    def __init__(self, me, device):
        self.a = me // 2
        self.b = lax.rem(me, 2)
        self.device = device

    def idx(self, da, db):
        return lax.rem(self.a + da + 4, 4) * 2 + lax.rem(self.b + db, 2)

    def dev(self, da, db):
        return self.device(self.idx(da, db))


class Net:
    def __init__(self, send, recv, local):
        self.s, self.r, self.l = send, recv, local
        self.n = 0
        self.m = 0

    def send(self, src, dst, to):
        k = self.n
        self.n += 1
        c = pltpu.make_async_remote_copy(
            src_ref=src, dst_ref=dst, send_sem=self.s.at[k], recv_sem=self.r.at[k],
            device_id=to, device_id_type=MESH,
        )
        c.start()
        return c

    def copy(self, src, dst):
        k = self.m
        self.m += 1
        c = pltpu.make_async_copy(src, dst, self.l.at[k])
        c.start()
        return c


def places():
    s = lax.axis_index("shard")
    c = lax.axis_index("ctx")
    core = lax.rem(s, 2)
    ctx = Ring(c, lambda i: (s, i))
    chips = Ring(s // 2, lambda i: (i * 2 + core, c))
    sibling = (s + 1 - 2 * core, c)
    half, rest = lax.rem(s, 2), s // 2
    goes = (8 * half + c, rest)
    comes = (2 * c + s // 8, lax.rem(s, 8))
    stays = jnp.logical_and(goes[0] == s, goes[1] == c)
    return s, c, core, ctx, chips, sibling, goes, comes, stays


def ring_devices(ring):
    return [ring.dev(-1, 0), ring.dev(1, 0), ring.dev(0, 1)]


def greet(devices, moved=None):
    barrier = pltpu.get_barrier_semaphore()
    for d in devices:
        pl.semaphore_signal(barrier, inc=1, device_id=d, device_id_type=MESH)
    if moved is not None:
        goes, comes, stays = moved

        @pl.when(jnp.logical_not(stays))
        def _():
            for d in (goes, comes):
                pl.semaphore_signal(barrier, inc=1, device_id=d, device_id_type=MESH)
            pl.semaphore_wait(barrier, len(devices) + 2)

        @pl.when(stays)
        def _():
            pl.semaphore_wait(barrier, len(devices))

    else:
        pl.semaphore_wait(barrier, len(devices))


def drive(*threads, until=None):
    threads = list(threads)
    ended = set()
    while threads:
        for x in list(threads):
            if id(x) in ended:
                continue
            try:
                next(x)
            except StopIteration:
                ended.add(id(x))
        threads = [x for x in threads if id(x) not in ended]
        if until is not None and id(until) in ended:
            break
    return threads


def move(net, items, to, stays):
    base = net.n
    net.n += len(items)

    def remote(k, src, dst):
        return pltpu.make_async_remote_copy(
            src_ref=src, dst_ref=dst, send_sem=net.s.at[base + k], recv_sem=net.r.at[base + k],
            device_id=to, device_id_type=MESH,
        )

    @pl.when(jnp.logical_not(stays))
    def _():
        for k, (src, dst) in enumerate(items):
            remote(k, src, dst).start()

    @pl.when(stays)
    def _():
        for k, (src, dst) in enumerate(items):
            pltpu.make_async_copy(src, dst, net.r.at[base + k]).start()

    yield

    @pl.when(jnp.logical_not(stays))
    def _():
        for k, (src, dst) in enumerate(items):
            remote(k, src, dst).wait()

    @pl.when(stays)
    def _():
        for k, (src, dst) in enumerate(items):
            pltpu.make_async_copy(src, dst, net.r.at[base + k]).wait()


def gather(net, ring, items, slot=lambda i: i, sibling=None):
    left, right, pair = ring_devices(ring)
    me = ring.idx(0, 0)
    over = []

    def pass_on(places):
        if sibling is not None:
            for _, at, _ in items:
                for i in places:
                    over.append(net.send(at(slot(i)), at(slot(i)), sibling))

    first, local = [], []
    for own, at, _ in items:
        here = at(slot(me))
        src = here if own is None else own
        for n in (left, right, pair):
            first.append(net.send(src, here, n))
        if sibling is not None:
            over.append(net.send(src, here, sibling))
        if own is not None:
            local.append(net.copy(own, here))
    yield
    for c in first:
        c.wait_recv()
    second = []
    a, b, z = ring.idx(-1, 0), ring.idx(1, 0), ring.idx(0, 1)
    for _, at, _ in items:
        for i, n in ((a, right), (z, left), (a, pair)):
            second.append(net.send(at(slot(i)), at(slot(i)), n))
    pass_on((a, b, z))
    yield
    for c in second:
        c.wait_recv()
    third = []
    az, bz, o, oz = ring.idx(-1, 1), ring.idx(1, 1), ring.idx(2, 0), ring.idx(2, 1)
    for _, at, parts in items:
        for i, n, part in ((az, right, parts[0]), (bz, left, parts[1]), (o, pair, parts[2])):
            if part is not None:
                r = view(at(slot(i)), part)
                third.append(net.send(r, r, n))
    pass_on((az, bz, o))
    yield
    for c in third:
        c.wait_recv()
    pass_on((oz,))
    for c in local:
        c.wait()
    for c in first + second + third:
        c.wait_send()
    if sibling is not None:
        yield
        for c in over:
            c.wait()


def reduce(net, ring, items, result):
    left, right, pair = ring_devices(ring)
    me, a, b, z = ring.idx(0, 0), ring.idx(-1, 0), ring.idx(1, 0), ring.idx(0, 1)
    az, bz, o, oz = ring.idx(-1, 1), ring.idx(1, 1), ring.idx(2, 0), ring.idx(2, 1)

    def plus(x, y):
        return (x.astype(F32) + y.astype(F32)).astype(BF)

    first, second, third = [], [], []
    for p, parts, land, _ in items:
        for n, part in zip((left, right, pair), parts):
            if part is None:
                continue
            first.append(net.send(view(p(oz), part), view(land.at[0], part), n))
    yield
    for c in first:
        c.wait_recv()
    for p, parts, land, sums in items:
        for k, (i, part, n) in enumerate(
            ((o, parts[2], left), (bz, parts[1], right), (az, parts[0], pair))
        ):
            if part is None:
                second.append(net.send(p(i), land.at[1 + k], n))
                continue
            sums[k] = p(i)[...]
            sums[(k,) + part] = plus(p(i)[part], land[(0,) + part])
            second.append(net.send(sums.at[k], land.at[1 + k], n))
    yield
    for c in second:
        c.wait_recv()
    for p, parts, land, sums in items:
        third.append(net.send(p(b), land.at[5], right))
        sums[4] = plus(p(z)[...], land[2])
        third.append(net.send(sums.at[4], land.at[6], pair))
        sums[3] = (p(a)[...].astype(F32) + land[1].astype(F32) + land[3].astype(F32)).astype(BF)
        third.append(net.send(sums.at[3], land.at[4], left))
    yield
    for c in third:
        c.wait_recv()
    for k, (p, parts, land, sums) in enumerate(items):
        result(
            k,
            (p(me)[...].astype(F32) + land[4].astype(F32))
            + (land[5].astype(F32) + land[6].astype(F32)),
        )
    for c in first + second + third:
        c.wait_send()


def at(ref):
    return lambda i: ref.at[i]


CHUNKS = 2
CROWS = T // CHUNKS
CPARTS = ((slice(0, 32), ALL), (slice(32, 64), ALL), None)


def rows(h):
    return pl.ds(CROWS * h, CROWS)


def chunk(ref, h):
    return lambda i: ref.at[i, rows(h)]


def chunk_scratch():
    return [pltpu.VMEM((7, CROWS, D), BF), pltpu.VMEM((5, CROWS, D), BF)] * CHUNKS


def reduce_scratch(shape):
    return [pltpu.VMEM((7,) + shape, BF), pltpu.VMEM((5,) + shape, BF)]


def reduce_shard(net, chips, core, sibling, items, result):
    over = []
    for p, _, half, _, _, _ in items:
        over.append(net.send(p.at[1 - core], half, sibling))
    yield
    for c in over:
        c.wait_recv()
    for p, _, half, both, _, _ in items:

        @pl.loop(0, 8)
        def _(j):
            both[j] = (p[core, j].astype(F32) + half[j].astype(F32)).astype(BF)

    yield from reduce(net, chips, [(at(i[3]), i[1], i[4], i[5]) for i in items], result)
    for c in over:
        c.wait_send()


def shard_scratch(shape):
    return [pltpu.VMEM((8,) + shape, BF), pltpu.VMEM((8,) + shape, BF)] + reduce_scratch(shape)


def rms_parts(v):
    inverse = lax.rsqrt(jnp.mean(v * v, -1, keepdims=True) + EPSILON)
    return v * inverse, inverse


def rms_back(g, n, inverse):
    return inverse * (g - n * jnp.mean(g * n, -1, keepdims=True))


def dot(a, b, dims, out=F32):
    return lax.dot_general(a, b, (dims, ((), ())), preferred_element_type=F32).astype(out)


NN = ((1,), (0,))
NT = ((1,), (1,))
TN = ((0,), (0,))


def remote_call(body, outs, ins, args, scratch, copies, locals_, number, vmem=None):
    sems = [
        pltpu.SemaphoreType.DMA((copies,)),
        pltpu.SemaphoreType.DMA((copies,)),
        pltpu.SemaphoreType.DMA((locals_,)),
    ]
    space = {"v": pl.BlockSpec(memory_space=pltpu.VMEM), "h": pl.BlockSpec(memory_space=pl.ANY)}
    return pl.pallas_call(
        body,
        out_shape=[jax.ShapeDtypeStruct(s, d) for s, d, _ in outs],
        in_specs=[space[k] for k in ins],
        out_specs=[space[k] for _, _, k in outs],
        scratch_shapes=list(scratch) + sems,
        compiler_params=pltpu.CompilerParams(
            collective_id=number, has_side_effects=True, vmem_limit_bytes=vmem
        ),
    )(*args)


WCOL1 = 640
WCOL2 = 768


def start_body(
    tok, cot, pos, wq, wk, wv, wg, wu, gblock, wo, wd, freq,
    g_all, w1_all, wo_all, w2_all, wd_all, hid_h, raw_h, qkv_h, tab_h, probs_h, heads_h, part, gvec, ghead,
    x_all, p_all, w1, w2, hid, raw, qkv, tab, probs, heads, ss, rs, ls,
):
    s, c, core, ctx, chips, sibling, goes, comes, stays = places()
    net = Net(ss, rs, ls)

    def cut(w, width):
        return w.at[:, pl.ds(pl.multiple_of(c * width, 128), width)]

    loads = [
        net.copy(x, y)
        for x, y in (
            (cut(wq, QW), w1.at[:, 0:QW]), (cut(wk, HD), w1.at[:, QW : QW + HD]),
            (cut(wv, HD), w1.at[:, QW + HD : 512]), (gblock, w1.at[:, 512:WCOL1]),
            (cut(wg, FW), w2.at[:, 0:FW]), (cut(wu, FW), w2.at[:, FW : 2 * FW]),
        )
    ]
    greet(ring_devices(ctx) + ring_devices(chips) + [sibling], (goes, comes, stays))
    for x in loads:
        x.wait()

    def weights():
        yield from gather(
            net, chips, [(w1, at(w1_all), lanes(WCOL1))], lambda i: i * 2 + core, sibling
        )
        yield from gather(
            net, chips,
            [
                (w2, at(w2_all), lanes(WCOL2)), (None, at(wd_all), lanes(D)),
                (None, at(wo_all), lanes(D)),
            ],
            lambda i: i * 2 + core, sibling,
        )

    def moved():
        moved = [(wo.at[c], wo_all.at[goes[0]]), (wd.at[c], wd_all.at[goes[0]])]
        yield from move(net, moved, goes, stays)

    def by_ctx(h):
        items = [(tok.at[rows(h)], chunk(x_all, h), CPARTS)]
        if h == 0:
            items.append((pos, at(p_all), ((ALL, ALL), None, None)))
        yield from gather(net, ctx, items)
        yield from gather(net, ctx, [(cot.at[rows(h)], chunk(g_all, h), CPARTS)])

    def gains():
        lane = lax.broadcasted_iota(jnp.int32, (8, 128), 1)
        t = [w1_all[i, 0:16, 512:640].astype(F32)[0:8] for i in range(NS)]
        for j in range(8):
            x, y = t[2 * j], t[2 * j + 1]
            low = lane < 64
            gvec[0:1, 128 * j : 128 * (j + 1)] = jnp.where(low, x, pltpu.roll(y, 64, 1))[0:1]
            gvec[1:2, 128 * j : 128 * (j + 1)] = jnp.where(low, pltpu.roll(x, 64, 1), y)[0:1]
        q = jnp.zeros((8, 128), F32)
        k = jnp.zeros((8, 128), F32)
        for i in range(NS):
            here = lane // 8 == i
            q = jnp.where(here, pltpu.roll(t[i], 8 * i, 1), q)
            k = jnp.where(here, pltpu.roll(t[i], (8 * i + 120) % 128, 1), k)
        ghead[0:1] = q[1:2]
        ghead[1:2] = k[1:2]

    def project(i):
        normed, _ = rms_parts(x_all[i].astype(F32))
        h = (normed * gvec[0:1]).astype(BF)
        hid[i] = h
        r = dot(h, w1_all[:, :, 0:512].reshape(D, 512), NN)
        raw[i] = r
        angle = freq[...] * p_all[i].astype(F32)
        cosine = jnp.cos(angle).T
        sine = jnp.sin(angle).T
        sine = jnp.where(lax.broadcasted_iota(jnp.int32, (T, HD), 1) < HD // 2, -sine, sine)
        tab[i, :, 0:HD] = cosine
        tab[i, :, HD:] = sine
        for k in range(3):
            n, _ = rms_parts(r[:, HD * k : HD * (k + 1)])
            u = n * ghead[k // 2 : k // 2 + 1]
            qkv[i, :, HD * k : HD * (k + 1)] = (u * cosine + pltpu.roll(u, 64, 1) * sine).astype(BF)
        qkv[i, :, 3 * HD :] = r[:, 3 * HD :].astype(BF)

    def attend(h, n):
        width = 256 * (n + 1)
        q = qkv[2 * n : 2 * n + 2, :, HD * h : HD * (h + 1)].reshape(256, HD)
        k = qkv[0 : 2 * n + 2, :, 2 * HD : 3 * HD].reshape(width, HD)
        v = qkv[0 : 2 * n + 2, :, 3 * HD :].reshape(width, HD)
        score = dot(q, k, NT) * HD**-0.5
        row = lax.broadcasted_iota(jnp.int32, (256, width), 0) + 256 * n
        col = lax.broadcasted_iota(jnp.int32, (256, width), 1)
        score = jnp.where(col <= row, score, BLOCKED_SCORE)
        top = jnp.max(score, -1, keepdims=True)
        e = jnp.exp(score - top)
        total = jnp.sum(e, -1, keepdims=True)
        share = 1.0 / total
        o = dot(e.astype(BF), v, NN) * share
        e = e * share
        for m in range(n + 1):
            probs[h, n * (n + 1) // 2 + m] = e[:, 256 * m : 256 * (m + 1)].astype(BF)
        heads[2 * n : 2 * n + 2, :, HD * h : HD * (h + 1)] = o.reshape(2, T, HD)

    def work():
        yield
        yield
        yield
        gains()
        pl.loop(0, 4)(project)
        yield
        pl.loop(4, 8)(project)
        for x, y in ((hid, hid_h), (raw, raw_h), (qkv, qkv_h), (tab, tab_h)):
            stores.append(net.copy(x, y))
        for h in range(2):
            attend(h, 0)
        yield
        for n in range(1, 4):
            for h in range(2):
                attend(h, n)
            if n < 3:
                yield
        stores.append(net.copy(heads, heads_h))
        stores.append(net.copy(probs, probs_h))

        @pl.loop(0, NC)
        def _(i):
            part[i] = dot(heads[i].astype(BF), wo_all[...].reshape(QW, D), NN, BF)

    stores = []
    side = weights()
    drive(by_ctx(0), side, by_ctx(1), side, moved(), work())
    for x in stores:
        x.wait()


def mid_body(
    part, tok, cot, gvec, wgu_h, wd_h, g_h,
    ga_all, gres_ref, ggain_ref, gw2_h, gwd_h, down_h, resid,
    wgu, wd, g_all, down_part, gw2, gwd, h_all, mixed, ggu, back_part, ga, gwd_f,
    la0, sa0, la1, sa1, lb0, sb0, lb1, sb1, ss, rs, ls,
):
    s, c, core, ctx, chips, sibling, goes, comes, stays = places()
    net = Net(ss, rs, ls)
    loads = [net.copy(x, y) for x, y in ((wgu_h, wgu), (wd_h, wd), (g_h, g_all))]
    stores = []
    greet(ring_devices(ctx))

    def forward(h, land, sums):
        def got(k, total):
            r = tok[rows(h)].astype(F32) + total
            resid[rows(h)] = r
            normed, _ = rms_parts(r)
            h_all[c, rows(h)] = (normed * gvec[1:2]).astype(BF)

        yield from reduce(net, ctx, [(chunk(part, h), CPARTS, land, sums)], got)
        yield from gather(net, ctx, [(None, chunk(h_all, h), CPARTS)])

    def block(i):
        both = dot(h_all[i], wgu[...], NN)
        gate, up = both[:, :FW], both[:, FW:]
        sig = jax.nn.sigmoid(gate)
        act = gate * sig
        m = (act * up).astype(BF)
        mixed[i] = m
        gm = dot(g_all[i], wd[...], NT)
        gg = (gm * up * sig * (1.0 + gate * (1.0 - sig))).astype(BF)
        gu = (gm * act).astype(BF)
        ggu[i, :, 0:FW] = gg
        ggu[i, :, FW:] = gu
        back_part[i] = dot(jnp.concatenate([gg, gu], 1), wgu[...], NT, BF)
        down_part[i] = dot(m, wd[...], NN, BF)

    def blocks(places):
        n = len(places)

        @pl.loop(0, n)
        def _(j):
            i = places[0]
            for k in range(1, n):
                i = jnp.where(j == k, places[k], i)
            block(i)

    def work():
        yield
        yield
        yield
        for x in loads:
            x.wait()
        blocks([c])
        yield
        blocks([ctx.idx(-1, 0), ctx.idx(1, 0), ctx.idx(0, 1)])
        yield
        blocks([ctx.idx(-1, 1), ctx.idx(1, 1), ctx.idx(2, 0)])
        yield
        blocks([ctx.idx(2, 1)])

    drive(forward(0, la0, sa0), forward(1, la1, sa1), work())
    stores.append(net.copy(down_part, down_h))

    def got_back(h):
        def got(k, total):
            normed, inverse = rms_parts(resid[rows(h)])
            g = jnp.sum(total * normed, 0, keepdims=True)
            if h == 0:
                ggain_ref[...] = g
            else:
                ggain_ref[...] += g
            gres = cot[rows(h)].astype(F32) + rms_back(total * gvec[1:2], normed, inverse)
            gres_ref[rows(h)] = gres
            ga[rows(h)] = gres.astype(BF)

        return got

    def backward(h, land, sums):
        yield from reduce(net, ctx, [(chunk(back_part, h), CPARTS, land, sums)], got_back(h))
        yield from gather(net, ctx, [(ga.at[rows(h)], chunk(ga_all, h), CPARTS)])

    def grads():
        for q in range(2):

            @pl.loop(4 * q, 4 * q + 4)
            def _(j):
                left = h_all[:, :, pl.ds(pl.multiple_of(j * 128, 128), 128)].reshape(SEQ, 128)
                g = dot(left, ggu[...].reshape(SEQ, 2 * FW), TN, BF)
                gw2[0, j] = g[0:64]
                gw2[1, j] = g[64:128]

            yield
        for j in range(3):
            left = mixed[:, :, 128 * j : 128 * (j + 1)].reshape(SEQ, 128)
            gwd_f[128 * j : 128 * (j + 1)] = dot(left, g_all[...].reshape(SEQ, D), TN)
        for i in range(NS):
            gwd[i % 2, i // 2] = gwd_f[24 * i : 24 * (i + 1)].astype(BF)
        stores.append(net.copy(gw2, gw2_h))
        stores.append(net.copy(gwd, gwd_h))

    drive(backward(0, lb0, sb0), backward(1, lb1, sb1), grads())
    for x in stores:
        x.wait()


def end_body(
    ga_all, tok, gres_ref, resid, gvec, ghead, ggain, wo_all,
    gw2_h, gwd_h, down_h, qkv_h, probs_h, heads_h, raw_h, tab_h, hid_h, w1_h,
    out_ref, gx_ref, small_ref, a1, ao, a2, ad,
    down_part, qkv, probs, heads, raw, tab, hid, w1_all, gw2, gwd,
    gatt, delta, gwo_f, gk_f, gv_f, gqkv, part, gw1, gwo,
    la0, sa0, la1, sa1, lb0, sb0, lb1, sb1, h1, b1, l1, t1, h2, b2, l2, t2,
    h3, b3, l3, t3, h4, b4, l4, t4,
    s1, so, gw2_sum, gwd_sum, own_d, sm, smc, sm2, sms, ss, rs, ls,
):
    s, c, core, ctx, chips, sibling, goes, comes, stays = places()
    net = Net(ss, rs, ls)
    loads = [
        net.copy(x, y)
        for x, y in (
            (heads_h, heads), (qkv_h, qkv), (probs_h, probs), (down_h, down_part),
            (raw_h, raw), (tab_h, tab), (hid_h, hid), (w1_h, w1_all), (gw2_h, gw2), (gwd_h, gwd),
        )
    ]
    ctx_peers = [(s, lax.rem(c + d, NC)) for d in range(1, NC)]
    shard_peers = [(lax.rem(s + d, NS), c) for d in range(1, NS)]
    greet(ctx_peers + shard_peers, (goes, comes, stays))

    def feed_forward(h, land, sums):
        def got(k, total):
            out_ref[rows(h)] = (resid[rows(h)] + total).astype(BF)

        if h == 0:
            loads[3].wait()
        yield from reduce(net, ctx, [(chunk(down_part, h), CPARTS, land, sums)], got)

    def got_ff(k, total):
        (gw2_sum, gwd_sum)[k][...] = total.astype(BF)

    def feed_forward_grads():
        loads[8].wait()
        loads[9].wait()
        yield from reduce_shard(
            net, chips, core, sibling,
            [(gw2, lanes(WCOL2), h3, b3, l3, t3), (gwd, lanes(D), h4, b4, l4, t4)], got_ff,
        )
        yield from move(net, [(gwd_sum, own_d)], comes, stays)
        yield from gather(net, ctx, [(gw2_sum, at(a2), lanes(WCOL2)), (own_d, at(ad), lanes(D))])

    def got_out(k, total):
        so[...] = total.astype(BF)

    def out_grad():
        for j in range(2):
            left = heads[:, :, HD * j : HD * (j + 1)].reshape(SEQ, HD).astype(BF)
            gwo_f[HD * j : HD * (j + 1)] = dot(left, ga_all[...].reshape(SEQ, D), TN)
        for i in range(NS):
            gwo[i % 2, i // 2] = gwo_f[16 * i : 16 * (i + 1)].astype(BF)
        yield from reduce_shard(
            net, chips, core, sibling, [(gwo, lanes(D), h2, b2, l2, t2)], got_out
        )
        yield from move(net, [(so, ao.at[comes[1]])], comes, stays)
        yield from gather(net, ctx, [(None, at(ao), lanes(D))])

    def head_grads(i):
        g = dot(ga_all[i], wo_all[...].reshape(QW, D), NT, BF)
        gatt[i] = g
        both = g.astype(F32) * heads[i]
        for h in range(2):
            delta[h, pl.ds(pl.multiple_of(i * T, T), T)] = jnp.sum(
                both[:, HD * h : HD * (h + 1)], -1, keepdims=True
            )

    def attend_back(h, n, fresh):
        here = slice(2 * n, 2 * n + 2)
        mine = slice(HD * h, HD * (h + 1))
        q = qkv[here, :, mine].reshape(256, HD)
        g = gatt[here, :, mine].reshape(256, HD)
        d = delta[h, 256 * n : 256 * (n + 1)]
        gq = None
        for m in range(n + 1):
            k = qkv[2 * m : 2 * m + 2, :, 2 * HD : 3 * HD].reshape(256, HD)
            v = qkv[2 * m : 2 * m + 2, :, 3 * HD :].reshape(256, HD)
            p = probs[h, n * (n + 1) // 2 + m]
            gv = dot(p, g, TN)
            gs = (p.astype(F32) * (dot(g, v, NT) - d)).astype(BF)
            gk = dot(gs, q, TN)
            span = slice(256 * m, 256 * (m + 1))
            if fresh:
                gv_f[span] = gv
                gk_f[span] = gk
            else:
                gv_f[span] += gv
                gk_f[span] += gk
            x = dot(gs, k, NN)
            gq = x if gq is None else gq + x
        turn_back(gq * HD**-0.5, here, mine, 0, fresh)

    def turn_back(g, here, mine, kind, fresh):
        n = g.shape[0]
        cosine = tab[here, :, 0:HD].reshape(n, HD)
        sine = tab[here, :, HD:].reshape(n, HD)
        w = g * cosine - pltpu.roll(g, 64, 1) * sine
        u, inverse = rms_parts(raw[here, :, mine].reshape(n, HD))
        gain = jnp.sum(w * u, 0, keepdims=True)
        place = slice(2 * D + HD * kind, 2 * D + HD * (kind + 1))
        if fresh:
            sm[:, place] = gain
        else:
            sm[:, place] += gain
        r = rms_back(w * ghead[kind : kind + 1], u, inverse).astype(BF)
        gqkv[here, :, mine] = r.reshape(n // T, T, HD)

    def work():
        pl.loop(0, NC)(head_grads)
        loads[1].wait()
        loads[2].wait()
        loads[4].wait()
        loads[5].wait()
        yield
        for n in (3, 2, 1, 0):
            for h in range(2):
                attend_back(h, n, n == 3 and h == 0)
            if n:
                yield
        for m in range(2):
            here = slice(4 * m, 4 * m + 4)
            span = slice(512 * m, 512 * (m + 1))
            turn_back(gk_f[span] * HD**-0.5, here, slice(2 * HD, 3 * HD), 1, m == 0)
            gqkv[here, :, 3 * HD :] = gv_f[span].astype(BF).reshape(4, T, HD)
        loads[6].wait()
        loads[7].wait()

        @pl.loop(0, NC)
        def _(i):
            part[i] = dot(gqkv[i], w1_all[:, :, 0:512].reshape(D, 512), NT, BF)

    loads[0].wait()
    main = work()
    rest = drive(
        feed_forward(0, lb0, sb0), feed_forward(1, lb1, sb1), out_grad(), feed_forward_grads(), main,
        until=main,
    )

    def got_input(h):
        def got(k, total):
            normed, inverse = rms_parts(tok[rows(h)].astype(F32))
            g = jnp.sum(total * normed, 0, keepdims=True)
            if h == 0:
                sm[:, 0:D] = g
            else:
                sm[:, 0:D] += g
            gx_ref[rows(h)] = gres_ref[rows(h)] + rms_back(total * gvec[0:1], normed, inverse)

        return got

    def by_ctx(h, land, sums):
        yield from reduce(net, ctx, [(chunk(part, h), CPARTS, land, sums)], got_input(h))

    def small():
        yield
        yield
        yield
        yield
        sm[:, D : 2 * D] = ggain[...]
        smc[c] = sm[...]
        sent = [net.send(sm, smc.at[c], d) for d in ctx_peers]
        yield
        for x in sent:
            x.wait()
        total = smc[0]
        for i in range(1, NC):
            total = total + smc[i]
        sm2[...] = total
        sms[s] = total
        sent = [net.send(sm2, sms.at[s], d) for d in shard_peers]
        yield
        for x in sent:
            x.wait()
        total = sms[0]
        for i in range(1, NS):
            total = total + sms[i]
        small_ref[...] = total

    def got_shard(k, total):
        s1[...] = total.astype(BF)

    def grads():
        @pl.loop(0, 8)
        def _(j):
            left = hid[:, :, pl.ds(pl.multiple_of(j * 128, 128), 128)].reshape(SEQ, 128)
            g = dot(left, gqkv[...].reshape(SEQ, 512), TN, BF)
            gw1[0, j] = g[0:64]
            gw1[1, j] = g[64:128]

        yield from reduce_shard(
            net, chips, core, sibling, [(gw1, lanes(512), h1, b1, l1, t1)], got_shard
        )
        yield from gather(net, ctx, [(s1, at(a1), lanes(512))])

    last = grads()
    drive(by_ctx(0, la0, sa0), last, by_ctx(1, la1, sa1), last, *rest, small())


def assemble_body(
    out_h, gx_h, a1_h, ao_h, a2_h, ad_h,
    out_ref, gx_ref, q_out, k_out, v_out, o_out, gate_out, up_out, down_out,
    a1, ao, a2, ad, sem,
):
    pairs = ((a2_h, a2), (a1_h, a1), (ao_h, ao), (ad_h, ad), (out_h, out_ref), (gx_h, gx_ref))
    loads = [pltpu.make_async_copy(x, y, sem.at[k]) for k, (x, y) in enumerate(pairs)]
    for x in loads:
        x.start()
    loads[0].wait()
    for i in range(NC):
        gate_out[:, FW * i : FW * (i + 1)] = a2[i, :, 0:FW].astype(F32)
        up_out[:, FW * i : FW * (i + 1)] = a2[i, :, FW : 2 * FW].astype(F32)
    for x in loads[1:]:
        x.wait()
    for i in range(NC):
        q_out[:, QW * i : QW * (i + 1)] = a1[i, :, 0:QW].astype(F32)
        k_out[:, HD * i : HD * (i + 1)] = a1[i, :, QW : QW + HD].astype(F32)
        v_out[:, HD * i : HD * (i + 1)] = a1[i, :, QW + HD :].astype(F32)
        o_out[16 * i : 16 * (i + 1), :] = ao[i].astype(F32)
        down_out[24 * i : 24 * (i + 1), :] = ad[i].astype(F32)


def shards(
    tokens, positions, attn_gain, query_weight, key_matrix, value_matrix, query_gain, key_gain,
    out_weight, mlp_gain, gate_weight, up_weight, down_weight, cotangent,
):
    c = lax.axis_index("ctx")
    s = lax.axis_index("shard")
    tok, cot = tokens[0], cotangent[0]

    row0 = jnp.concatenate([attn_gain, mlp_gain])[None]
    row1 = jnp.concatenate([query_gain, key_gain, jnp.zeros((112,), BF)])[None]
    gains = jnp.concatenate([row0, row1, jnp.zeros((62, 128), BF)], 0)
    wo = out_weight.reshape(8, 16, D)
    wd = down_weight.reshape(8, 24, D)

    freq = np.power(ROPE_BASE, -np.arange(HD // 2) * (2.0 / HD)).astype(np.float32)
    freq = np.concatenate([freq, freq])[:, None]

    (
        g_all, w1_all, wo_all, w2_all, wd_all, hid, raw, qkv, tab, probs, heads, out_part, gvec, ghead,
    ) = remote_call(
        start_body,
        [
            ((NC, T, D), BF, "h"), ((NS, 64, WCOL1), BF, "v"), ((NS, 16, D), BF, "v"),
            ((NS, 64, WCOL2), BF, "h"), ((NS, 24, D), BF, "h"),
            ((NC, T, D), BF, "h"), ((NC, T, 512), F32, "h"), ((NC, T, 512), BF, "h"),
            ((NC, T, 2 * HD), F32, "h"), ((2, 10, 256, 256), BF, "h"), ((NC, T, QW), F32, "h"),
            ((NC, T, D), BF, "v"), ((2, D), F32, "v"), ((2, HD), F32, "v"),
        ],
        "h" * 11 + "v",
        (
            tok, cot, positions, query_weight, key_matrix, value_matrix, gate_weight, up_weight,
            gains, wo, wd, freq,
        ),
        [
            pltpu.VMEM((NC, T, D), BF), pltpu.VMEM((NC, 1, T), jnp.int32),
            pltpu.VMEM((64, WCOL1), BF), pltpu.VMEM((64, WCOL2), BF),
            pltpu.VMEM((NC, T, D), BF), pltpu.VMEM((NC, T, 512), F32),
            pltpu.VMEM((NC, T, 512), BF), pltpu.VMEM((NC, T, 2 * HD), F32),
            pltpu.VMEM((2, 10, 256, 256), BF), pltpu.VMEM((NC, T, QW), F32),
        ],
        144, 24, 0, 58 << 20,
    )
    ga_all, grad_resid, ggain_mlp, gw2, gwd, down_part, resid = remote_call(
        mid_body,
        [
            ((NC, T, D), BF, "h"), ((T, D), F32, "v"), ((1, D), F32, "v"),
            ((2, 8, 64, WCOL2), BF, "h"), ((2, 8, 24, D), BF, "h"),
            ((NC, T, D), BF, "h"), ((T, D), F32, "v"),
        ],
        "vvvvhhh",
        (out_part, tok, cot, gvec, w2_all.reshape(D, 2 * FW), wd_all.reshape(FW, D), g_all),
        [
            pltpu.VMEM((D, 2 * FW), BF), pltpu.VMEM((FW, D), BF), pltpu.VMEM((NC, T, D), BF),
            pltpu.VMEM((NC, T, D), BF), pltpu.VMEM((2, 8, 64, WCOL2), BF),
            pltpu.VMEM((2, 8, 24, D), BF),
            pltpu.VMEM((NC, T, D), BF), pltpu.VMEM((NC, T, FW), BF), pltpu.VMEM((NC, T, 2 * FW), BF),
            pltpu.VMEM((NC, T, D), BF), pltpu.VMEM((T, D), BF), pltpu.VMEM((FW, D), F32),
        ]
        + chunk_scratch() * 2,
        96, 16, 1, 58 << 20,
    )
    output, gx, small, a1, ao, a2, ad = remote_call(
        end_body,
        [
            ((T, D), BF, "v"), ((T, D), F32, "v"), ((1, SMALL), F32, "v"),
            ((NC, 64, 512), BF, "v"), ((NC, 16, D), BF, "v"),
            ((NC, 64, WCOL2), BF, "v"), ((NC, 24, D), BF, "v"),
        ],
        "v" * 8 + "h" * 10,
        (
            ga_all, tok, grad_resid, resid, gvec, ghead, ggain_mlp, wo_all, gw2, gwd,
            down_part, qkv, probs, heads, raw, tab, hid, w1_all,
        ),
        [
            pltpu.VMEM((NC, T, D), BF), pltpu.VMEM((NC, T, 512), BF),
            pltpu.VMEM((2, 10, 256, 256), BF),
            pltpu.VMEM((NC, T, QW), F32), pltpu.VMEM((NC, T, 512), F32),
            pltpu.VMEM((NC, T, 2 * HD), F32), pltpu.VMEM((NC, T, D), BF),
            pltpu.VMEM((NS, 64, WCOL1), BF),
            pltpu.VMEM((2, 8, 64, WCOL2), BF), pltpu.VMEM((2, 8, 24, D), BF),
            pltpu.VMEM((NC, T, QW), BF), pltpu.VMEM((2, SEQ, 1), F32), pltpu.VMEM((QW, D), F32),
            pltpu.VMEM((SEQ, HD), F32), pltpu.VMEM((SEQ, HD), F32), pltpu.VMEM((NC, T, 512), BF),
            pltpu.VMEM((NC, T, D), BF), pltpu.VMEM((2, 8, 64, 512), BF),
            pltpu.VMEM((2, 8, 16, D), BF),
        ]
        + chunk_scratch() * 2 + shard_scratch((64, 512)) + shard_scratch((16, D))
        + shard_scratch((64, WCOL2)) + shard_scratch((24, D))
        + [
            pltpu.VMEM((64, 512), BF), pltpu.VMEM((16, D), BF),
            pltpu.VMEM((64, WCOL2), BF), pltpu.VMEM((24, D), BF), pltpu.VMEM((24, D), BF),
            pltpu.VMEM((1, SMALL), F32), pltpu.VMEM((NC, 1, SMALL), F32),
            pltpu.VMEM((1, SMALL), F32), pltpu.VMEM((NS, 1, SMALL), F32),
        ],
        176, 24, 2, 58 << 20,
    )
    any_, whole = pl.BlockSpec(memory_space=pl.ANY), pl.BlockSpec(memory_space=pltpu.VMEM)
    output, gx, gwq, gwk, gwv, gwo_out, gwg, gwu, gwd_out = pl.pallas_call(
        assemble_body,
        out_shape=[
            jax.ShapeDtypeStruct((T, D), BF), jax.ShapeDtypeStruct((T, D), F32),
            jax.ShapeDtypeStruct((64, 2048), F32), jax.ShapeDtypeStruct((64, 1024), F32),
            jax.ShapeDtypeStruct((64, 1024), F32), jax.ShapeDtypeStruct((128, D), F32),
            jax.ShapeDtypeStruct((64, 3072), F32), jax.ShapeDtypeStruct((64, 3072), F32),
            jax.ShapeDtypeStruct((192, D), F32),
        ],
        in_specs=[any_] * 6,
        out_specs=[whole] * 9,
        scratch_shapes=[
            pltpu.VMEM((NC, 64, 512), BF), pltpu.VMEM((NC, 16, D), BF),
            pltpu.VMEM((NC, 64, WCOL2), BF), pltpu.VMEM((NC, 24, D), BF),
            pltpu.SemaphoreType.DMA((6,)),
        ],
        compiler_params=pltpu.CompilerParams(vmem_limit_bytes=58 << 20),
    )(output, gx, a1, ao, a2, ad)
    small = small[0]

    def own(offset, width):
        return lax.dynamic_slice(small, (offset + s * width,), (width,))

    return (
        output[None], gx[None], own(0, 64), gwq, gwk, gwv, own(2 * D, 8), own(2 * D + HD, 8),
        gwo_out, own(D, 64), gwg, gwu, gwd_out,
    )


def solution(mesh):
    split = P("shard", "ctx", None)
    rows, vec = P("shard", None), P("shard")
    in_specs = (
        split, P("shard", "ctx"), vec, rows, rows, rows, vec, vec, rows, vec, rows, rows, rows, split,
    )
    out_specs = (split, split, vec, rows, rows, rows, vec, vec, rows, vec, rows, rows, rows)
    return jax.shard_map(shards, mesh=mesh, in_specs=in_specs, out_specs=out_specs, check_vma=False)
```

```python
import jax
import jax.numpy as jnp
import numpy as np
from jax import lax
from jax.experimental import pallas as pl
from jax.experimental.pallas import tpu as pltpu
from jax.sharding import PartitionSpec as P

MESH = pl.DeviceIdType.MESH
BF = jnp.bfloat16
F32 = jnp.float32

NS = 16
NC = 8
T = 128
SEQ = 1024
D = 1024
HD = 128
QW = 256
FW = 384
EPSILON = 1e-06
ROPE_BASE = 1000000.0
BLOCKED_SCORE = -1e30
SMALL = 2304

ALL = slice(None)


def view(ref, part):
    return ref.at[tuple(pl.ds(p.start, p.stop - p.start) if p != ALL else p for p in part)]


class Ring:
    def __init__(self, me, device):
        self.a = me // 2
        self.b = lax.rem(me, 2)
        self.device = device

    def idx(self, da, db):
        return lax.rem(self.a + da + 4, 4) * 2 + lax.rem(self.b + db, 2)

    def dev(self, da, db):
        return self.device(self.idx(da, db))


class Net:
    def __init__(self, send, recv, local):
        self.s, self.r, self.l = send, recv, local
        self.n = 0
        self.m = 0

    def send(self, src, dst, to):
        k = self.n
        self.n += 1
        c = pltpu.make_async_remote_copy(
            src_ref=src, dst_ref=dst, send_sem=self.s.at[k], recv_sem=self.r.at[k],
            device_id=to, device_id_type=MESH,
        )
        c.start()
        return c

    def copy(self, src, dst):
        k = self.m
        self.m += 1
        c = pltpu.make_async_copy(src, dst, self.l.at[k])
        c.start()
        return c


def places():
    s = lax.axis_index("shard")
    c = lax.axis_index("ctx")
    core = lax.rem(s, 2)
    ctx = Ring(c, lambda i: (s, i))
    chips = Ring(s // 2, lambda i: (i * 2 + core, c))
    sibling = (s + 1 - 2 * core, c)
    half, rest = lax.rem(s, 2), s // 2
    goes = (8 * half + c, rest)
    comes = (2 * c + s // 8, lax.rem(s, 8))
    stays = jnp.logical_and(goes[0] == s, goes[1] == c)
    return s, c, core, ctx, chips, sibling, goes, comes, stays


def ring_devices(ring):
    return [ring.dev(-1, 0), ring.dev(1, 0), ring.dev(0, 1)]


def greet(devices, moved=None):
    barrier = pltpu.get_barrier_semaphore()
    for d in devices:
        pl.semaphore_signal(barrier, inc=1, device_id=d, device_id_type=MESH)
    if moved is not None:
        goes, comes, stays = moved

        @pl.when(jnp.logical_not(stays))
        def _():
            for d in (goes, comes):
                pl.semaphore_signal(barrier, inc=1, device_id=d, device_id_type=MESH)
            pl.semaphore_wait(barrier, len(devices) + 2)

        @pl.when(stays)
        def _():
            pl.semaphore_wait(barrier, len(devices))

    else:
        pl.semaphore_wait(barrier, len(devices))


def drive(*threads, until=None):
    threads = list(threads)
    ended = set()
    while threads:
        for x in list(threads):
            if id(x) in ended:
                continue
            try:
                next(x)
            except StopIteration:
                ended.add(id(x))
        threads = [x for x in threads if id(x) not in ended]
        if until is not None and id(until) in ended:
            break
    return threads


def move(net, items, to, stays):
    base = net.n
    net.n += len(items)

    def remote(k, src, dst):
        return pltpu.make_async_remote_copy(
            src_ref=src, dst_ref=dst, send_sem=net.s.at[base + k], recv_sem=net.r.at[base + k],
            device_id=to, device_id_type=MESH,
        )

    @pl.when(jnp.logical_not(stays))
    def _():
        for k, (src, dst) in enumerate(items):
            remote(k, src, dst).start()

    @pl.when(stays)
    def _():
        for k, (src, dst) in enumerate(items):
            pltpu.make_async_copy(src, dst, net.r.at[base + k]).start()

    yield

    @pl.when(jnp.logical_not(stays))
    def _():
        for k, (src, dst) in enumerate(items):
            remote(k, src, dst).wait()

    @pl.when(stays)
    def _():
        for k, (src, dst) in enumerate(items):
            pltpu.make_async_copy(src, dst, net.r.at[base + k]).wait()


def gather(net, ring, items, slot=lambda i: i, sibling=None):
    left, right, pair = ring_devices(ring)
    me = ring.idx(0, 0)
    over = []

    def pass_on(places):
        if sibling is not None:
            for _, at, _ in items:
                for i in places:
                    over.append(net.send(at(slot(i)), at(slot(i)), sibling))

    first, local = [], []
    for own, at, _ in items:
        here = at(slot(me))
        src = here if own is None else own
        for n in (left, right, pair):
            first.append(net.send(src, here, n))
        if sibling is not None:
            over.append(net.send(src, here, sibling))
        if own is not None:
            local.append(net.copy(own, here))
    yield
    for c in first:
        c.wait_recv()
    second = []
    a, b, z = ring.idx(-1, 0), ring.idx(1, 0), ring.idx(0, 1)
    for _, at, _ in items:
        for i, n in ((a, right), (z, left), (a, pair)):
            second.append(net.send(at(slot(i)), at(slot(i)), n))
    pass_on((a, b, z))
    yield
    for c in second:
        c.wait_recv()
    third = []
    az, bz, o, oz = ring.idx(-1, 1), ring.idx(1, 1), ring.idx(2, 0), ring.idx(2, 1)
    for _, at, parts in items:
        for i, n, part in ((az, right, parts[0]), (bz, left, parts[1]), (o, pair, parts[2])):
            if part is not None:
                r = view(at(slot(i)), part)
                third.append(net.send(r, r, n))
    pass_on((az, bz, o))
    yield
    for c in third:
        c.wait_recv()
    pass_on((oz,))
    for c in local:
        c.wait()
    for c in first + second + third:
        c.wait_send()
    if sibling is not None:
        yield
        for c in over:
            c.wait()


def gather_shard(net, ring, slot, across, sibling, items):
    me, z = ring.idx(0, 0), ring.idx(0, 1)
    over, local, first = [], [], []

    def pass_on(at, *places):
        for i in places:
            over.append(net.send(at(slot(i)), at(slot(i)), sibling))

    for own, other, at in items:
        for i in (me, z) if own is None else (me,):
            here = at(slot(i))
            src = here if own is None else own
            for d in (1, 3, 2):
                first.append(net.send(src, here, ring.dev(d, 0)))
            over.append(net.send(src, here, sibling))
        if own is not None:
            for d in across:
                first.append(net.send(other, here, d))
            local.append(net.copy(own, here))
    yield
    yield
    for c in first:
        c.wait_recv()
    for own, _, at in items:
        for d in (1, 3, 2):
            pass_on(at, ring.idx(d, 0), ring.idx(d, 1))
        if own is not None:
            pass_on(at, z)
    for c in local:
        c.wait()
    yield
    for c in first:
        c.wait_send()
    for c in over:
        c.wait()


def gather_peers(net, ring, items):
    me = ring.idx(0, 0)
    sent, local = [], []
    for own, at in items:
        here = at(me)
        for d in range(1, 8):
            sent.append(net.send(here if own is None else own, here, ring.device(lax.rem(me + d, 8))))
        if own is not None:
            local.append(net.copy(own, here))
    yield
    for c in sent + local:
        c.wait()


def reduce(net, ring, items, result):
    left, right, pair = ring_devices(ring)
    me, a, b, z = ring.idx(0, 0), ring.idx(-1, 0), ring.idx(1, 0), ring.idx(0, 1)
    az, bz, o, oz = ring.idx(-1, 1), ring.idx(1, 1), ring.idx(2, 0), ring.idx(2, 1)

    def plus(x, y):
        return (x.astype(F32) + y.astype(F32)).astype(BF)

    first, second, third = [], [], []
    for p, parts, land, _ in items:
        for n, part in zip((left, right, pair), parts):
            if part is None:
                continue
            first.append(net.send(view(p(oz), part), view(land.at[0], part), n))
    yield
    for c in first:
        c.wait_recv()
    for p, parts, land, sums in items:
        for k, (i, part, n) in enumerate(
            ((o, parts[2], left), (bz, parts[1], right), (az, parts[0], pair))
        ):
            if part is None:
                second.append(net.send(p(i), land.at[1 + k], n))
                continue
            sums[k] = p(i)[...]
            sums[(k,) + part] = plus(p(i)[part], land[(0,) + part])
            second.append(net.send(sums.at[k], land.at[1 + k], n))
    yield
    for c in second:
        c.wait_recv()
    for p, parts, land, sums in items:
        third.append(net.send(p(b), land.at[5], right))
        sums[4] = plus(p(z)[...], land[2])
        third.append(net.send(sums.at[4], land.at[6], pair))
        sums[3] = (p(a)[...].astype(F32) + land[1].astype(F32) + land[3].astype(F32)).astype(BF)
        third.append(net.send(sums.at[3], land.at[4], left))
    yield
    for c in third:
        c.wait_recv()
    for k, (p, parts, land, sums) in enumerate(items):
        result(
            k,
            (p(me)[...].astype(F32) + land[4].astype(F32))
            + (land[5].astype(F32) + land[6].astype(F32)),
        )
    for c in first + second + third:
        c.wait_send()


def at(ref):
    return lambda i: ref.at[i]


CHUNKS = 4
CROWS = T // CHUNKS
CPARTS = ((slice(0, CROWS // 2), ALL), (slice(CROWS // 2, CROWS), ALL), None)


def rows(h):
    return pl.ds(CROWS * h, CROWS)


def chunk(ref, h):
    return lambda i: ref.at[i, rows(h)]


def each(thread, land, sums):
    return [thread(h, land.at[:, rows(h)], sums.at[:, rows(h)]) for h in range(CHUNKS)]


def chunk_scratch():
    return [pltpu.VMEM((7, T, D), BF), pltpu.VMEM((5, T, D), BF)]


def reduce_shard(net, chips, core, sibling, items, result):
    over, sent = [], []
    for p, half, _, _ in items:
        over.append(net.send(p.at[1 - core], half, sibling))
    yield
    me = chips.idx(0, 0)
    for c in over:
        c.wait_recv()
    for p, half, both, land in items:

        @pl.loop(0, 8)
        def _(j):
            both[j] = (p[core, j].astype(F32) + half[j].astype(F32)).astype(BF)

        for d in range(1, 8):
            j = lax.rem(me + d, 8)
            sent.append(net.send(both.at[j], land.at[me], chips.device(j)))
    yield
    for c in sent:
        c.wait_recv()
    for k, (_, _, both, land) in enumerate(items):
        total = both[me].astype(F32)
        for d in range(1, 8):
            total = total + land[lax.rem(me + d, 8)].astype(F32)
        result(k, total)
    for c in over + sent:
        c.wait_send()


def shard_scratch(shape):
    return [pltpu.VMEM((8,) + shape, BF)] * 3


def rms_parts(v):
    inverse = lax.rsqrt(jnp.mean(v * v, -1, keepdims=True) + EPSILON)
    return v * inverse, inverse


def rms_back(g, n, inverse):
    return inverse * (g - n * jnp.mean(g * n, -1, keepdims=True))


def dot(a, b, dims, out=F32):
    return lax.dot_general(a, b, (dims, ((), ())), preferred_element_type=F32).astype(out)


NN = ((1,), (0,))
NT = ((1,), (1,))
TN = ((0,), (0,))


def remote_call(body, outs, ins, args, scratch, copies, locals_, number, vmem=None):
    sems = [
        pltpu.SemaphoreType.DMA((copies,)),
        pltpu.SemaphoreType.DMA((copies,)),
        pltpu.SemaphoreType.DMA((locals_,)),
    ]
    space = {"v": pl.BlockSpec(memory_space=pltpu.VMEM), "h": pl.BlockSpec(memory_space=pl.ANY)}
    return pl.pallas_call(
        body,
        out_shape=[jax.ShapeDtypeStruct(s, d) for s, d, _ in outs],
        in_specs=[space[k] for k in ins],
        out_specs=[space[k] for _, _, k in outs],
        scratch_shapes=list(scratch) + sems,
        compiler_params=pltpu.CompilerParams(
            collective_id=number, has_side_effects=True, vmem_limit_bytes=vmem
        ),
    )(*args)


WCOL1 = 640
WCOL2 = 768


def start_body(
    tok, cot, pos, wq, wk, wv, wg, wu, gblock, wo, wd, freq,
    g_all, w1_all, wo_all, w2_all, wd_all, hid_h, raw_h, qkv_h, tab_h, probs_h, heads_h, part, gvec, ghead,
    x_all, p_all, w1, w2, v1, v2, hid, raw, qkv, tab, probs, heads, ss, rs, ls,
):
    s, c, core, ctx, chips, sibling, goes, comes, stays = places()
    net = Net(ss, rs, ls)

    other = c + 1 - 2 * lax.rem(c, 2)
    flip = s + 2 - 4 * lax.rem(s // 2, 2)
    across = [((lax.rem(s // 4 + d, 4)) * 4 + lax.rem(flip, 4), other) for d in (0, 1, 3, 2)]
    goes_z = (goes[0] + 2 - 4 * lax.rem(goes[0] // 2, 2), goes[1])
    comes_z = (2 * c + flip // 8, lax.rem(flip, 8))

    def cut(w, width, i):
        return w.at[:, pl.ds(pl.multiple_of(i * width, 128), width)]

    loads = [
        net.copy(x, y)
        for i, one, two in ((c, w1, w2), (other, v1, v2))
        for x, y in (
            (cut(wq, QW, i), one.at[:, 0:QW]), (cut(wk, HD, i), one.at[:, QW : QW + HD]),
            (cut(wv, HD, i), one.at[:, QW + HD : 512]), (gblock, one.at[:, 512:WCOL1]),
            (cut(wg, FW, i), two.at[:, 0:FW]), (cut(wu, FW, i), two.at[:, FW : 2 * FW]),
        )
    ]
    greet(
        ring_devices(ctx) + [chips.dev(d, 0) for d in (1, 2, 3)] + across + [sibling, goes_z, comes_z],
        (goes, comes, stays),
    )
    for x in loads:
        x.wait()

    def place(i):
        return i * 2 + core

    def weights():
        yield from gather_shard(
            net, chips, place, across, sibling, [(w1, v1, at(w1_all))]
        )
        yield from gather_shard(
            net, chips, place, across, sibling,
            [
                (w2, v2, at(w2_all)), (None, None, at(wd_all)), (None, None, at(wo_all)),
            ],
        )

    def moved():
        moved = [(wo.at[c], wo_all.at[goes[0]]), (wd.at[c], wd_all.at[goes[0]])]
        second = [net.send(x, y, goes_z) for x, y in moved]
        yield from move(net, moved, goes, stays)
        for x in second:
            x.wait()

    def by_ctx(h):
        items = [(tok.at[rows(h)], chunk(x_all, h), CPARTS)]
        if h == 0:
            items.append((pos, at(p_all), ((ALL, ALL), None, None)))
        yield from gather(net, ctx, items)
        yield from gather(net, ctx, [(cot.at[rows(h)], chunk(g_all, h), CPARTS)])

    def gains():
        lane = lax.broadcasted_iota(jnp.int32, (8, 128), 1)
        t = [w1_all[i, 0:16, 512:640].astype(F32)[0:8] for i in range(NS)]
        for j in range(8):
            x, y = t[2 * j], t[2 * j + 1]
            low = lane < 64
            gvec[0:1, 128 * j : 128 * (j + 1)] = jnp.where(low, x, pltpu.roll(y, 64, 1))[0:1]
            gvec[1:2, 128 * j : 128 * (j + 1)] = jnp.where(low, pltpu.roll(x, 64, 1), y)[0:1]
        q = jnp.zeros((8, 128), F32)
        k = jnp.zeros((8, 128), F32)
        for i in range(NS):
            here = lane // 8 == i
            q = jnp.where(here, pltpu.roll(t[i], 8 * i, 1), q)
            k = jnp.where(here, pltpu.roll(t[i], (8 * i + 120) % 128, 1), k)
        ghead[0:1] = q[1:2]
        ghead[1:2] = k[1:2]

    def project(i):
        normed, _ = rms_parts(x_all[i].astype(F32))
        h = (normed * gvec[0:1]).astype(BF)
        hid[i] = h
        r = dot(h, w1_all[:, :, 0:512].reshape(D, 512), NN)
        raw[i] = r
        angle = freq[...] * p_all[i].astype(F32)
        cosine = jnp.cos(angle).T
        sine = jnp.sin(angle).T
        sine = jnp.where(lax.broadcasted_iota(jnp.int32, (T, HD), 1) < HD // 2, -sine, sine)
        tab[i, :, 0:HD] = cosine
        tab[i, :, HD:] = sine
        for k in range(3):
            n, _ = rms_parts(r[:, HD * k : HD * (k + 1)])
            u = n * ghead[k // 2 : k // 2 + 1]
            qkv[i, :, HD * k : HD * (k + 1)] = (u * cosine + pltpu.roll(u, 64, 1) * sine).astype(BF)
        qkv[i, :, 3 * HD :] = r[:, 3 * HD :].astype(BF)

    def attend(h, n):
        width = 256 * (n + 1)
        q = qkv[2 * n : 2 * n + 2, :, HD * h : HD * (h + 1)].reshape(256, HD)
        k = qkv[0 : 2 * n + 2, :, 2 * HD : 3 * HD].reshape(width, HD)
        v = qkv[0 : 2 * n + 2, :, 3 * HD :].reshape(width, HD)
        score = dot(q, k, NT) * HD**-0.5
        row = lax.broadcasted_iota(jnp.int32, (256, width), 0) + 256 * n
        col = lax.broadcasted_iota(jnp.int32, (256, width), 1)
        score = jnp.where(col <= row, score, BLOCKED_SCORE)
        top = jnp.max(score, -1, keepdims=True)
        e = jnp.exp(score - top)
        total = jnp.sum(e, -1, keepdims=True)
        share = 1.0 / total
        o = dot(e.astype(BF), v, NN) * share
        e = e * share
        for m in range(n + 1):
            probs[h, n * (n + 1) // 2 + m] = e[:, 256 * m : 256 * (m + 1)].astype(BF)
        heads[2 * n : 2 * n + 2, :, HD * h : HD * (h + 1)] = o.reshape(2, T, HD)

    def work():
        yield
        yield
        yield
        gains()
        pl.loop(0, 4)(project)
        yield
        pl.loop(4, 8)(project)
        for x, y in ((hid, hid_h), (raw, raw_h), (qkv, qkv_h), (tab, tab_h)):
            stores.append(net.copy(x, y))
        for h in range(2):
            attend(h, 0)
        yield
        for n in range(1, 4):
            for h in range(2):
                attend(h, n)
            if n < 3:
                yield
        stores.append(net.copy(heads, heads_h))
        stores.append(net.copy(probs, probs_h))

        @pl.loop(0, NC)
        def _(i):
            part[i] = dot(heads[i].astype(BF), wo_all[...].reshape(QW, D), NN, BF)

    stores = []
    side = weights()
    drive(side, *[by_ctx(h) for h in range(CHUNKS)], moved(), work())
    for x in stores:
        x.wait()


def mid_body(
    part, tok, cot, gvec, wgu_h, wd_h, g_h,
    ga_all, gres_ref, ggain_ref, gw2_h, gwd_h, down_h, resid,
    wgu, wd, g_all, down_part, gw2, gwd, h_all, mixed, ggu, back_part, ga, gwd_f,
    la, sa, lb, sb, ss, rs, ls,
):
    s, c, core, ctx, chips, sibling, goes, comes, stays = places()
    net = Net(ss, rs, ls)
    loads = [net.copy(x, y) for x, y in ((wgu_h, wgu), (wd_h, wd), (g_h, g_all))]
    stores = []
    greet(ring_devices(ctx))

    def forward(h, land, sums):
        def got(k, total):
            r = tok[rows(h)].astype(F32) + total
            resid[rows(h)] = r
            normed, _ = rms_parts(r)
            h_all[c, rows(h)] = (normed * gvec[1:2]).astype(BF)

        yield from reduce(net, ctx, [(chunk(part, h), CPARTS, land, sums)], got)
        yield from gather(net, ctx, [(None, chunk(h_all, h), CPARTS)])

    def block(i):
        both = dot(h_all[i], wgu[...], NN)
        gate, up = both[:, :FW], both[:, FW:]
        sig = jax.nn.sigmoid(gate)
        act = gate * sig
        m = (act * up).astype(BF)
        mixed[i] = m
        gm = dot(g_all[i], wd[...], NT)
        gg = (gm * up * sig * (1.0 + gate * (1.0 - sig))).astype(BF)
        gu = (gm * act).astype(BF)
        ggu[i, :, 0:FW] = gg
        ggu[i, :, FW:] = gu
        back_part[i] = dot(jnp.concatenate([gg, gu], 1), wgu[...], NT, BF)
        down_part[i] = dot(m, wd[...], NN, BF)

    def blocks(places):
        n = len(places)

        @pl.loop(0, n)
        def _(j):
            i = places[0]
            for k in range(1, n):
                i = jnp.where(j == k, places[k], i)
            block(i)

    def work():
        yield
        yield
        yield
        for x in loads:
            x.wait()
        blocks([c])
        yield
        blocks([ctx.idx(-1, 0), ctx.idx(1, 0), ctx.idx(0, 1)])
        yield
        blocks([ctx.idx(-1, 1), ctx.idx(1, 1), ctx.idx(2, 0)])
        yield
        blocks([ctx.idx(2, 1)])

    drive(*each(forward, la, sa), work())
    stores.append(net.copy(down_part, down_h))

    def got_back(h):
        def got(k, total):
            normed, inverse = rms_parts(resid[rows(h)])
            g = jnp.sum(total * normed, 0, keepdims=True)
            if h == 0:
                ggain_ref[...] = g
            else:
                ggain_ref[...] += g
            gres = cot[rows(h)].astype(F32) + rms_back(total * gvec[1:2], normed, inverse)
            gres_ref[rows(h)] = gres
            ga[rows(h)] = gres.astype(BF)

        return got

    def backward(h, land, sums):
        yield from reduce(net, ctx, [(chunk(back_part, h), CPARTS, land, sums)], got_back(h))
        yield from gather(net, ctx, [(ga.at[rows(h)], chunk(ga_all, h), CPARTS)])

    def grads():
        for q in range(2):

            @pl.loop(4 * q, 4 * q + 4)
            def _(j):
                left = h_all[:, :, pl.ds(pl.multiple_of(j * 128, 128), 128)].reshape(SEQ, 128)
                g = dot(left, ggu[...].reshape(SEQ, 2 * FW), TN, BF)
                gw2[0, j] = g[0:64]
                gw2[1, j] = g[64:128]

            yield
        for j in range(3):
            left = mixed[:, :, 128 * j : 128 * (j + 1)].reshape(SEQ, 128)
            gwd_f[128 * j : 128 * (j + 1)] = dot(left, g_all[...].reshape(SEQ, D), TN)
        for i in range(NS):
            gwd[i % 2, i // 2] = gwd_f[24 * i : 24 * (i + 1)].astype(BF)
        stores.append(net.copy(gw2, gw2_h))
        stores.append(net.copy(gwd, gwd_h))

    drive(*each(backward, lb, sb), grads())
    for x in stores:
        x.wait()


def end_body(
    ga_all, tok, gres_ref, resid, gvec, ghead, ggain, wo_all,
    gw2_h, gwd_h, down_h, qkv_h, probs_h, heads_h, raw_h, tab_h, hid_h, w1_h,
    out_ref, gx_ref, small_ref, a1, ao, a2, ad,
    down_part, qkv, probs, heads, raw, tab, hid, w1_all, gw2, gwd,
    gatt, delta, gwo_f, gk_f, gv_f, gqkv, part, gw1, gwo,
    la, sa, lb, sb, h1, b1, l1, h2, b2, l2,
    h3, b3, l3, h4, b4, l4,
    s1, so, gw2_sum, gwd_sum, own_d, sm, smc, sm2, sms, ss, rs, ls,
):
    s, c, core, ctx, chips, sibling, goes, comes, stays = places()
    net = Net(ss, rs, ls)
    loads = [
        net.copy(x, y)
        for x, y in (
            (heads_h, heads), (qkv_h, qkv), (probs_h, probs), (down_h, down_part),
            (raw_h, raw), (tab_h, tab), (hid_h, hid), (w1_h, w1_all), (gw2_h, gw2), (gwd_h, gwd),
        )
    ]
    ctx_peers = [(s, lax.rem(c + d, NC)) for d in range(1, NC)]
    shard_peers = [(lax.rem(s + d, NS), c) for d in range(1, NS)]
    greet(ctx_peers + shard_peers, (goes, comes, stays))

    def feed_forward(h, land, sums):
        def got(k, total):
            out_ref[rows(h)] = (resid[rows(h)] + total).astype(BF)

        if h == 0:
            loads[3].wait()
        yield from reduce(net, ctx, [(chunk(down_part, h), CPARTS, land, sums)], got)

    def got_ff(k, total):
        (gw2_sum, gwd_sum)[k][...] = total.astype(BF)

    def feed_forward_grads():
        loads[8].wait()
        loads[9].wait()
        yield from reduce_shard(
            net, chips, core, sibling,
            [(gw2, h3, b3, l3), (gwd, h4, b4, l4)], got_ff,
        )
        yield from move(net, [(gwd_sum, own_d)], comes, stays)
        yield from gather_peers(net, ctx, [(gw2_sum, at(a2)), (own_d, at(ad))])

    def got_out(k, total):
        so[...] = total.astype(BF)

    def out_grad():
        for j in range(2):
            left = heads[:, :, HD * j : HD * (j + 1)].reshape(SEQ, HD).astype(BF)
            gwo_f[HD * j : HD * (j + 1)] = dot(left, ga_all[...].reshape(SEQ, D), TN)
        for i in range(NS):
            gwo[i % 2, i // 2] = gwo_f[16 * i : 16 * (i + 1)].astype(BF)
        yield from reduce_shard(
            net, chips, core, sibling, [(gwo, h2, b2, l2)], got_out
        )
        yield from move(net, [(so, ao.at[comes[1]])], comes, stays)
        yield from gather_peers(net, ctx, [(None, at(ao))])

    def head_grads(i):
        g = dot(ga_all[i], wo_all[...].reshape(QW, D), NT, BF)
        gatt[i] = g
        both = g.astype(F32) * heads[i]
        for h in range(2):
            delta[h, pl.ds(pl.multiple_of(i * T, T), T)] = jnp.sum(
                both[:, HD * h : HD * (h + 1)], -1, keepdims=True
            )

    def attend_back(h, n, fresh):
        here = slice(2 * n, 2 * n + 2)
        mine = slice(HD * h, HD * (h + 1))
        q = qkv[here, :, mine].reshape(256, HD)
        g = gatt[here, :, mine].reshape(256, HD)
        d = delta[h, 256 * n : 256 * (n + 1)]
        gq = None
        for m in range(n + 1):
            k = qkv[2 * m : 2 * m + 2, :, 2 * HD : 3 * HD].reshape(256, HD)
            v = qkv[2 * m : 2 * m + 2, :, 3 * HD :].reshape(256, HD)
            p = probs[h, n * (n + 1) // 2 + m]
            gv = dot(p, g, TN)
            gs = (p.astype(F32) * (dot(g, v, NT) - d)).astype(BF)
            gk = dot(gs, q, TN)
            span = slice(256 * m, 256 * (m + 1))
            if fresh:
                gv_f[span] = gv
                gk_f[span] = gk
            else:
                gv_f[span] += gv
                gk_f[span] += gk
            x = dot(gs, k, NN)
            gq = x if gq is None else gq + x
        turn_back(gq * HD**-0.5, here, mine, 0, fresh)

    def turn_back(g, here, mine, kind, fresh):
        n = g.shape[0]
        cosine = tab[here, :, 0:HD].reshape(n, HD)
        sine = tab[here, :, HD:].reshape(n, HD)
        w = g * cosine - pltpu.roll(g, 64, 1) * sine
        u, inverse = rms_parts(raw[here, :, mine].reshape(n, HD))
        gain = jnp.sum(w * u, 0, keepdims=True)
        place = slice(2 * D + HD * kind, 2 * D + HD * (kind + 1))
        if fresh:
            sm[:, place] = gain
        else:
            sm[:, place] += gain
        r = rms_back(w * ghead[kind : kind + 1], u, inverse).astype(BF)
        gqkv[here, :, mine] = r.reshape(n // T, T, HD)

    def work():
        pl.loop(0, NC)(head_grads)
        loads[1].wait()
        loads[2].wait()
        loads[4].wait()
        loads[5].wait()
        yield
        for n in (3, 2, 1, 0):
            for h in range(2):
                attend_back(h, n, n == 3 and h == 0)
            if n:
                yield
        for m in range(2):
            here = slice(4 * m, 4 * m + 4)
            span = slice(512 * m, 512 * (m + 1))
            turn_back(gk_f[span] * HD**-0.5, here, slice(2 * HD, 3 * HD), 1, m == 0)
            gqkv[here, :, 3 * HD :] = gv_f[span].astype(BF).reshape(4, T, HD)
        loads[6].wait()
        loads[7].wait()

        @pl.loop(0, NC)
        def _(i):
            part[i] = dot(gqkv[i], w1_all[:, :, 0:512].reshape(D, 512), NT, BF)

    loads[0].wait()
    main = work()
    rest = drive(
        *each(feed_forward, lb, sb), out_grad(), feed_forward_grads(), main,
        until=main,
    )

    def got_input(h):
        def got(k, total):
            normed, inverse = rms_parts(tok[rows(h)].astype(F32))
            g = jnp.sum(total * normed, 0, keepdims=True)
            if h == 0:
                sm[:, 0:D] = g
            else:
                sm[:, 0:D] += g
            gx_ref[rows(h)] = gres_ref[rows(h)] + rms_back(total * gvec[0:1], normed, inverse)

        return got

    def by_ctx(h, land, sums):
        yield from reduce(net, ctx, [(chunk(part, h), CPARTS, land, sums)], got_input(h))

    def small():
        yield
        yield
        yield
        yield
        sm[:, D : 2 * D] = ggain[...]
        smc[c] = sm[...]
        sent = [net.send(sm, smc.at[c], d) for d in ctx_peers]
        yield
        for x in sent:
            x.wait()
        total = smc[0]
        for i in range(1, NC):
            total = total + smc[i]
        sm2[...] = total
        sms[s] = total
        sent = [net.send(sm2, sms.at[s], d) for d in shard_peers]
        yield
        for x in sent:
            x.wait()
        total = sms[0]
        for i in range(1, NS):
            total = total + sms[i]
        small_ref[...] = total

    def got_shard(k, total):
        s1[...] = total.astype(BF)

    def grads():
        @pl.loop(0, 8)
        def _(j):
            left = hid[:, :, pl.ds(pl.multiple_of(j * 128, 128), 128)].reshape(SEQ, 128)
            g = dot(left, gqkv[...].reshape(SEQ, 512), TN, BF)
            gw1[0, j] = g[0:64]
            gw1[1, j] = g[64:128]

        yield from reduce_shard(
            net, chips, core, sibling, [(gw1, h1, b1, l1)], got_shard
        )
        yield from gather_peers(net, ctx, [(s1, at(a1))])

    last = grads()
    tokens = each(by_ctx, la, sa)
    drive(*tokens, last, *rest, small())


def assemble_body(
    out_h, gx_h, a1_h, ao_h, a2_h, ad_h,
    out_ref, gx_ref, q_out, k_out, v_out, o_out, gate_out, up_out, down_out,
    a1, ao, a2, ad, sem,
):
    pairs = ((a2_h, a2), (a1_h, a1), (ao_h, ao), (ad_h, ad), (out_h, out_ref), (gx_h, gx_ref))
    loads = [pltpu.make_async_copy(x, y, sem.at[k]) for k, (x, y) in enumerate(pairs)]
    for x in loads:
        x.start()
    loads[0].wait()
    for i in range(NC):
        gate_out[:, FW * i : FW * (i + 1)] = a2[i, :, 0:FW].astype(F32)
        up_out[:, FW * i : FW * (i + 1)] = a2[i, :, FW : 2 * FW].astype(F32)
    for x in loads[1:]:
        x.wait()
    for i in range(NC):
        q_out[:, QW * i : QW * (i + 1)] = a1[i, :, 0:QW].astype(F32)
        k_out[:, HD * i : HD * (i + 1)] = a1[i, :, QW : QW + HD].astype(F32)
        v_out[:, HD * i : HD * (i + 1)] = a1[i, :, QW + HD :].astype(F32)
        o_out[16 * i : 16 * (i + 1), :] = ao[i].astype(F32)
        down_out[24 * i : 24 * (i + 1), :] = ad[i].astype(F32)


def shards(
    tokens, positions, attn_gain, query_weight, key_matrix, value_matrix, query_gain, key_gain,
    out_weight, mlp_gain, gate_weight, up_weight, down_weight, cotangent,
):
    c = lax.axis_index("ctx")
    s = lax.axis_index("shard")
    tok, cot = tokens[0], cotangent[0]

    row0 = jnp.concatenate([attn_gain, mlp_gain])[None]
    row1 = jnp.concatenate([query_gain, key_gain, jnp.zeros((112,), BF)])[None]
    gains = jnp.concatenate([row0, row1, jnp.zeros((62, 128), BF)], 0)
    wo = out_weight.reshape(8, 16, D)
    wd = down_weight.reshape(8, 24, D)

    freq = np.power(ROPE_BASE, -np.arange(HD // 2) * (2.0 / HD)).astype(np.float32)
    freq = np.concatenate([freq, freq])[:, None]

    (
        g_all, w1_all, wo_all, w2_all, wd_all, hid, raw, qkv, tab, probs, heads, out_part, gvec, ghead,
    ) = remote_call(
        start_body,
        [
            ((NC, T, D), BF, "h"), ((NS, 64, WCOL1), BF, "v"), ((NS, 16, D), BF, "v"),
            ((NS, 64, WCOL2), BF, "h"), ((NS, 24, D), BF, "h"),
            ((NC, T, D), BF, "h"), ((NC, T, 512), F32, "h"), ((NC, T, 512), BF, "h"),
            ((NC, T, 2 * HD), F32, "h"), ((2, 10, 256, 256), BF, "h"), ((NC, T, QW), F32, "h"),
            ((NC, T, D), BF, "v"), ((2, D), F32, "v"), ((2, HD), F32, "v"),
        ],
        "h" * 11 + "v",
        (
            tok, cot, positions, query_weight, key_matrix, value_matrix, gate_weight, up_weight,
            gains, wo, wd, freq,
        ),
        [
            pltpu.VMEM((NC, T, D), BF), pltpu.VMEM((NC, 1, T), jnp.int32),
            pltpu.VMEM((64, WCOL1), BF), pltpu.VMEM((64, WCOL2), BF),
            pltpu.VMEM((64, WCOL1), BF), pltpu.VMEM((64, WCOL2), BF),
            pltpu.VMEM((NC, T, D), BF), pltpu.VMEM((NC, T, 512), F32),
            pltpu.VMEM((NC, T, 512), BF), pltpu.VMEM((NC, T, 2 * HD), F32),
            pltpu.VMEM((2, 10, 256, 256), BF), pltpu.VMEM((NC, T, QW), F32),
        ],
        224, 32, 0, 58 << 20,
    )
    ga_all, grad_resid, ggain_mlp, gw2, gwd, down_part, resid = remote_call(
        mid_body,
        [
            ((NC, T, D), BF, "h"), ((T, D), F32, "v"), ((1, D), F32, "v"),
            ((2, 8, 64, WCOL2), BF, "h"), ((2, 8, 24, D), BF, "h"),
            ((NC, T, D), BF, "h"), ((T, D), F32, "v"),
        ],
        "vvvvhhh",
        (out_part, tok, cot, gvec, w2_all.reshape(D, 2 * FW), wd_all.reshape(FW, D), g_all),
        [
            pltpu.VMEM((D, 2 * FW), BF), pltpu.VMEM((FW, D), BF), pltpu.VMEM((NC, T, D), BF),
            pltpu.VMEM((NC, T, D), BF), pltpu.VMEM((2, 8, 64, WCOL2), BF),
            pltpu.VMEM((2, 8, 24, D), BF),
            pltpu.VMEM((NC, T, D), BF), pltpu.VMEM((NC, T, FW), BF), pltpu.VMEM((NC, T, 2 * FW), BF),
            pltpu.VMEM((NC, T, D), BF), pltpu.VMEM((T, D), BF), pltpu.VMEM((FW, D), F32),
        ]
        + chunk_scratch() * 2,
        192, 16, 1, 58 << 20,
    )
    output, gx, small, a1, ao, a2, ad = remote_call(
        end_body,
        [
            ((T, D), BF, "v"), ((T, D), F32, "v"), ((1, SMALL), F32, "v"),
            ((NC, 64, 512), BF, "v"), ((NC, 16, D), BF, "v"),
            ((NC, 64, WCOL2), BF, "v"), ((NC, 24, D), BF, "v"),
        ],
        "v" * 8 + "h" * 10,
        (
            ga_all, tok, grad_resid, resid, gvec, ghead, ggain_mlp, wo_all, gw2, gwd,
            down_part, qkv, probs, heads, raw, tab, hid, w1_all,
        ),
        [
            pltpu.VMEM((NC, T, D), BF), pltpu.VMEM((NC, T, 512), BF),
            pltpu.VMEM((2, 10, 256, 256), BF),
            pltpu.VMEM((NC, T, QW), F32), pltpu.VMEM((NC, T, 512), F32),
            pltpu.VMEM((NC, T, 2 * HD), F32), pltpu.VMEM((NC, T, D), BF),
            pltpu.VMEM((NS, 64, WCOL1), BF),
            pltpu.VMEM((2, 8, 64, WCOL2), BF), pltpu.VMEM((2, 8, 24, D), BF),
            pltpu.VMEM((NC, T, QW), BF), pltpu.VMEM((2, SEQ, 1), F32), pltpu.VMEM((QW, D), F32),
            pltpu.VMEM((SEQ, HD), F32), pltpu.VMEM((SEQ, HD), F32), pltpu.VMEM((NC, T, 512), BF),
            pltpu.VMEM((NC, T, D), BF), pltpu.VMEM((2, 8, 64, 512), BF),
            pltpu.VMEM((2, 8, 16, D), BF),
        ]
        + chunk_scratch() * 2 + shard_scratch((64, 512)) + shard_scratch((16, D))
        + shard_scratch((64, WCOL2)) + shard_scratch((24, D))
        + [
            pltpu.VMEM((64, 512), BF), pltpu.VMEM((16, D), BF),
            pltpu.VMEM((64, WCOL2), BF), pltpu.VMEM((24, D), BF), pltpu.VMEM((24, D), BF),
            pltpu.VMEM((1, SMALL), F32), pltpu.VMEM((NC, 1, SMALL), F32),
            pltpu.VMEM((1, SMALL), F32), pltpu.VMEM((NS, 1, SMALL), F32),
        ],
        224, 32, 2, 58 << 20,
    )
    any_, whole = pl.BlockSpec(memory_space=pl.ANY), pl.BlockSpec(memory_space=pltpu.VMEM)
    output, gx, gwq, gwk, gwv, gwo_out, gwg, gwu, gwd_out = pl.pallas_call(
        assemble_body,
        out_shape=[
            jax.ShapeDtypeStruct((T, D), BF), jax.ShapeDtypeStruct((T, D), F32),
            jax.ShapeDtypeStruct((64, 2048), F32), jax.ShapeDtypeStruct((64, 1024), F32),
            jax.ShapeDtypeStruct((64, 1024), F32), jax.ShapeDtypeStruct((128, D), F32),
            jax.ShapeDtypeStruct((64, 3072), F32), jax.ShapeDtypeStruct((64, 3072), F32),
            jax.ShapeDtypeStruct((192, D), F32),
        ],
        in_specs=[any_] * 6,
        out_specs=[whole] * 9,
        scratch_shapes=[
            pltpu.VMEM((NC, 64, 512), BF), pltpu.VMEM((NC, 16, D), BF),
            pltpu.VMEM((NC, 64, WCOL2), BF), pltpu.VMEM((NC, 24, D), BF),
            pltpu.SemaphoreType.DMA((6,)),
        ],
        compiler_params=pltpu.CompilerParams(vmem_limit_bytes=58 << 20),
    )(output, gx, a1, ao, a2, ad)
    small = small[0]

    def own(offset, width):
        return lax.dynamic_slice(small, (offset + s * width,), (width,))

    return (
        output[None], gx[None], own(0, 64), gwq, gwk, gwv, own(2 * D, 8), own(2 * D + HD, 8),
        gwo_out, own(D, 64), gwg, gwu, gwd_out,
    )


def solution(mesh):
    split = P("shard", "ctx", None)
    rows, vec = P("shard", None), P("shard")
    in_specs = (
        split, P("shard", "ctx"), vec, rows, rows, rows, vec, vec, rows, vec, rows, rows, rows, split,
    )
    out_specs = (split, split, vec, rows, rows, rows, vec, vec, rows, vec, rows, rows, rows)
    return jax.shard_map(shards, mesh=mesh, in_specs=in_specs, out_specs=out_specs, check_vma=False)
```

```python
import jax
import jax.numpy as jnp
import numpy as np
from jax import lax
from jax.experimental import pallas as pl
from jax.experimental.pallas import tpu as pltpu
from jax.sharding import PartitionSpec as P

MESH = pl.DeviceIdType.MESH
BF = jnp.bfloat16
F32 = jnp.float32

NS = 16
NC = 8
T = 128
SEQ = 1024
D = 1024
HD = 128
QW = 256
FW = 384
EPSILON = 1e-06
ROPE_BASE = 1000000.0
BLOCKED_SCORE = -1e30
SMALL = 2304

ALL = slice(None)


def lanes(width):
    a = (width // 128 + 1) // 2 * 128
    return ((ALL, slice(0, a)), (ALL, slice(a, width)), None)


def view(ref, part):
    return ref.at[tuple(pl.ds(p.start, p.stop - p.start) if p != ALL else p for p in part)]


class Ring:
    def __init__(self, me, device):
        self.a = me // 2
        self.b = lax.rem(me, 2)
        self.device = device

    def idx(self, da, db):
        return lax.rem(self.a + da + 4, 4) * 2 + lax.rem(self.b + db, 2)

    def dev(self, da, db):
        return self.device(self.idx(da, db))


class Net:
    def __init__(self, send, recv, local):
        self.s, self.r, self.l = send, recv, local
        self.n = 0
        self.m = 0

    def send(self, src, dst, to):
        k = self.n
        self.n += 1
        c = pltpu.make_async_remote_copy(
            src_ref=src, dst_ref=dst, send_sem=self.s.at[k], recv_sem=self.r.at[k],
            device_id=to, device_id_type=MESH,
        )
        c.start()
        return c

    def copy(self, src, dst):
        k = self.m
        self.m += 1
        c = pltpu.make_async_copy(src, dst, self.l.at[k])
        c.start()
        return c


def places():
    s = lax.axis_index("shard")
    c = lax.axis_index("ctx")
    core = lax.rem(s, 2)
    ctx = Ring(c, lambda i: (s, i))
    chips = Ring(s // 2, lambda i: (i * 2 + core, c))
    sibling = (s + 1 - 2 * core, c)
    half, rest = lax.rem(s, 2), s // 2
    goes = (8 * half + c, rest)
    comes = (2 * c + s // 8, lax.rem(s, 8))
    stays = jnp.logical_and(goes[0] == s, goes[1] == c)
    return s, c, core, ctx, chips, sibling, goes, comes, stays


def ring_devices(ring):
    return [ring.dev(-1, 0), ring.dev(1, 0), ring.dev(0, 1)]


def greet(devices, moved=None):
    barrier = pltpu.get_barrier_semaphore()
    for d in devices:
        pl.semaphore_signal(barrier, inc=1, device_id=d, device_id_type=MESH)
    if moved is not None:
        goes, comes, stays = moved

        @pl.when(jnp.logical_not(stays))
        def _():
            for d in (goes, comes):
                pl.semaphore_signal(barrier, inc=1, device_id=d, device_id_type=MESH)
            pl.semaphore_wait(barrier, len(devices) + 2)

        @pl.when(stays)
        def _():
            pl.semaphore_wait(barrier, len(devices))

    else:
        pl.semaphore_wait(barrier, len(devices))


def drive(*threads, until=None):
    threads = list(threads)
    ended = set()
    while threads:
        for x in list(threads):
            if id(x) in ended:
                continue
            try:
                next(x)
            except StopIteration:
                ended.add(id(x))
        threads = [x for x in threads if id(x) not in ended]
        if until is not None and id(until) in ended:
            break
    return threads


def move(net, items, to, stays):
    base = net.n
    net.n += len(items)

    def remote(k, src, dst):
        return pltpu.make_async_remote_copy(
            src_ref=src, dst_ref=dst, send_sem=net.s.at[base + k], recv_sem=net.r.at[base + k],
            device_id=to, device_id_type=MESH,
        )

    @pl.when(jnp.logical_not(stays))
    def _():
        for k, (src, dst) in enumerate(items):
            remote(k, src, dst).start()

    @pl.when(stays)
    def _():
        for k, (src, dst) in enumerate(items):
            pltpu.make_async_copy(src, dst, net.r.at[base + k]).start()

    yield

    @pl.when(jnp.logical_not(stays))
    def _():
        for k, (src, dst) in enumerate(items):
            remote(k, src, dst).wait()

    @pl.when(stays)
    def _():
        for k, (src, dst) in enumerate(items):
            pltpu.make_async_copy(src, dst, net.r.at[base + k]).wait()


def gather(net, ring, items, slot=lambda i: i, sibling=None):
    left, right, pair = ring_devices(ring)
    me = ring.idx(0, 0)
    over = []

    def pass_on(places):
        if sibling is not None:
            for _, at, _ in items:
                for i in places:
                    over.append(net.send(at(slot(i)), at(slot(i)), sibling))

    first, local = [], []
    for own, at, _ in items:
        here = at(slot(me))
        src = here if own is None else own
        for n in (left, right, pair):
            first.append(net.send(src, here, n))
        if sibling is not None:
            over.append(net.send(src, here, sibling))
        if own is not None:
            local.append(net.copy(own, here))
    yield
    for c in first:
        c.wait_recv()
    second = []
    a, b, z = ring.idx(-1, 0), ring.idx(1, 0), ring.idx(0, 1)
    for _, at, _ in items:
        for i, n in ((a, right), (z, left), (a, pair)):
            second.append(net.send(at(slot(i)), at(slot(i)), n))
    pass_on((a, b, z))
    yield
    for c in second:
        c.wait_recv()
    third = []
    az, bz, o, oz = ring.idx(-1, 1), ring.idx(1, 1), ring.idx(2, 0), ring.idx(2, 1)
    for _, at, parts in items:
        for i, n, part in ((az, right, parts[0]), (bz, left, parts[1]), (o, pair, parts[2])):
            if part is not None:
                r = view(at(slot(i)), part)
                third.append(net.send(r, r, n))
    pass_on((az, bz, o))
    yield
    for c in third:
        c.wait_recv()
    pass_on((oz,))
    for c in local:
        c.wait()
    for c in first + second + third:
        c.wait_send()
    if sibling is not None:
        yield
        for c in over:
            c.wait()


def gather_shard(net, ring, slot, across, sibling, items):
    me, z = ring.idx(0, 0), ring.idx(0, 1)
    over, local, first = [], [], []

    def pass_on(at, *places):
        for i in places:
            over.append(net.send(at(slot(i)), at(slot(i)), sibling))

    for own, other, at in items:
        for i in (me, z) if own is None else (me,):
            here = at(slot(i))
            src = here if own is None else own
            for d in (1, 3, 2):
                first.append(net.send(src, here, ring.dev(d, 0)))
            over.append(net.send(src, here, sibling))
        if own is not None:
            for d in across:
                first.append(net.send(other, here, d))
            local.append(net.copy(own, here))
    yield
    yield
    for c in first:
        c.wait_recv()
    for own, _, at in items:
        for d in (1, 3, 2):
            pass_on(at, ring.idx(d, 0), ring.idx(d, 1))
        if own is not None:
            pass_on(at, z)
    for c in local:
        c.wait()
    yield
    for c in first:
        c.wait_send()
    for c in over:
        c.wait()


def reduce(net, ring, items, result):
    left, right, pair = ring_devices(ring)
    me, a, b, z = ring.idx(0, 0), ring.idx(-1, 0), ring.idx(1, 0), ring.idx(0, 1)
    az, bz, o, oz = ring.idx(-1, 1), ring.idx(1, 1), ring.idx(2, 0), ring.idx(2, 1)

    def plus(x, y):
        return (x.astype(F32) + y.astype(F32)).astype(BF)

    first, second, third = [], [], []
    for p, parts, land, _ in items:
        for n, part in zip((left, right, pair), parts):
            if part is None:
                continue
            first.append(net.send(view(p(oz), part), view(land.at[0], part), n))
    yield
    for c in first:
        c.wait_recv()
    for p, parts, land, sums in items:
        for k, (i, part, n) in enumerate(
            ((o, parts[2], left), (bz, parts[1], right), (az, parts[0], pair))
        ):
            if part is None:
                second.append(net.send(p(i), land.at[1 + k], n))
                continue
            sums[k] = p(i)[...]
            sums[(k,) + part] = plus(p(i)[part], land[(0,) + part])
            second.append(net.send(sums.at[k], land.at[1 + k], n))
    yield
    for c in second:
        c.wait_recv()
    for p, parts, land, sums in items:
        third.append(net.send(p(b), land.at[5], right))
        sums[4] = plus(p(z)[...], land[2])
        third.append(net.send(sums.at[4], land.at[6], pair))
        sums[3] = (p(a)[...].astype(F32) + land[1].astype(F32) + land[3].astype(F32)).astype(BF)
        third.append(net.send(sums.at[3], land.at[4], left))
    yield
    for c in third:
        c.wait_recv()
    for k, (p, parts, land, sums) in enumerate(items):
        result(
            k,
            (p(me)[...].astype(F32) + land[4].astype(F32))
            + (land[5].astype(F32) + land[6].astype(F32)),
        )
    for c in first + second + third:
        c.wait_send()


def at(ref):
    return lambda i: ref.at[i]


CHUNKS = 4
CROWS = T // CHUNKS
CPARTS = ((slice(0, CROWS // 2), ALL), (slice(CROWS // 2, CROWS), ALL), None)


def rows(h):
    return pl.ds(CROWS * h, CROWS)


def chunk(ref, h):
    return lambda i: ref.at[i, rows(h)]


def each(thread, land, sums):
    return [thread(h, land.at[:, rows(h)], sums.at[:, rows(h)]) for h in range(CHUNKS)]


def chunk_scratch():
    return [pltpu.VMEM((7, T, D), BF), pltpu.VMEM((5, T, D), BF)]


def reduce_scratch(shape):
    return [pltpu.VMEM((7,) + shape, BF), pltpu.VMEM((5,) + shape, BF)]


def reduce_shard(net, chips, core, sibling, items, result):
    over = []
    for p, _, half, _, _, _ in items:
        over.append(net.send(p.at[1 - core], half, sibling))
    yield
    for c in over:
        c.wait_recv()
    for p, _, half, both, _, _ in items:

        @pl.loop(0, 8)
        def _(j):
            both[j] = (p[core, j].astype(F32) + half[j].astype(F32)).astype(BF)

    yield from reduce(net, chips, [(at(i[3]), i[1], i[4], i[5]) for i in items], result)
    for c in over:
        c.wait_send()


def shard_scratch(shape):
    return [pltpu.VMEM((8,) + shape, BF), pltpu.VMEM((8,) + shape, BF)] + reduce_scratch(shape)


def rms_parts(v):
    inverse = lax.rsqrt(jnp.mean(v * v, -1, keepdims=True) + EPSILON)
    return v * inverse, inverse


def rms_back(g, n, inverse):
    return inverse * (g - n * jnp.mean(g * n, -1, keepdims=True))


def dot(a, b, dims, out=F32):
    return lax.dot_general(a, b, (dims, ((), ())), preferred_element_type=F32).astype(out)


NN = ((1,), (0,))
NT = ((1,), (1,))
TN = ((0,), (0,))


def remote_call(body, outs, ins, args, scratch, copies, locals_, number, vmem=None):
    sems = [
        pltpu.SemaphoreType.DMA((copies,)),
        pltpu.SemaphoreType.DMA((copies,)),
        pltpu.SemaphoreType.DMA((locals_,)),
    ]
    space = {"v": pl.BlockSpec(memory_space=pltpu.VMEM), "h": pl.BlockSpec(memory_space=pl.ANY)}
    return pl.pallas_call(
        body,
        out_shape=[jax.ShapeDtypeStruct(s, d) for s, d, _ in outs],
        in_specs=[space[k] for k in ins],
        out_specs=[space[k] for _, _, k in outs],
        scratch_shapes=list(scratch) + sems,
        compiler_params=pltpu.CompilerParams(
            collective_id=number, has_side_effects=True, vmem_limit_bytes=vmem
        ),
    )(*args)


WCOL1 = 640
WCOL2 = 768


def start_body(
    tok, cot, pos, wq, wk, wv, wg, wu, gblock, wo, wd, freq,
    g_all, w1_all, wo_all, w2_all, wd_all, hid_h, raw_h, qkv_h, tab_h, probs_h, heads_h, part, gvec, ghead,
    x_all, p_all, w1, w2, v1, v2, hid, raw, qkv, tab, probs, heads, ss, rs, ls,
):
    s, c, core, ctx, chips, sibling, goes, comes, stays = places()
    net = Net(ss, rs, ls)

    other = c + 1 - 2 * lax.rem(c, 2)
    flip = s + 2 - 4 * lax.rem(s // 2, 2)
    across = [((lax.rem(s // 4 + d, 4)) * 4 + lax.rem(flip, 4), other) for d in (0, 1, 3, 2)]
    goes_z = (goes[0] + 2 - 4 * lax.rem(goes[0] // 2, 2), goes[1])
    comes_z = (2 * c + flip // 8, lax.rem(flip, 8))

    def cut(w, width, i):
        return w.at[:, pl.ds(pl.multiple_of(i * width, 128), width)]

    loads = [
        net.copy(x, y)
        for i, one, two in ((c, w1, w2), (other, v1, v2))
        for x, y in (
            (cut(wq, QW, i), one.at[:, 0:QW]), (cut(wk, HD, i), one.at[:, QW : QW + HD]),
            (cut(wv, HD, i), one.at[:, QW + HD : 512]), (gblock, one.at[:, 512:WCOL1]),
            (cut(wg, FW, i), two.at[:, 0:FW]), (cut(wu, FW, i), two.at[:, FW : 2 * FW]),
        )
    ]
    greet(
        ring_devices(ctx) + [chips.dev(d, 0) for d in (1, 2, 3)] + across + [sibling, goes_z, comes_z],
        (goes, comes, stays),
    )
    for x in loads:
        x.wait()

    def place(i):
        return i * 2 + core

    def weights():
        yield from gather_shard(
            net, chips, place, across, sibling, [(w1, v1, at(w1_all))]
        )
        yield from gather_shard(
            net, chips, place, across, sibling,
            [
                (w2, v2, at(w2_all)), (None, None, at(wd_all)), (None, None, at(wo_all)),
            ],
        )

    def moved():
        moved = [(wo.at[c], wo_all.at[goes[0]]), (wd.at[c], wd_all.at[goes[0]])]
        second = [net.send(x, y, goes_z) for x, y in moved]
        yield from move(net, moved, goes, stays)
        for x in second:
            x.wait()

    def by_ctx(h):
        items = [(tok.at[rows(h)], chunk(x_all, h), CPARTS)]
        if h == 0:
            items.append((pos, at(p_all), ((ALL, ALL), None, None)))
        yield from gather(net, ctx, items)
        yield from gather(net, ctx, [(cot.at[rows(h)], chunk(g_all, h), CPARTS)])

    def gains():
        lane = lax.broadcasted_iota(jnp.int32, (8, 128), 1)
        t = [w1_all[i, 0:16, 512:640].astype(F32)[0:8] for i in range(NS)]
        for j in range(8):
            x, y = t[2 * j], t[2 * j + 1]
            low = lane < 64
            gvec[0:1, 128 * j : 128 * (j + 1)] = jnp.where(low, x, pltpu.roll(y, 64, 1))[0:1]
            gvec[1:2, 128 * j : 128 * (j + 1)] = jnp.where(low, pltpu.roll(x, 64, 1), y)[0:1]
        q = jnp.zeros((8, 128), F32)
        k = jnp.zeros((8, 128), F32)
        for i in range(NS):
            here = lane // 8 == i
            q = jnp.where(here, pltpu.roll(t[i], 8 * i, 1), q)
            k = jnp.where(here, pltpu.roll(t[i], (8 * i + 120) % 128, 1), k)
        ghead[0:1] = q[1:2]
        ghead[1:2] = k[1:2]

    def project(i):
        normed, _ = rms_parts(x_all[i].astype(F32))
        h = (normed * gvec[0:1]).astype(BF)
        hid[i] = h
        r = dot(h, w1_all[:, :, 0:512].reshape(D, 512), NN)
        raw[i] = r
        angle = freq[...] * p_all[i].astype(F32)
        cosine = jnp.cos(angle).T
        sine = jnp.sin(angle).T
        sine = jnp.where(lax.broadcasted_iota(jnp.int32, (T, HD), 1) < HD // 2, -sine, sine)
        tab[i, :, 0:HD] = cosine
        tab[i, :, HD:] = sine
        for k in range(3):
            n, _ = rms_parts(r[:, HD * k : HD * (k + 1)])
            u = n * ghead[k // 2 : k // 2 + 1]
            qkv[i, :, HD * k : HD * (k + 1)] = (u * cosine + pltpu.roll(u, 64, 1) * sine).astype(BF)
        qkv[i, :, 3 * HD :] = r[:, 3 * HD :].astype(BF)

    def attend(h, n):
        width = 256 * (n + 1)
        q = qkv[2 * n : 2 * n + 2, :, HD * h : HD * (h + 1)].reshape(256, HD)
        k = qkv[0 : 2 * n + 2, :, 2 * HD : 3 * HD].reshape(width, HD)
        v = qkv[0 : 2 * n + 2, :, 3 * HD :].reshape(width, HD)
        score = dot(q, k, NT) * HD**-0.5
        row = lax.broadcasted_iota(jnp.int32, (256, width), 0) + 256 * n
        col = lax.broadcasted_iota(jnp.int32, (256, width), 1)
        score = jnp.where(col <= row, score, BLOCKED_SCORE)
        top = jnp.max(score, -1, keepdims=True)
        e = jnp.exp(score - top)
        total = jnp.sum(e, -1, keepdims=True)
        share = 1.0 / total
        o = dot(e.astype(BF), v, NN) * share
        e = e * share
        for m in range(n + 1):
            probs[h, n * (n + 1) // 2 + m] = e[:, 256 * m : 256 * (m + 1)].astype(BF).T
        heads[2 * n : 2 * n + 2, :, HD * h : HD * (h + 1)] = o.reshape(2, T, HD)

    def work():
        yield
        yield
        yield
        gains()
        pl.loop(0, 4)(project)
        yield
        pl.loop(4, 8)(project)
        for x, y in ((hid, hid_h), (raw, raw_h), (qkv, qkv_h), (tab, tab_h)):
            stores.append(net.copy(x, y))
        for h in range(2):
            attend(h, 0)
        yield
        for n in range(1, 4):
            for h in range(2):
                attend(h, n)
            if n < 3:
                yield
        stores.append(net.copy(heads, heads_h))
        stores.append(net.copy(probs, probs_h))

        @pl.loop(0, NC)
        def _(i):
            part[i] = dot(heads[i].astype(BF), wo_all[...].reshape(QW, D), NN, BF)

    stores = []
    side = weights()
    drive(side, *[by_ctx(h) for h in range(CHUNKS)], moved(), work())
    for x in stores:
        x.wait()


def mid_body(
    part, tok, cot, gvec, wgu_h, wd_h, g_h,
    ga_all, gres_ref, ggain_ref, gw2_h, gwd_h, down_h, resid,
    wgu, wd, g_all, down_part, gw2, gwd, h_all, mixed, ggu, back_part, ga, gwd_f,
    la, sa, lb, sb, ss, rs, ls,
):
    s, c, core, ctx, chips, sibling, goes, comes, stays = places()
    net = Net(ss, rs, ls)
    loads = [net.copy(x, y) for x, y in ((wgu_h, wgu), (wd_h, wd), (g_h, g_all))]
    stores = []
    greet(ring_devices(ctx))

    def forward(h, land, sums):
        def got(k, total):
            r = tok[rows(h)].astype(F32) + total
            resid[rows(h)] = r
            normed, _ = rms_parts(r)
            h_all[c, rows(h)] = (normed * gvec[1:2]).astype(BF)

        yield from reduce(net, ctx, [(chunk(part, h), CPARTS, land, sums)], got)
        yield from gather(net, ctx, [(None, chunk(h_all, h), CPARTS)])

    def block(i):
        both = dot(h_all[i], wgu[...], NN)
        gate, up = both[:, :FW], both[:, FW:]
        sig = jax.nn.sigmoid(gate)
        act = gate * sig
        m = (act * up).astype(BF)
        mixed[i] = m
        gm = dot(g_all[i], wd[...], NT)
        gg = (gm * up * sig * (1.0 + gate * (1.0 - sig))).astype(BF)
        gu = (gm * act).astype(BF)
        ggu[i, :, 0:FW] = gg
        ggu[i, :, FW:] = gu
        back_part[i] = dot(jnp.concatenate([gg, gu], 1), wgu[...], NT, BF)
        down_part[i] = dot(m, wd[...], NN, BF)

    def blocks(places):
        n = len(places)

        @pl.loop(0, n)
        def _(j):
            i = places[0]
            for k in range(1, n):
                i = jnp.where(j == k, places[k], i)
            block(i)

    def work():
        yield
        yield
        yield
        for x in loads:
            x.wait()
        blocks([c])
        yield
        blocks([ctx.idx(-1, 0), ctx.idx(1, 0), ctx.idx(0, 1)])
        yield
        blocks([ctx.idx(-1, 1), ctx.idx(1, 1), ctx.idx(2, 0)])
        yield
        blocks([ctx.idx(2, 1)])

    drive(*each(forward, la, sa), work())
    stores.append(net.copy(down_part, down_h))

    def got_back(h):
        def got(k, total):
            normed, inverse = rms_parts(resid[rows(h)])
            g = jnp.sum(total * normed, 0, keepdims=True)
            if h == 0:
                ggain_ref[...] = g
            else:
                ggain_ref[...] += g
            gres = cot[rows(h)].astype(F32) + rms_back(total * gvec[1:2], normed, inverse)
            gres_ref[rows(h)] = gres
            ga[rows(h)] = gres.astype(BF)

        return got

    def backward(h, land, sums):
        yield from reduce(net, ctx, [(chunk(back_part, h), CPARTS, land, sums)], got_back(h))
        yield from gather(net, ctx, [(ga.at[rows(h)], chunk(ga_all, h), CPARTS)])

    def grads():
        for q in range(2):

            @pl.loop(4 * q, 4 * q + 4)
            def _(j):
                left = h_all[:, :, pl.ds(pl.multiple_of(j * 128, 128), 128)].reshape(SEQ, 128)
                g = dot(left, ggu[...].reshape(SEQ, 2 * FW), TN, BF)
                gw2[0, j] = g[0:64]
                gw2[1, j] = g[64:128]

            yield
        for j in range(3):
            left = mixed[:, :, 128 * j : 128 * (j + 1)].reshape(SEQ, 128)
            gwd_f[128 * j : 128 * (j + 1)] = dot(left, g_all[...].reshape(SEQ, D), TN)
        for i in range(NS):
            gwd[i % 2, i // 2] = gwd_f[24 * i : 24 * (i + 1)].astype(BF)
        stores.append(net.copy(gw2, gw2_h))
        stores.append(net.copy(gwd, gwd_h))

    drive(*each(backward, lb, sb), grads())
    for x in stores:
        x.wait()


def end_body(
    ga_all, tok, gres_ref, resid, gvec, ghead, ggain, wo_all,
    gw2_h, gwd_h, down_h, qkv_h, probs_h, heads_h, raw_h, tab_h, hid_h, w1_h,
    out_ref, gx_ref, small_ref, a1, ao, a2, ad,
    down_part, qkv, probs, heads, raw, tab, hid, w1_all, gw2, gwd,
    gatt, delta, gwo_f, gk_f, gv_f, gqkv, part, gw1, gwo,
    la, sa, lb, sb, h1, b1, l1, t1, h2, b2, l2, t2,
    h3, b3, l3, t3, h4, b4, l4, t4,
    s1, so, gw2_sum, gwd_sum, own_d, sm, smc, sm2, sms, ss, rs, ls,
):
    s, c, core, ctx, chips, sibling, goes, comes, stays = places()
    net = Net(ss, rs, ls)
    loads = [
        net.copy(x, y)
        for x, y in (
            (heads_h, heads), (qkv_h, qkv), (probs_h, probs), (down_h, down_part),
            (raw_h, raw), (tab_h, tab), (hid_h, hid), (w1_h, w1_all), (gw2_h, gw2), (gwd_h, gwd),
        )
    ]
    ctx_peers = [(s, lax.rem(c + d, NC)) for d in range(1, NC)]
    shard_peers = [(lax.rem(s + d, NS), c) for d in range(1, NS)]
    greet(ctx_peers + shard_peers, (goes, comes, stays))

    def feed_forward(h, land, sums):
        def got(k, total):
            out_ref[rows(h)] = (resid[rows(h)] + total).astype(BF)

        if h == 0:
            loads[3].wait()
        yield from reduce(net, ctx, [(chunk(down_part, h), CPARTS, land, sums)], got)

    def got_ff(k, total):
        (gw2_sum, gwd_sum)[k][...] = total.astype(BF)

    def feed_forward_grads():
        loads[8].wait()
        loads[9].wait()
        yield from reduce_shard(
            net, chips, core, sibling,
            [(gw2, lanes(WCOL2), h3, b3, l3, t3), (gwd, lanes(D), h4, b4, l4, t4)], got_ff,
        )
        yield from move(net, [(gwd_sum, own_d)], comes, stays)
        yield from gather(net, ctx, [(gw2_sum, at(a2), lanes(WCOL2)), (own_d, at(ad), lanes(D))])

    def got_out(k, total):
        so[...] = total.astype(BF)

    def out_grad():
        for j in range(2):
            left = heads[:, :, HD * j : HD * (j + 1)].reshape(SEQ, HD).astype(BF)
            gwo_f[HD * j : HD * (j + 1)] = dot(left, ga_all[...].reshape(SEQ, D), TN)
        for i in range(NS):
            gwo[i % 2, i // 2] = gwo_f[16 * i : 16 * (i + 1)].astype(BF)
        yield from reduce_shard(
            net, chips, core, sibling, [(gwo, lanes(D), h2, b2, l2, t2)], got_out
        )
        yield from move(net, [(so, ao.at[comes[1]])], comes, stays)
        yield from gather(net, ctx, [(None, at(ao), lanes(D))])

    def head_grads(i):
        g = dot(ga_all[i], wo_all[...].reshape(QW, D), NT, BF)
        gatt[i] = g
        both = g.astype(F32) * heads[i]
        for h in range(2):
            d = jnp.sum(both[:, HD * h : HD * (h + 1)], -1, keepdims=True)
            delta[h, 0:1, pl.ds(pl.multiple_of(i * T, T), T)] = jnp.broadcast_to(d, (T, T)).T[0:1]

    def attend_back(h, n, fresh):
        here = slice(2 * n, 2 * n + 2)
        mine = slice(HD * h, HD * (h + 1))
        q = qkv[here, :, mine].reshape(256, HD)
        g = gatt[here, :, mine].reshape(256, HD)
        d = delta[h, 0:1, 256 * n : 256 * (n + 1)]
        gq = None
        for m in range(n + 1):
            k = qkv[2 * m : 2 * m + 2, :, 2 * HD : 3 * HD].reshape(256, HD)
            v = qkv[2 * m : 2 * m + 2, :, 3 * HD :].reshape(256, HD)
            p = probs[h, n * (n + 1) // 2 + m]
            gv = dot(p, g, NN)
            gs = (p.astype(F32) * (dot(v, g, NT) - d)).astype(BF)
            gk = dot(gs, q, NN)
            span = slice(256 * m, 256 * (m + 1))
            if fresh:
                gv_f[span] = gv
                gk_f[span] = gk
            else:
                gv_f[span] += gv
                gk_f[span] += gk
            x = dot(gs, k, TN)
            gq = x if gq is None else gq + x
        turn_back(gq * HD**-0.5, here, mine, 0, fresh)

    def turn_back(g, here, mine, kind, fresh):
        n = g.shape[0]
        cosine = tab[here, :, 0:HD].reshape(n, HD)
        sine = tab[here, :, HD:].reshape(n, HD)
        w = g * cosine - pltpu.roll(g, 64, 1) * sine
        u, inverse = rms_parts(raw[here, :, mine].reshape(n, HD))
        gain = jnp.sum(w * u, 0, keepdims=True)
        place = slice(2 * D + HD * kind, 2 * D + HD * (kind + 1))
        if fresh:
            sm[:, place] = gain
        else:
            sm[:, place] += gain
        r = rms_back(w * ghead[kind : kind + 1], u, inverse).astype(BF)
        gqkv[here, :, mine] = r.reshape(n // T, T, HD)

    def work():
        pl.loop(0, NC)(head_grads)
        loads[1].wait()
        loads[2].wait()
        loads[4].wait()
        loads[5].wait()
        yield
        for n in (3, 2, 1, 0):
            for h in range(2):
                attend_back(h, n, n == 3 and h == 0)
            if n:
                yield
        for m in range(2):
            here = slice(4 * m, 4 * m + 4)
            span = slice(512 * m, 512 * (m + 1))
            turn_back(gk_f[span] * HD**-0.5, here, slice(2 * HD, 3 * HD), 1, m == 0)
            gqkv[here, :, 3 * HD :] = gv_f[span].astype(BF).reshape(4, T, HD)
        loads[6].wait()
        loads[7].wait()

        @pl.loop(0, NC)
        def _(i):
            part[i] = dot(gqkv[i], w1_all[:, :, 0:512].reshape(D, 512), NT, BF)

    loads[0].wait()
    main = work()
    rest = drive(
        *each(feed_forward, lb, sb), out_grad(), feed_forward_grads(), main,
        until=main,
    )

    def got_input(h):
        def got(k, total):
            normed, inverse = rms_parts(tok[rows(h)].astype(F32))
            g = jnp.sum(total * normed, 0, keepdims=True)
            if h == 0:
                sm[:, 0:D] = g
            else:
                sm[:, 0:D] += g
            gx_ref[rows(h)] = gres_ref[rows(h)] + rms_back(total * gvec[0:1], normed, inverse)

        return got

    def by_ctx(h, land, sums):
        yield from reduce(net, ctx, [(chunk(part, h), CPARTS, land, sums)], got_input(h))

    def small():
        yield
        yield
        yield
        yield
        sm[:, D : 2 * D] = ggain[...]
        smc[c] = sm[...]
        sent = [net.send(sm, smc.at[c], d) for d in ctx_peers]
        yield
        for x in sent:
            x.wait()
        total = smc[0]
        for i in range(1, NC):
            total = total + smc[i]
        sm2[...] = total
        sms[s] = total
        sent = [net.send(sm2, sms.at[s], d) for d in shard_peers]
        yield
        for x in sent:
            x.wait()
        total = sms[0]
        for i in range(1, NS):
            total = total + sms[i]
        small_ref[...] = total

    def got_shard(k, total):
        s1[...] = total.astype(BF)

    def grads():
        @pl.loop(0, 8)
        def _(j):
            left = hid[:, :, pl.ds(pl.multiple_of(j * 128, 128), 128)].reshape(SEQ, 128)
            g = dot(left, gqkv[...].reshape(SEQ, 512), TN, BF)
            gw1[0, j] = g[0:64]
            gw1[1, j] = g[64:128]

        yield from reduce_shard(
            net, chips, core, sibling, [(gw1, lanes(512), h1, b1, l1, t1)], got_shard
        )
        yield from gather(net, ctx, [(s1, at(a1), lanes(512))])

    last = grads()
    tokens = each(by_ctx, la, sa)
    drive(*tokens[:2], last, *tokens[2:], last, *rest, small())


def assemble_body(
    out_h, gx_h, a1_h, ao_h, a2_h, ad_h,
    out_ref, gx_ref, q_out, k_out, v_out, o_out, gate_out, up_out, down_out,
    a1, ao, a2, ad, sem,
):
    pairs = ((a2_h, a2), (a1_h, a1), (ao_h, ao), (ad_h, ad), (out_h, out_ref), (gx_h, gx_ref))
    loads = [pltpu.make_async_copy(x, y, sem.at[k]) for k, (x, y) in enumerate(pairs)]
    for x in loads:
        x.start()
    loads[0].wait()
    for i in range(NC):
        gate_out[:, FW * i : FW * (i + 1)] = a2[i, :, 0:FW].astype(F32)
        up_out[:, FW * i : FW * (i + 1)] = a2[i, :, FW : 2 * FW].astype(F32)
    for x in loads[1:]:
        x.wait()
    for i in range(NC):
        q_out[:, QW * i : QW * (i + 1)] = a1[i, :, 0:QW].astype(F32)
        k_out[:, HD * i : HD * (i + 1)] = a1[i, :, QW : QW + HD].astype(F32)
        v_out[:, HD * i : HD * (i + 1)] = a1[i, :, QW + HD :].astype(F32)
        o_out[16 * i : 16 * (i + 1), :] = ao[i].astype(F32)
        down_out[24 * i : 24 * (i + 1), :] = ad[i].astype(F32)


def shards(
    tokens, positions, attn_gain, query_weight, key_matrix, value_matrix, query_gain, key_gain,
    out_weight, mlp_gain, gate_weight, up_weight, down_weight, cotangent,
):
    c = lax.axis_index("ctx")
    s = lax.axis_index("shard")
    tok, cot = tokens[0], cotangent[0]

    row0 = jnp.concatenate([attn_gain, mlp_gain])[None]
    row1 = jnp.concatenate([query_gain, key_gain, jnp.zeros((112,), BF)])[None]
    gains = jnp.concatenate([row0, row1, jnp.zeros((62, 128), BF)], 0)
    wo = out_weight.reshape(8, 16, D)
    wd = down_weight.reshape(8, 24, D)

    freq = np.power(ROPE_BASE, -np.arange(HD // 2) * (2.0 / HD)).astype(np.float32)
    freq = np.concatenate([freq, freq])[:, None]

    (
        g_all, w1_all, wo_all, w2_all, wd_all, hid, raw, qkv, tab, probs, heads, out_part, gvec, ghead,
    ) = remote_call(
        start_body,
        [
            ((NC, T, D), BF, "h"), ((NS, 64, WCOL1), BF, "v"), ((NS, 16, D), BF, "v"),
            ((NS, 64, WCOL2), BF, "h"), ((NS, 24, D), BF, "h"),
            ((NC, T, D), BF, "h"), ((NC, T, 512), F32, "h"), ((NC, T, 512), BF, "h"),
            ((NC, T, 2 * HD), F32, "h"), ((2, 10, 256, 256), BF, "h"), ((NC, T, QW), F32, "h"),
            ((NC, T, D), BF, "v"), ((2, D), F32, "v"), ((2, HD), F32, "v"),
        ],
        "h" * 11 + "v",
        (
            tok, cot, positions, query_weight, key_matrix, value_matrix, gate_weight, up_weight,
            gains, wo, wd, freq,
        ),
        [
            pltpu.VMEM((NC, T, D), BF), pltpu.VMEM((NC, 1, T), jnp.int32),
            pltpu.VMEM((64, WCOL1), BF), pltpu.VMEM((64, WCOL2), BF),
            pltpu.VMEM((64, WCOL1), BF), pltpu.VMEM((64, WCOL2), BF),
            pltpu.VMEM((NC, T, D), BF), pltpu.VMEM((NC, T, 512), F32),
            pltpu.VMEM((NC, T, 512), BF), pltpu.VMEM((NC, T, 2 * HD), F32),
            pltpu.VMEM((2, 10, 256, 256), BF), pltpu.VMEM((NC, T, QW), F32),
        ],
        224, 32, 0, 58 << 20,
    )
    ga_all, grad_resid, ggain_mlp, gw2, gwd, down_part, resid = remote_call(
        mid_body,
        [
            ((NC, T, D), BF, "h"), ((T, D), F32, "v"), ((1, D), F32, "v"),
            ((2, 8, 64, WCOL2), BF, "h"), ((2, 8, 24, D), BF, "h"),
            ((NC, T, D), BF, "h"), ((T, D), F32, "v"),
        ],
        "vvvvhhh",
        (out_part, tok, cot, gvec, w2_all.reshape(D, 2 * FW), wd_all.reshape(FW, D), g_all),
        [
            pltpu.VMEM((D, 2 * FW), BF), pltpu.VMEM((FW, D), BF), pltpu.VMEM((NC, T, D), BF),
            pltpu.VMEM((NC, T, D), BF), pltpu.VMEM((2, 8, 64, WCOL2), BF),
            pltpu.VMEM((2, 8, 24, D), BF),
            pltpu.VMEM((NC, T, D), BF), pltpu.VMEM((NC, T, FW), BF), pltpu.VMEM((NC, T, 2 * FW), BF),
            pltpu.VMEM((NC, T, D), BF), pltpu.VMEM((T, D), BF), pltpu.VMEM((FW, D), F32),
        ]
        + chunk_scratch() * 2,
        192, 16, 1, 58 << 20,
    )
    output, gx, small, a1, ao, a2, ad = remote_call(
        end_body,
        [
            ((T, D), BF, "v"), ((T, D), F32, "v"), ((1, SMALL), F32, "v"),
            ((NC, 64, 512), BF, "v"), ((NC, 16, D), BF, "v"),
            ((NC, 64, WCOL2), BF, "v"), ((NC, 24, D), BF, "v"),
        ],
        "v" * 8 + "h" * 10,
        (
            ga_all, tok, grad_resid, resid, gvec, ghead, ggain_mlp, wo_all, gw2, gwd,
            down_part, qkv, probs, heads, raw, tab, hid, w1_all,
        ),
        [
            pltpu.VMEM((NC, T, D), BF), pltpu.VMEM((NC, T, 512), BF),
            pltpu.VMEM((2, 10, 256, 256), BF),
            pltpu.VMEM((NC, T, QW), F32), pltpu.VMEM((NC, T, 512), F32),
            pltpu.VMEM((NC, T, 2 * HD), F32), pltpu.VMEM((NC, T, D), BF),
            pltpu.VMEM((NS, 64, WCOL1), BF),
            pltpu.VMEM((2, 8, 64, WCOL2), BF), pltpu.VMEM((2, 8, 24, D), BF),
            pltpu.VMEM((NC, T, QW), BF), pltpu.VMEM((2, 8, SEQ), F32), pltpu.VMEM((QW, D), F32),
            pltpu.VMEM((SEQ, HD), F32), pltpu.VMEM((SEQ, HD), F32), pltpu.VMEM((NC, T, 512), BF),
            pltpu.VMEM((NC, T, D), BF), pltpu.VMEM((2, 8, 64, 512), BF),
            pltpu.VMEM((2, 8, 16, D), BF),
        ]
        + chunk_scratch() * 2 + shard_scratch((64, 512)) + shard_scratch((16, D))
        + shard_scratch((64, WCOL2)) + shard_scratch((24, D))
        + [
            pltpu.VMEM((64, 512), BF), pltpu.VMEM((16, D), BF),
            pltpu.VMEM((64, WCOL2), BF), pltpu.VMEM((24, D), BF), pltpu.VMEM((24, D), BF),
            pltpu.VMEM((1, SMALL), F32), pltpu.VMEM((NC, 1, SMALL), F32),
            pltpu.VMEM((1, SMALL), F32), pltpu.VMEM((NS, 1, SMALL), F32),
        ],
        224, 32, 2, 58 << 20,
    )
    any_, whole = pl.BlockSpec(memory_space=pl.ANY), pl.BlockSpec(memory_space=pltpu.VMEM)
    output, gx, gwq, gwk, gwv, gwo_out, gwg, gwu, gwd_out = pl.pallas_call(
        assemble_body,
        out_shape=[
            jax.ShapeDtypeStruct((T, D), BF), jax.ShapeDtypeStruct((T, D), F32),
            jax.ShapeDtypeStruct((64, 2048), F32), jax.ShapeDtypeStruct((64, 1024), F32),
            jax.ShapeDtypeStruct((64, 1024), F32), jax.ShapeDtypeStruct((128, D), F32),
            jax.ShapeDtypeStruct((64, 3072), F32), jax.ShapeDtypeStruct((64, 3072), F32),
            jax.ShapeDtypeStruct((192, D), F32),
        ],
        in_specs=[any_] * 6,
        out_specs=[whole] * 9,
        scratch_shapes=[
            pltpu.VMEM((NC, 64, 512), BF), pltpu.VMEM((NC, 16, D), BF),
            pltpu.VMEM((NC, 64, WCOL2), BF), pltpu.VMEM((NC, 24, D), BF),
            pltpu.SemaphoreType.DMA((6,)),
        ],
        compiler_params=pltpu.CompilerParams(vmem_limit_bytes=58 << 20),
    )(output, gx, a1, ao, a2, ad)
    small = small[0]

    def own(offset, width):
        return lax.dynamic_slice(small, (offset + s * width,), (width,))

    return (
        output[None], gx[None], own(0, 64), gwq, gwk, gwv, own(2 * D, 8), own(2 * D + HD, 8),
        gwo_out, own(D, 64), gwg, gwu, gwd_out,
    )


def solution(mesh):
    split = P("shard", "ctx", None)
    rows, vec = P("shard", None), P("shard")
    in_specs = (
        split, P("shard", "ctx"), vec, rows, rows, rows, vec, vec, rows, vec, rows, rows, rows, split,
    )
    out_specs = (split, split, vec, rows, rows, rows, vec, vec, rows, vec, rows, rows, rows)
    return jax.shard_map(shards, mesh=mesh, in_specs=in_specs, out_specs=out_specs, check_vma=False)
```

```python
import jax
import jax.numpy as jnp
import numpy as np
from jax import lax
from jax.experimental import pallas as pl
from jax.experimental.pallas import tpu as pltpu
from jax.sharding import PartitionSpec as P

MESH = pl.DeviceIdType.MESH
BF = jnp.bfloat16
F32 = jnp.float32

NS = 16
NC = 8
T = 128
SEQ = 1024
D = 1024
HD = 128
QW = 256
FW = 384
EPSILON = 1e-06
ROPE_BASE = 1000000.0
BLOCKED_SCORE = -1e30
SMALL = 2304

ALL = slice(None)


def lanes(width):
    a = (width // 128 + 1) // 2 * 128
    return ((ALL, slice(0, a)), (ALL, slice(a, width)), None)


def view(ref, part):
    return ref.at[tuple(pl.ds(p.start, p.stop - p.start) if p != ALL else p for p in part)]


class Ring:
    def __init__(self, me, device):
        self.a = me // 2
        self.b = lax.rem(me, 2)
        self.device = device

    def idx(self, da, db):
        return lax.rem(self.a + da + 4, 4) * 2 + lax.rem(self.b + db, 2)

    def dev(self, da, db):
        return self.device(self.idx(da, db))


class Net:
    def __init__(self, send, recv, local):
        self.s, self.r, self.l = send, recv, local
        self.n = 0
        self.m = 0

    def send(self, src, dst, to):
        k = self.n
        self.n += 1
        c = pltpu.make_async_remote_copy(
            src_ref=src, dst_ref=dst, send_sem=self.s.at[k], recv_sem=self.r.at[k],
            device_id=to, device_id_type=MESH,
        )
        c.start()
        return c

    def copy(self, src, dst):
        k = self.m
        self.m += 1
        c = pltpu.make_async_copy(src, dst, self.l.at[k])
        c.start()
        return c


def places():
    s = lax.axis_index("shard")
    c = lax.axis_index("ctx")
    core = lax.rem(s, 2)
    ctx = Ring(c, lambda i: (s, i))
    chips = Ring(s // 2, lambda i: (i * 2 + core, c))
    sibling = (s + 1 - 2 * core, c)
    half, rest = lax.rem(s, 2), s // 2
    goes = (8 * half + c, rest)
    comes = (2 * c + s // 8, lax.rem(s, 8))
    stays = jnp.logical_and(goes[0] == s, goes[1] == c)
    return s, c, core, ctx, chips, sibling, goes, comes, stays


def ring_devices(ring):
    return [ring.dev(-1, 0), ring.dev(1, 0), ring.dev(0, 1)]


def greet(devices, moved=None):
    barrier = pltpu.get_barrier_semaphore()
    for d in devices:
        pl.semaphore_signal(barrier, inc=1, device_id=d, device_id_type=MESH)
    if moved is not None:
        goes, comes, stays = moved

        @pl.when(jnp.logical_not(stays))
        def _():
            for d in (goes, comes):
                pl.semaphore_signal(barrier, inc=1, device_id=d, device_id_type=MESH)
            pl.semaphore_wait(barrier, len(devices) + 2)

        @pl.when(stays)
        def _():
            pl.semaphore_wait(barrier, len(devices))

    else:
        pl.semaphore_wait(barrier, len(devices))


def drive(*threads, until=None):
    threads = list(threads)
    ended = set()
    while threads:
        for x in list(threads):
            if id(x) in ended:
                continue
            try:
                next(x)
            except StopIteration:
                ended.add(id(x))
        threads = [x for x in threads if id(x) not in ended]
        if until is not None and id(until) in ended:
            break
    return threads


def move(net, items, to, stays):
    base = net.n
    net.n += len(items)

    def remote(k, src, dst):
        return pltpu.make_async_remote_copy(
            src_ref=src, dst_ref=dst, send_sem=net.s.at[base + k], recv_sem=net.r.at[base + k],
            device_id=to, device_id_type=MESH,
        )

    @pl.when(jnp.logical_not(stays))
    def _():
        for k, (src, dst) in enumerate(items):
            remote(k, src, dst).start()

    @pl.when(stays)
    def _():
        for k, (src, dst) in enumerate(items):
            pltpu.make_async_copy(src, dst, net.r.at[base + k]).start()

    yield

    @pl.when(jnp.logical_not(stays))
    def _():
        for k, (src, dst) in enumerate(items):
            remote(k, src, dst).wait()

    @pl.when(stays)
    def _():
        for k, (src, dst) in enumerate(items):
            pltpu.make_async_copy(src, dst, net.r.at[base + k]).wait()


def gather(net, ring, items, slot=lambda i: i, sibling=None):
    left, right, pair = ring_devices(ring)
    me = ring.idx(0, 0)
    over = []

    def pass_on(places):
        if sibling is not None:
            for _, at, _ in items:
                for i in places:
                    over.append(net.send(at(slot(i)), at(slot(i)), sibling))

    first, local = [], []
    for own, at, _ in items:
        here = at(slot(me))
        src = here if own is None else own
        for n in (left, right, pair):
            first.append(net.send(src, here, n))
        if sibling is not None:
            over.append(net.send(src, here, sibling))
        if own is not None:
            local.append(net.copy(own, here))
    yield
    for c in first:
        c.wait_recv()
    second = []
    a, b, z = ring.idx(-1, 0), ring.idx(1, 0), ring.idx(0, 1)
    for _, at, _ in items:
        for i, n in ((a, right), (z, left), (a, pair)):
            second.append(net.send(at(slot(i)), at(slot(i)), n))
    pass_on((a, b, z))
    yield
    for c in second:
        c.wait_recv()
    third = []
    az, bz, o, oz = ring.idx(-1, 1), ring.idx(1, 1), ring.idx(2, 0), ring.idx(2, 1)
    for _, at, parts in items:
        for i, n, part in ((az, right, parts[0]), (bz, left, parts[1]), (o, pair, parts[2])):
            if part is not None:
                r = view(at(slot(i)), part)
                third.append(net.send(r, r, n))
    pass_on((az, bz, o))
    yield
    for c in third:
        c.wait_recv()
    pass_on((oz,))
    for c in local:
        c.wait()
    for c in first + second + third:
        c.wait_send()
    if sibling is not None:
        yield
        for c in over:
            c.wait()


def gather_shard(net, ring, slot, across, sibling, items):
    me, z = ring.idx(0, 0), ring.idx(0, 1)
    over, local, first = [], [], []

    def pass_on(at, *places):
        for i in places:
            over.append(net.send(at(slot(i)), at(slot(i)), sibling))

    for own, other, at in items:
        for i in (me, z) if own is None else (me,):
            here = at(slot(i))
            src = here if own is None else own
            for d in (1, 3, 2):
                first.append(net.send(src, here, ring.dev(d, 0)))
            over.append(net.send(src, here, sibling))
        if own is not None:
            for d in across:
                first.append(net.send(other, here, d))
            local.append(net.copy(own, here))
    yield
    yield
    for c in first:
        c.wait_recv()
    for own, _, at in items:
        for d in (1, 3, 2):
            pass_on(at, ring.idx(d, 0), ring.idx(d, 1))
        if own is not None:
            pass_on(at, z)
    for c in local:
        c.wait()
    yield
    for c in first:
        c.wait_send()
    for c in over:
        c.wait()


def reduce(net, ring, items, result):
    left, right, pair = ring_devices(ring)
    me, a, b, z = ring.idx(0, 0), ring.idx(-1, 0), ring.idx(1, 0), ring.idx(0, 1)
    az, bz, o, oz = ring.idx(-1, 1), ring.idx(1, 1), ring.idx(2, 0), ring.idx(2, 1)

    def plus(x, y):
        return (x.astype(F32) + y.astype(F32)).astype(BF)

    first, second, third = [], [], []
    for p, parts, land, _ in items:
        for n, part in zip((left, right, pair), parts):
            if part is None:
                continue
            first.append(net.send(view(p(oz), part), view(land.at[0], part), n))
    yield
    for c in first:
        c.wait_recv()
    for p, parts, land, sums in items:
        for k, (i, part, n) in enumerate(
            ((o, parts[2], left), (bz, parts[1], right), (az, parts[0], pair))
        ):
            if part is None:
                second.append(net.send(p(i), land.at[1 + k], n))
                continue
            sums[k] = p(i)[...]
            sums[(k,) + part] = plus(p(i)[part], land[(0,) + part])
            second.append(net.send(sums.at[k], land.at[1 + k], n))
    yield
    for c in second:
        c.wait_recv()
    for p, parts, land, sums in items:
        third.append(net.send(p(b), land.at[5], right))
        sums[4] = plus(p(z)[...], land[2])
        third.append(net.send(sums.at[4], land.at[6], pair))
        sums[3] = (p(a)[...].astype(F32) + land[1].astype(F32) + land[3].astype(F32)).astype(BF)
        third.append(net.send(sums.at[3], land.at[4], left))
    yield
    for c in third:
        c.wait_recv()
    for k, (p, parts, land, sums) in enumerate(items):
        result(
            k,
            (p(me)[...].astype(F32) + land[4].astype(F32))
            + (land[5].astype(F32) + land[6].astype(F32)),
        )
    for c in first + second + third:
        c.wait_send()


def at(ref):
    return lambda i: ref.at[i]


CHUNKS = 4
CROWS = T // CHUNKS
CPARTS = ((slice(0, CROWS // 2), ALL), (slice(CROWS // 2, CROWS), ALL), None)


def rows(h):
    return pl.ds(CROWS * h, CROWS)


def chunk(ref, h):
    return lambda i: ref.at[i, rows(h)]


def each(thread, land, sums):
    return [thread(h, land.at[:, rows(h)], sums.at[:, rows(h)]) for h in range(CHUNKS)]


def chunk_scratch():
    return [pltpu.VMEM((7, T, D), BF), pltpu.VMEM((5, T, D), BF)]


def reduce_scratch(shape):
    return [pltpu.VMEM((7,) + shape, BF), pltpu.VMEM((5,) + shape, BF)]


def reduce_shard(net, chips, core, sibling, items, result):
    over = []
    for p, _, half, _, _, _ in items:
        over.append(net.send(p.at[1 - core], half, sibling))
    yield
    for c in over:
        c.wait_recv()
    for p, _, half, both, _, _ in items:

        @pl.loop(0, 8)
        def _(j):
            both[j] = (p[core, j].astype(F32) + half[j].astype(F32)).astype(BF)

    yield from reduce(net, chips, [(at(i[3]), i[1], i[4], i[5]) for i in items], result)
    for c in over:
        c.wait_send()


def shard_scratch(shape):
    return [pltpu.VMEM((8,) + shape, BF), pltpu.VMEM((8,) + shape, BF)] + reduce_scratch(shape)


def rms_parts(v):
    inverse = lax.rsqrt(jnp.mean(v * v, -1, keepdims=True) + EPSILON)
    return v * inverse, inverse


def rms_back(g, n, inverse):
    return inverse * (g - n * jnp.mean(g * n, -1, keepdims=True))


def dot(a, b, dims, out=F32):
    return lax.dot_general(a, b, (dims, ((), ())), preferred_element_type=F32).astype(out)


NN = ((1,), (0,))
NT = ((1,), (1,))
TN = ((0,), (0,))


def remote_call(body, outs, ins, args, scratch, copies, locals_, number, vmem=None):
    sems = [
        pltpu.SemaphoreType.DMA((copies,)),
        pltpu.SemaphoreType.DMA((copies,)),
        pltpu.SemaphoreType.DMA((locals_,)),
    ]
    space = {"v": pl.BlockSpec(memory_space=pltpu.VMEM), "h": pl.BlockSpec(memory_space=pl.ANY)}
    return pl.pallas_call(
        body,
        out_shape=[jax.ShapeDtypeStruct(s, d) for s, d, _ in outs],
        in_specs=[space[k] for k in ins],
        out_specs=[space[k] for _, _, k in outs],
        scratch_shapes=list(scratch) + sems,
        compiler_params=pltpu.CompilerParams(
            collective_id=number, has_side_effects=True, vmem_limit_bytes=vmem
        ),
    )(*args)


WCOL1 = 640
WCOL2 = 768


def start_body(
    tok, cot, pos, wq, wk, wv, wg, wu, gblock, wo, wd, freq,
    g_all, w1_all, wo_all, w2_all, wd_all, hid_h, raw_h, qkv_h, tab_h, probs_h, heads_h, part, gvec, ghead,
    x_all, p_all, w1, w2, v1, v2, hid, raw, qkv, tab, probs, heads, ss, rs, ls,
):
    s, c, core, ctx, chips, sibling, goes, comes, stays = places()
    net = Net(ss, rs, ls)

    other = c + 1 - 2 * lax.rem(c, 2)
    flip = s + 2 - 4 * lax.rem(s // 2, 2)
    across = [((lax.rem(s // 4 + d, 4)) * 4 + lax.rem(flip, 4), other) for d in (0, 1, 3, 2)]
    goes_z = (goes[0] + 2 - 4 * lax.rem(goes[0] // 2, 2), goes[1])
    comes_z = (2 * c + flip // 8, lax.rem(flip, 8))

    def cut(w, width, i):
        return w.at[:, pl.ds(pl.multiple_of(i * width, 128), width)]

    loads = [
        net.copy(x, y)
        for i, one, two in ((c, w1, w2), (other, v1, v2))
        for x, y in (
            (cut(wq, QW, i), one.at[:, 0:QW]), (cut(wk, HD, i), one.at[:, QW : QW + HD]),
            (cut(wv, HD, i), one.at[:, QW + HD : 512]), (gblock, one.at[:, 512:WCOL1]),
            (cut(wg, FW, i), two.at[:, 0:FW]), (cut(wu, FW, i), two.at[:, FW : 2 * FW]),
        )
    ]
    greet(
        ring_devices(ctx) + [chips.dev(d, 0) for d in (1, 2, 3)] + across + [sibling, goes_z, comes_z],
        (goes, comes, stays),
    )
    for x in loads:
        x.wait()

    def place(i):
        return i * 2 + core

    def weights():
        yield from gather_shard(
            net, chips, place, across, sibling, [(w1, v1, at(w1_all))]
        )
        yield from gather_shard(
            net, chips, place, across, sibling,
            [
                (w2, v2, at(w2_all)), (None, None, at(wd_all)), (None, None, at(wo_all)),
            ],
        )

    def moved():
        moved = [(wo.at[c], wo_all.at[goes[0]]), (wd.at[c], wd_all.at[goes[0]])]
        second = [net.send(x, y, goes_z) for x, y in moved]
        yield from move(net, moved, goes, stays)
        for x in second:
            x.wait()

    def by_ctx(h):
        items = [(tok.at[rows(h)], chunk(x_all, h), CPARTS)]
        if h == 0:
            items.append((pos, at(p_all), ((ALL, ALL), None, None)))
        yield from gather(net, ctx, items)
        yield from gather(net, ctx, [(cot.at[rows(h)], chunk(g_all, h), CPARTS)])

    def gains():
        lane = lax.broadcasted_iota(jnp.int32, (8, 128), 1)
        t = [w1_all[i, 0:16, 512:640].astype(F32)[0:8] for i in range(NS)]
        for j in range(8):
            x, y = t[2 * j], t[2 * j + 1]
            low = lane < 64
            gvec[0:1, 128 * j : 128 * (j + 1)] = jnp.where(low, x, pltpu.roll(y, 64, 1))[0:1]
            gvec[1:2, 128 * j : 128 * (j + 1)] = jnp.where(low, pltpu.roll(x, 64, 1), y)[0:1]
        q = jnp.zeros((8, 128), F32)
        k = jnp.zeros((8, 128), F32)
        for i in range(NS):
            here = lane // 8 == i
            q = jnp.where(here, pltpu.roll(t[i], 8 * i, 1), q)
            k = jnp.where(here, pltpu.roll(t[i], (8 * i + 120) % 128, 1), k)
        ghead[0:1] = q[1:2]
        ghead[1:2] = k[1:2]

    def project(i):
        normed, _ = rms_parts(x_all[i].astype(F32))
        h = (normed * gvec[0:1]).astype(BF)
        hid[i] = h
        r = dot(h, w1_all[:, :, 0:512].reshape(D, 512), NN)
        raw[i] = r
        angle = freq[...] * p_all[i].astype(F32)
        cosine = jnp.cos(angle).T
        sine = jnp.sin(angle).T
        sine = jnp.where(lax.broadcasted_iota(jnp.int32, (T, HD), 1) < HD // 2, -sine, sine)
        tab[i, :, 0:HD] = cosine
        tab[i, :, HD:] = sine
        for k in range(3):
            n, _ = rms_parts(r[:, HD * k : HD * (k + 1)])
            u = n * ghead[k // 2 : k // 2 + 1]
            qkv[i, :, HD * k : HD * (k + 1)] = (u * cosine + pltpu.roll(u, 64, 1) * sine).astype(BF)
        qkv[i, :, 3 * HD :] = r[:, 3 * HD :].astype(BF)

    def attend(h, n):
        width = 256 * (n + 1)
        q = qkv[2 * n : 2 * n + 2, :, HD * h : HD * (h + 1)].reshape(256, HD)
        k = qkv[0 : 2 * n + 2, :, 2 * HD : 3 * HD].reshape(width, HD)
        v = qkv[0 : 2 * n + 2, :, 3 * HD :].reshape(width, HD)
        score = dot(q, k, NT) * HD**-0.5
        row = lax.broadcasted_iota(jnp.int32, (256, width), 0) + 256 * n
        col = lax.broadcasted_iota(jnp.int32, (256, width), 1)
        score = jnp.where(col <= row, score, BLOCKED_SCORE)
        top = jnp.max(score, -1, keepdims=True)
        e = jnp.exp(score - top)
        total = jnp.sum(e, -1, keepdims=True)
        share = 1.0 / total
        o = dot(e.astype(BF), v, NN) * share
        e = e * share
        for m in range(n + 1):
            probs[h, n * (n + 1) // 2 + m] = e[:, 256 * m : 256 * (m + 1)].astype(BF).T
        heads[2 * n : 2 * n + 2, :, HD * h : HD * (h + 1)] = o.reshape(2, T, HD)

    def work():
        yield
        yield
        yield
        gains()
        pl.loop(0, 4)(project)
        yield
        pl.loop(4, 8)(project)
        for x, y in ((hid, hid_h), (raw, raw_h), (qkv, qkv_h), (tab, tab_h)):
            stores.append(net.copy(x, y))
        for h in range(2):
            attend(h, 0)
        yield
        for n in range(1, 4):
            for h in range(2):
                attend(h, n)
            if n < 3:
                yield
        stores.append(net.copy(heads, heads_h))
        stores.append(net.copy(probs, probs_h))

        @pl.loop(0, NC)
        def _(i):
            part[i] = dot(heads[i].astype(BF), wo_all[...].reshape(QW, D), NN, BF)

    stores = []
    side = weights()
    drive(side, *[by_ctx(h) for h in range(CHUNKS)], moved(), work())
    for x in stores:
        x.wait()


def mid_body(
    part, tok, cot, gvec, wgu_h, wd_h, g_h,
    ga_all, gres_ref, ggain_ref, gw2_h, gwd_h, down_h, resid,
    wgu, wd, g_all, down_part, gw2, gwd, h_all, mixed, ggu, back_part, ga, gwd_f,
    la, sa, lb, sb, ss, rs, ls,
):
    s, c, core, ctx, chips, sibling, goes, comes, stays = places()
    net = Net(ss, rs, ls)
    loads = [net.copy(x, y) for x, y in ((wgu_h, wgu), (wd_h, wd), (g_h, g_all))]
    stores = []
    greet(ring_devices(ctx))

    def forward(h, land, sums):
        def got(k, total):
            r = tok[rows(h)].astype(F32) + total
            resid[rows(h)] = r
            normed, _ = rms_parts(r)
            h_all[c, rows(h)] = (normed * gvec[1:2]).astype(BF)

        yield from reduce(net, ctx, [(chunk(part, h), CPARTS, land, sums)], got)
        yield from gather(net, ctx, [(None, chunk(h_all, h), CPARTS)])

    def block(i):
        both = dot(h_all[i], wgu[...], NN)
        gate, up = both[:, :FW], both[:, FW:]
        sig = jax.nn.sigmoid(gate)
        act = gate * sig
        m = (act * up).astype(BF)
        mixed[i] = m
        gm = dot(g_all[i], wd[...], NT)
        gg = (gm * up * sig * (1.0 + gate * (1.0 - sig))).astype(BF)
        gu = (gm * act).astype(BF)
        ggu[i, :, 0:FW] = gg
        ggu[i, :, FW:] = gu
        back_part[i] = dot(jnp.concatenate([gg, gu], 1), wgu[...], NT, BF)
        down_part[i] = dot(m, wd[...], NN, BF)

    def blocks(places):
        n = len(places)

        @pl.loop(0, n)
        def _(j):
            i = places[0]
            for k in range(1, n):
                i = jnp.where(j == k, places[k], i)
            block(i)

    def work():
        yield
        yield
        yield
        for x in loads:
            x.wait()
        blocks([c])
        yield
        blocks([ctx.idx(-1, 0), ctx.idx(1, 0), ctx.idx(0, 1)])
        yield
        blocks([ctx.idx(-1, 1), ctx.idx(1, 1), ctx.idx(2, 0)])
        yield
        blocks([ctx.idx(2, 1)])

    drive(*each(forward, la, sa), work())
    stores.append(net.copy(down_part, down_h))

    def got_back(h):
        def got(k, total):
            normed, inverse = rms_parts(resid[rows(h)])
            g = jnp.sum(total * normed, 0, keepdims=True)
            if h == 0:
                ggain_ref[...] = g
            else:
                ggain_ref[...] += g
            gres = cot[rows(h)].astype(F32) + rms_back(total * gvec[1:2], normed, inverse)
            gres_ref[rows(h)] = gres
            ga[rows(h)] = gres.astype(BF)

        return got

    def backward(h, land, sums):
        yield from reduce(net, ctx, [(chunk(back_part, h), CPARTS, land, sums)], got_back(h))
        yield from gather(net, ctx, [(ga.at[rows(h)], chunk(ga_all, h), CPARTS)])

    def grads():
        for q in range(2):

            @pl.loop(4 * q, 4 * q + 4)
            def _(j):
                left = h_all[:, :, pl.ds(pl.multiple_of(j * 128, 128), 128)].reshape(SEQ, 128)
                g = dot(left, ggu[...].reshape(SEQ, 2 * FW), TN, BF)
                gw2[0, j] = g[0:64]
                gw2[1, j] = g[64:128]

            yield
        for j in range(3):
            left = mixed[:, :, 128 * j : 128 * (j + 1)].reshape(SEQ, 128)
            gwd_f[128 * j : 128 * (j + 1)] = dot(left, g_all[...].reshape(SEQ, D), TN)
        for i in range(NS):
            gwd[i % 2, i // 2] = gwd_f[24 * i : 24 * (i + 1)].astype(BF)
        stores.append(net.copy(gw2, gw2_h))
        stores.append(net.copy(gwd, gwd_h))

    drive(*each(backward, lb, sb), grads())
    for x in stores:
        x.wait()


def end_body(
    ga_all, tok, gres_ref, resid, gvec, ghead, ggain, wo_all,
    gw2_h, gwd_h, down_h, qkv_h, probs_h, heads_h, raw_h, tab_h, hid_h, w1_h,
    out_ref, gx_ref, small_ref, a1, ao, a2, ad,
    down_part, qkv, probs, heads, raw, tab, hid, w1_all, gw2, gwd,
    gatt, delta, gwo_f, gk_f, gv_f, gqkv, part, gw1, gwo,
    la, sa, lb, sb, h1, b1, l1, t1, h2, b2, l2, t2,
    h3, b3, l3, t3, h4, b4, l4, t4,
    s1, so, gw2_sum, gwd_sum, own_d, sm, smc, sm2, sms, ss, rs, ls,
):
    s, c, core, ctx, chips, sibling, goes, comes, stays = places()
    net = Net(ss, rs, ls)
    loads = [
        net.copy(x, y)
        for x, y in (
            (heads_h, heads), (qkv_h, qkv), (probs_h, probs), (down_h, down_part),
            (raw_h, raw), (tab_h, tab), (hid_h, hid), (w1_h, w1_all), (gw2_h, gw2), (gwd_h, gwd),
        )
    ]
    ctx_peers = [(s, lax.rem(c + d, NC)) for d in range(1, NC)]
    shard_peers = [(lax.rem(s + d, NS), c) for d in range(1, NS)]
    greet(ctx_peers + shard_peers, (goes, comes, stays))

    def feed_forward(h, land, sums):
        def got(k, total):
            out_ref[rows(h)] = (resid[rows(h)] + total).astype(BF)

        if h == 0:
            loads[3].wait()
        yield from reduce(net, ctx, [(chunk(down_part, h), CPARTS, land, sums)], got)

    def got_ff(k, total):
        (gw2_sum, gwd_sum)[k][...] = total.astype(BF)

    def feed_forward_grads():
        loads[8].wait()
        loads[9].wait()
        yield from reduce_shard(
            net, chips, core, sibling,
            [(gw2, lanes(WCOL2), h3, b3, l3, t3), (gwd, lanes(D), h4, b4, l4, t4)], got_ff,
        )
        yield from move(net, [(gwd_sum, own_d)], comes, stays)
        yield from gather(net, ctx, [(gw2_sum, at(a2), lanes(WCOL2)), (own_d, at(ad), lanes(D))])

    def got_out(k, total):
        so[...] = total.astype(BF)

    def out_grad():
        for j in range(2):
            left = heads[:, :, HD * j : HD * (j + 1)].reshape(SEQ, HD).astype(BF)
            gwo_f[HD * j : HD * (j + 1)] = dot(left, ga_all[...].reshape(SEQ, D), TN)
        for i in range(NS):
            gwo[i % 2, i // 2] = gwo_f[16 * i : 16 * (i + 1)].astype(BF)
        yield from reduce_shard(
            net, chips, core, sibling, [(gwo, lanes(D), h2, b2, l2, t2)], got_out
        )
        yield from move(net, [(so, ao.at[comes[1]])], comes, stays)
        yield from gather(net, ctx, [(None, at(ao), lanes(D))])

    def head_grads(i):
        g = dot(ga_all[i], wo_all[...].reshape(QW, D), NT, BF)
        gatt[i] = g
        both = g.astype(F32) * heads[i]
        for h in range(2):
            d = jnp.sum(both[:, HD * h : HD * (h + 1)], -1, keepdims=True)
            delta[h, 0:1, pl.ds(pl.multiple_of(i * T, T), T)] = jnp.broadcast_to(d, (T, T)).T[0:1]

    def attend_back(h, n, fresh):
        here = slice(2 * n, 2 * n + 2)
        mine = slice(HD * h, HD * (h + 1))
        q = qkv[here, :, mine].reshape(256, HD)
        g = gatt[here, :, mine].reshape(256, HD)
        d = delta[h, 0:1, 256 * n : 256 * (n + 1)]
        gq = None
        for m in range(n + 1):
            k = qkv[2 * m : 2 * m + 2, :, 2 * HD : 3 * HD].reshape(256, HD)
            v = qkv[2 * m : 2 * m + 2, :, 3 * HD :].reshape(256, HD)
            p = probs[h, n * (n + 1) // 2 + m]
            gv = dot(p, g, NN)
            gs = (p.astype(F32) * (dot(v, g, NT) - d)).astype(BF)
            gk = dot(gs, q, NN)
            span = slice(256 * m, 256 * (m + 1))
            if fresh:
                gv_f[span] = gv
                gk_f[span] = gk
            else:
                gv_f[span] += gv
                gk_f[span] += gk
            x = dot(gs, k, TN)
            gq = x if gq is None else gq + x
        turn_back(gq * HD**-0.5, here, mine, 0, fresh)

    def turn_back(g, here, mine, kind, fresh):
        n = g.shape[0]
        cosine = tab[here, :, 0:HD].reshape(n, HD)
        sine = tab[here, :, HD:].reshape(n, HD)
        w = g * cosine - pltpu.roll(g, 64, 1) * sine
        u, inverse = rms_parts(raw[here, :, mine].reshape(n, HD))
        gain = jnp.sum(w * u, 0, keepdims=True)
        place = slice(2 * D + HD * kind, 2 * D + HD * (kind + 1))
        if fresh:
            sm[:, place] = gain
        else:
            sm[:, place] += gain
        r = rms_back(w * ghead[kind : kind + 1], u, inverse).astype(BF)
        gqkv[here, :, mine] = r.reshape(n // T, T, HD)

    def work():
        pl.loop(0, NC)(head_grads)
        loads[1].wait()
        loads[2].wait()
        loads[4].wait()
        loads[5].wait()
        yield
        for n in (3, 2, 1, 0):
            for h in range(2):
                attend_back(h, n, n == 3 and h == 0)
                if n:
                    yield
        for m in range(2):
            here = slice(4 * m, 4 * m + 4)
            span = slice(512 * m, 512 * (m + 1))
            turn_back(gk_f[span] * HD**-0.5, here, slice(2 * HD, 3 * HD), 1, m == 0)
            gqkv[here, :, 3 * HD :] = gv_f[span].astype(BF).reshape(4, T, HD)
        loads[6].wait()
        loads[7].wait()

        @pl.loop(0, NC)
        def _(i):
            part[i] = dot(gqkv[i], w1_all[:, :, 0:512].reshape(D, 512), NT, BF)

    loads[0].wait()
    main = work()
    rest = drive(
        *each(feed_forward, lb, sb), out_grad(), feed_forward_grads(), main,
        until=main,
    )

    def got_input(h):
        def got(k, total):
            normed, inverse = rms_parts(tok[rows(h)].astype(F32))
            g = jnp.sum(total * normed, 0, keepdims=True)
            if h == 0:
                sm[:, 0:D] = g
            else:
                sm[:, 0:D] += g
            gx_ref[rows(h)] = gres_ref[rows(h)] + rms_back(total * gvec[0:1], normed, inverse)

        return got

    def by_ctx(h, land, sums):
        yield from reduce(net, ctx, [(chunk(part, h), CPARTS, land, sums)], got_input(h))

    def small():
        yield
        yield
        yield
        yield
        sm[:, D : 2 * D] = ggain[...]
        smc[c] = sm[...]
        sent = [net.send(sm, smc.at[c], d) for d in ctx_peers]
        yield
        for x in sent:
            x.wait()
        total = smc[0]
        for i in range(1, NC):
            total = total + smc[i]
        sm2[...] = total
        sms[s] = total
        sent = [net.send(sm2, sms.at[s], d) for d in shard_peers]
        yield
        for x in sent:
            x.wait()
        total = sms[0]
        for i in range(1, NS):
            total = total + sms[i]
        small_ref[...] = total

    def got_shard(k, total):
        s1[...] = total.astype(BF)

    def grads():
        @pl.loop(0, 8)
        def _(j):
            left = hid[:, :, pl.ds(pl.multiple_of(j * 128, 128), 128)].reshape(SEQ, 128)
            g = dot(left, gqkv[...].reshape(SEQ, 512), TN, BF)
            gw1[0, j] = g[0:64]
            gw1[1, j] = g[64:128]

        yield from reduce_shard(
            net, chips, core, sibling, [(gw1, lanes(512), h1, b1, l1, t1)], got_shard
        )
        yield from gather(net, ctx, [(s1, at(a1), lanes(512))])

    last = grads()
    tokens = each(by_ctx, la, sa)
    drive(*tokens[:2], last, *tokens[2:], last, *rest, small())


def assemble_body(
    out_h, gx_h, a1_h, ao_h, a2_h, ad_h,
    out_ref, gx_ref, q_out, k_out, v_out, o_out, gate_out, up_out, down_out,
    a1, ao, a2, ad, sem,
):
    pairs = ((a2_h, a2), (a1_h, a1), (ao_h, ao), (ad_h, ad), (out_h, out_ref), (gx_h, gx_ref))
    loads = [pltpu.make_async_copy(x, y, sem.at[k]) for k, (x, y) in enumerate(pairs)]
    for x in loads:
        x.start()
    loads[0].wait()
    for i in range(NC):
        gate_out[:, FW * i : FW * (i + 1)] = a2[i, :, 0:FW].astype(F32)
        up_out[:, FW * i : FW * (i + 1)] = a2[i, :, FW : 2 * FW].astype(F32)
    for x in loads[1:]:
        x.wait()
    for i in range(NC):
        q_out[:, QW * i : QW * (i + 1)] = a1[i, :, 0:QW].astype(F32)
        k_out[:, HD * i : HD * (i + 1)] = a1[i, :, QW : QW + HD].astype(F32)
        v_out[:, HD * i : HD * (i + 1)] = a1[i, :, QW + HD :].astype(F32)
        o_out[16 * i : 16 * (i + 1), :] = ao[i].astype(F32)
        down_out[24 * i : 24 * (i + 1), :] = ad[i].astype(F32)


def shards(
    tokens, positions, attn_gain, query_weight, key_matrix, value_matrix, query_gain, key_gain,
    out_weight, mlp_gain, gate_weight, up_weight, down_weight, cotangent,
):
    c = lax.axis_index("ctx")
    s = lax.axis_index("shard")
    tok, cot = tokens[0], cotangent[0]

    row0 = jnp.concatenate([attn_gain, mlp_gain])[None]
    row1 = jnp.concatenate([query_gain, key_gain, jnp.zeros((112,), BF)])[None]
    gains = jnp.concatenate([row0, row1, jnp.zeros((62, 128), BF)], 0)
    wo = out_weight.reshape(8, 16, D)
    wd = down_weight.reshape(8, 24, D)

    freq = np.power(ROPE_BASE, -np.arange(HD // 2) * (2.0 / HD)).astype(np.float32)
    freq = np.concatenate([freq, freq])[:, None]

    (
        g_all, w1_all, wo_all, w2_all, wd_all, hid, raw, qkv, tab, probs, heads, out_part, gvec, ghead,
    ) = remote_call(
        start_body,
        [
            ((NC, T, D), BF, "h"), ((NS, 64, WCOL1), BF, "v"), ((NS, 16, D), BF, "v"),
            ((NS, 64, WCOL2), BF, "h"), ((NS, 24, D), BF, "h"),
            ((NC, T, D), BF, "h"), ((NC, T, 512), F32, "h"), ((NC, T, 512), BF, "h"),
            ((NC, T, 2 * HD), F32, "h"), ((2, 10, 256, 256), BF, "h"), ((NC, T, QW), F32, "h"),
            ((NC, T, D), BF, "v"), ((2, D), F32, "v"), ((2, HD), F32, "v"),
        ],
        "h" * 11 + "v",
        (
            tok, cot, positions, query_weight, key_matrix, value_matrix, gate_weight, up_weight,
            gains, wo, wd, freq,
        ),
        [
            pltpu.VMEM((NC, T, D), BF), pltpu.VMEM((NC, 1, T), jnp.int32),
            pltpu.VMEM((64, WCOL1), BF), pltpu.VMEM((64, WCOL2), BF),
            pltpu.VMEM((64, WCOL1), BF), pltpu.VMEM((64, WCOL2), BF),
            pltpu.VMEM((NC, T, D), BF), pltpu.VMEM((NC, T, 512), F32),
            pltpu.VMEM((NC, T, 512), BF), pltpu.VMEM((NC, T, 2 * HD), F32),
            pltpu.VMEM((2, 10, 256, 256), BF), pltpu.VMEM((NC, T, QW), F32),
        ],
        224, 32, 0, 58 << 20,
    )
    ga_all, grad_resid, ggain_mlp, gw2, gwd, down_part, resid = remote_call(
        mid_body,
        [
            ((NC, T, D), BF, "h"), ((T, D), F32, "v"), ((1, D), F32, "v"),
            ((2, 8, 64, WCOL2), BF, "h"), ((2, 8, 24, D), BF, "h"),
            ((NC, T, D), BF, "h"), ((T, D), F32, "v"),
        ],
        "vvvvhhh",
        (out_part, tok, cot, gvec, w2_all.reshape(D, 2 * FW), wd_all.reshape(FW, D), g_all),
        [
            pltpu.VMEM((D, 2 * FW), BF), pltpu.VMEM((FW, D), BF), pltpu.VMEM((NC, T, D), BF),
            pltpu.VMEM((NC, T, D), BF), pltpu.VMEM((2, 8, 64, WCOL2), BF),
            pltpu.VMEM((2, 8, 24, D), BF),
            pltpu.VMEM((NC, T, D), BF), pltpu.VMEM((NC, T, FW), BF), pltpu.VMEM((NC, T, 2 * FW), BF),
            pltpu.VMEM((NC, T, D), BF), pltpu.VMEM((T, D), BF), pltpu.VMEM((FW, D), F32),
        ]
        + chunk_scratch() * 2,
        192, 16, 1, 58 << 20,
    )
    output, gx, small, a1, ao, a2, ad = remote_call(
        end_body,
        [
            ((T, D), BF, "v"), ((T, D), F32, "v"), ((1, SMALL), F32, "v"),
            ((NC, 64, 512), BF, "v"), ((NC, 16, D), BF, "v"),
            ((NC, 64, WCOL2), BF, "v"), ((NC, 24, D), BF, "v"),
        ],
        "v" * 8 + "h" * 10,
        (
            ga_all, tok, grad_resid, resid, gvec, ghead, ggain_mlp, wo_all, gw2, gwd,
            down_part, qkv, probs, heads, raw, tab, hid, w1_all,
        ),
        [
            pltpu.VMEM((NC, T, D), BF), pltpu.VMEM((NC, T, 512), BF),
            pltpu.VMEM((2, 10, 256, 256), BF),
            pltpu.VMEM((NC, T, QW), F32), pltpu.VMEM((NC, T, 512), F32),
            pltpu.VMEM((NC, T, 2 * HD), F32), pltpu.VMEM((NC, T, D), BF),
            pltpu.VMEM((NS, 64, WCOL1), BF),
            pltpu.VMEM((2, 8, 64, WCOL2), BF), pltpu.VMEM((2, 8, 24, D), BF),
            pltpu.VMEM((NC, T, QW), BF), pltpu.VMEM((2, 8, SEQ), F32), pltpu.VMEM((QW, D), F32),
            pltpu.VMEM((SEQ, HD), F32), pltpu.VMEM((SEQ, HD), F32), pltpu.VMEM((NC, T, 512), BF),
            pltpu.VMEM((NC, T, D), BF), pltpu.VMEM((2, 8, 64, 512), BF),
            pltpu.VMEM((2, 8, 16, D), BF),
        ]
        + chunk_scratch() * 2 + shard_scratch((64, 512)) + shard_scratch((16, D))
        + shard_scratch((64, WCOL2)) + shard_scratch((24, D))
        + [
            pltpu.VMEM((64, 512), BF), pltpu.VMEM((16, D), BF),
            pltpu.VMEM((64, WCOL2), BF), pltpu.VMEM((24, D), BF), pltpu.VMEM((24, D), BF),
            pltpu.VMEM((1, SMALL), F32), pltpu.VMEM((NC, 1, SMALL), F32),
            pltpu.VMEM((1, SMALL), F32), pltpu.VMEM((NS, 1, SMALL), F32),
        ],
        224, 32, 2, 58 << 20,
    )
    any_, whole = pl.BlockSpec(memory_space=pl.ANY), pl.BlockSpec(memory_space=pltpu.VMEM)
    output, gx, gwq, gwk, gwv, gwo_out, gwg, gwu, gwd_out = pl.pallas_call(
        assemble_body,
        out_shape=[
            jax.ShapeDtypeStruct((T, D), BF), jax.ShapeDtypeStruct((T, D), F32),
            jax.ShapeDtypeStruct((64, 2048), F32), jax.ShapeDtypeStruct((64, 1024), F32),
            jax.ShapeDtypeStruct((64, 1024), F32), jax.ShapeDtypeStruct((128, D), F32),
            jax.ShapeDtypeStruct((64, 3072), F32), jax.ShapeDtypeStruct((64, 3072), F32),
            jax.ShapeDtypeStruct((192, D), F32),
        ],
        in_specs=[any_] * 6,
        out_specs=[whole] * 9,
        scratch_shapes=[
            pltpu.VMEM((NC, 64, 512), BF), pltpu.VMEM((NC, 16, D), BF),
            pltpu.VMEM((NC, 64, WCOL2), BF), pltpu.VMEM((NC, 24, D), BF),
            pltpu.SemaphoreType.DMA((6,)),
        ],
        compiler_params=pltpu.CompilerParams(vmem_limit_bytes=58 << 20),
    )(output, gx, a1, ao, a2, ad)
    small = small[0]

    def own(offset, width):
        return lax.dynamic_slice(small, (offset + s * width,), (width,))

    return (
        output[None], gx[None], own(0, 64), gwq, gwk, gwv, own(2 * D, 8), own(2 * D + HD, 8),
        gwo_out, own(D, 64), gwg, gwu, gwd_out,
    )


def solution(mesh):
    split = P("shard", "ctx", None)
    rows, vec = P("shard", None), P("shard")
    in_specs = (
        split, P("shard", "ctx"), vec, rows, rows, rows, vec, vec, rows, vec, rows, rows, rows, split,
    )
    out_specs = (split, split, vec, rows, rows, rows, vec, vec, rows, vec, rows, rows, rows)
    return jax.shard_map(shards, mesh=mesh, in_specs=in_specs, out_specs=out_specs, check_vma=False)
```
